128 devices in a mesh: space: 8 (over y, core), terms: 16 (over x, z).
Axes of the slice: x: 4, y: 4, z: 4, core: 2. Of those that a mesh axis runs over, the one named last changes fastest.
Arguments:
- forcing: float32 [176, 3, 16, 32, 128], P('terms', None, 'space'), may hold values from -6 to 6
- stencil: float32 [27, 3, 3], replicated, may hold values from -0.12 to 3, as said below
- fields: float32 [5, 16, 32, 128], P(None, 'space'), may hold values from -3 to 3
- coupling: float32 [126, 5], replicated, may hold values from 0.25 to 1
- slot_term: int32 [176], replicated, may hold values from -1 to 125, as said below
Outputs:
- solution: float32 [176, 3, 16, 32, 128], P('terms', None, 'space')
The draws below stay inside these ranges and needn't reach their ends.
Inputs may be any that keep to these rules, and one draw needn't show every extreme that they name: `slot_term`: device k of terms holds the slots k * 11 to (k + 1) * 11 - 1; of these, the first 1 hold level-0 terms or -1, the next 1 level 1, then 1 level 2, 3 level 3 and 5 level 4. Every term stands in exactly one slot. The central diagonal entries stencil[13, a, a] lie in 2 to 3; every other entry lies in -0.12 to 0.05.
All inputs are finite; a program needn't handle non-finite values.
Results may differ from the reference program's by a relative error of at most 0.00014.
Values sent between devices are 32-bit elements; how exact they have to be, the bound alone decides.
A program may use at most 128 MiB of HBM per device.

```python
import math
import jax
import jax.numpy as jnp
import numpy as np
from jax import lax

DIMS = 5
DEGREE = 4
TERMS = 126
NY = 32
NZ = 128
NX = 16
SLOTS_L0 = 1
SLOTS_L1 = 1
SLOTS_L2 = 1
SLOTS_L3 = 3
SLOTS_L4 = 5
SLOT_DEV = 11
SLOTS = 176


def draw_stencil(key, part):
    subkeys = jax.random.split(key, 3)
    offsets = jnp.arange(27)[:, None, None]
    rows_index = jnp.arange(3)[None, :, None]
    cols_index = jnp.arange(3)[None, None, :]
    same_comp = rows_index == cols_index
    central = offsets == 13
    along = jax.random.uniform(subkeys[0], (27, 3, 3), minval=-0.12, maxval=-0.02)
    across = jax.random.uniform(subkeys[1], (27, 3, 3), minval=-0.05, maxval=0.05)
    pivot_draw = jax.random.uniform(subkeys[2], (27, 3, 3), minval=2.0, maxval=3.0)
    table = jnp.where(central & same_comp, pivot_draw, jnp.where(same_comp, along, across))
    return table.astype(jnp.float32)


def draw_slot_term(key, part):
    groups_count = SLOTS // SLOT_DEV
    level_caps = [SLOTS_L0, SLOTS_L1, SLOTS_L2, SLOTS_L3, SLOTS_L4]
    pieces = []
    first_term = 0
    for level_now in range(DEGREE + 1):
        level_count = math.comb(level_now + DIMS - 1, DIMS - 1)
        extent = groups_count * level_caps[level_now]
        shuffled = jax.random.permutation(jax.random.fold_in(key, level_now + 11), extent)
        values = jnp.where(shuffled < level_count, shuffled + first_term, -1).astype(jnp.int32)
        pieces.append(values.reshape(groups_count, level_caps[level_now]))
        first_term += level_count
    return jnp.concatenate(pieces, axis=1).reshape(-1)


def level_of(own_key, shape, cuts, low, largest):
    factor_of = 1.0
    for position, shards_of in cuts:
        heights = jax.random.uniform(jax.random.fold_in(jax.random.fold_in(own_key, 6), position), (shards_of,), jnp.float32, low / len(cuts), largest / len(cuts))
        factor_of = factor_of * jnp.repeat(jnp.exp(heights), shape[position] // shards_of).reshape((-1,) + (1,) * (len(shape) - 1 - position))
    return factor_of


def gaussian(stream_key, shape, scale, bound, shards=(), held_as=jnp.bfloat16):
    values = scale * jax.random.normal(stream_key, shape, jnp.float32)
    if shards:
        values = values * level_of(stream_key, shape, shards, -0.22, 0.18)
    return jnp.clip(values, -bound, bound).astype(held_as)


def setup_inputs(seed: int = 0) -> dict:
    keys = jax.random.split(jax.random.key(seed), 6)
    return {
        "forcing": gaussian(keys[0], (SLOTS, 3, NX, NY, NZ), 1.0, 6.0, ((0, 16), (2, 8)), jnp.float32),
        "stencil": draw_stencil(jax.random.fold_in(keys[5], 71), 0),
        "fields": gaussian(keys[2], (DIMS, NX, NY, NZ), 0.5, 3.0, ((1, 8),), jnp.float32),
        "coupling": jnp.clip(jnp.exp(jax.random.uniform(keys[3], (TERMS, DIMS), jnp.float32, math.log(0.25), math.log(1.0))), 0.25, 1.0),
        "slot_term": draw_slot_term(jax.random.fold_in(keys[5], 71), 0),
    }


def compositions(total, pieces_left):
    if pieces_left == 1:
        return [[total]]
    result = []
    for leading in range(total, -1, -1):
        for remainder in compositions(total - leading, pieces_left - 1):
            result.append([leading] + remainder)
    return result


def chaos_parents(dimensions, top_degree):
    indices = []
    for level_now in range(top_degree + 1):
        indices.extend(compositions(level_now, dimensions))
    lookup = {}
    for number, vector in enumerate(indices):
        lookup[tuple(vector)] = number
    parents = np.full((len(indices), dimensions), -1, dtype=np.int32)
    for number, vector in enumerate(indices):
        for dimension in range(dimensions):
            if vector[dimension] > 0:
                lowered = list(vector)
                lowered[dimension] -= 1
                parents[number, dimension] = lookup[tuple(lowered)]
    return parents


def shifted(array, offset, axis_dim):
    if offset == 0:
        return array
    length = array.shape[axis_dim]
    zeros_edge = jnp.zeros_like(lax.slice_in_dim(array, 0, 1, axis=axis_dim))
    if offset > 0:
        return jnp.concatenate([lax.slice_in_dim(array, 1, length, axis=axis_dim), zeros_edge], axis=axis_dim)
    return jnp.concatenate([zeros_edge, lax.slice_in_dim(array, 0, length - 1, axis=axis_dim)], axis=axis_dim)


def apply_stencil(extended, stencil):
    inner_x = extended.shape[2] - 2
    summed = jnp.zeros(extended.shape[:2] + (inner_x,) + extended.shape[3:], jnp.float32)
    for step_y in range(3):
        for step_z in range(3):
            moved_yz = shifted(shifted(extended, step_y - 1, 3), step_z - 1, 4)
            for step_x in range(3):
                window = lax.slice_in_dim(moved_yz, step_x, step_x + inner_x, axis=2)
                block_coef = stencil[9 * step_x + 3 * step_y + step_z]
                summed = summed + jnp.einsum('ab,sbxyz->saxyz', block_coef, window, precision=lax.Precision.HIGHEST)
    return summed


def pad_first(field):
    return jnp.pad(field, ((0, 0), (0, 0), (1, 1), (0, 0), (0, 0)))


def reference(forcing, stencil, fields, coupling, slot_term):
    parents = chaos_parents(DIMS, DEGREE)
    safe_slots = jnp.where(slot_term >= 0, slot_term, TERMS).astype(jnp.int32)
    slot_of = jnp.zeros((TERMS + 1,), jnp.int32).at[safe_slots].set(jnp.arange(SLOTS, dtype=jnp.int32))
    ordered = forcing[slot_of[:TERMS]]
    pivots = jnp.diagonal(stencil[13])[None, :, None, None, None]
    solutions = []
    images = []
    offset = 0
    for level_now in range(DEGREE + 1):
        level_count = math.comb(level_now + DIMS - 1, DIMS - 1)
        level_load = ordered[offset:offset + level_count]
        if level_now > 0:
            known_images = jnp.concatenate(images, axis=0)
            for dimension in range(DIMS):
                linked = parents[offset:offset + level_count, dimension]
                present = linked >= 0
                picked = known_images[np.where(present, linked, 0)]
                weight = coupling[offset:offset + level_count, dimension] * jnp.asarray(present, jnp.float32)
                level_load = level_load - weight[:, None, None, None, None] * fields[dimension][None, None] * picked
        first_pass = level_load / pivots
        settled = first_pass + (level_load - apply_stencil(pad_first(first_pass), stencil)) / pivots
        solutions.append(settled)
        if level_now < DEGREE:
            images.append(apply_stencil(pad_first(settled), stencil))
        offset += level_count
    ordered_solution = jnp.concatenate(solutions + [jnp.zeros_like(solutions[0][:1])], axis=0)
    return ordered_solution[safe_slots]
```

```python
import functools

import jax
import jax.numpy as jnp
import numpy as np
from jax import lax
from jax.experimental import pallas as pl
from jax.experimental.pallas import tpu as pltpu
from jax.sharding import PartitionSpec as P

DIMS = 5
DEGREE = 4
TERMS = 126
GROUPS = 16
SLOT_DEV = 11
COUNT = (1, 5, 15, 35, 70)
START = (0, 1, 6, 21, 56)
CAP = (1, 1, 1, 3, 5)
BASE = (0, 1, 2, 3, 6)
T8 = (8, 8, 16, 40, 72)
T16 = (16, 16, 16, 48, 80)
WIDE = (True, True, True, False, False)
CHUNKS = ((0, 3, 20, 40), (3, 3, 20, 40), (6, 5, 32, 64))
CHUNK_OF = ((0, 0), (0, 1), (0, 2), (1, 0), (2, 0))
DIRS = tuple((dx, dy) for dx in (-1, 0, 1) for dy in (-1, 0, 1) if (dx, dy) != (0, 0))


def compositions(total, pieces_left):
    if pieces_left == 1:
        return [[total]]
    result = []
    for leading in range(total, -1, -1):
        for remainder in compositions(total - leading, pieces_left - 1):
            result.append([leading] + remainder)
    return result


def parent_hot(level):
    below = {tuple(v): n for n, v in enumerate(compositions(level - 1, DIMS))}
    hot = np.zeros((DIMS, T16[level], T16[level - 1]), np.float32)
    for n, v in enumerate(compositions(level, DIMS)):
        for d in range(DIMS):
            if v[d] > 0:
                w = list(v)
                w[d] -= 1
                hot[d, n, below[tuple(w)]] = 1.0
    hot = hot.reshape(DIMS * T16[level], T16[level - 1])
    return np.concatenate([hot, hot, hot], axis=1)


def parts3(x):
    hi = x.astype(jnp.bfloat16)
    rest = x - hi.astype(jnp.float32)
    mid = rest.astype(jnp.bfloat16)
    lo = (rest - mid.astype(jnp.float32)).astype(jnp.bfloat16)
    return hi, mid, lo


def dot(a, b):
    return jnp.dot(a, b, preferred_element_type=jnp.float32)


def dot3(hot, x):
    hi, mid, lo = parts3(x)
    return dot(hot, hi) + dot(hot, mid) + dot(hot, lo)


def term_of(i):
    q, r = i // 4, i % 4
    return q * 4 + r + (q % 2) * (3 - 2 * r)


def kernel(ns, fin, fl, cp, a1, a2, a3, a4, slots, sten, out, *scr):
    it = iter(scr)
    sb = [next(it) for _ in range(3)]
    rb = [next(it) for _ in range(3)]
    ob = [next(it) for _ in range(3)]
    qb = [next(it) for _ in range(3)]
    load_buf = [next(it) for _ in range(5)]
    sett_buf = [next(it) for _ in range(5)]
    img_buf = [next(it) for _ in range(4)]
    ct = next(it)
    ff = next(it)
    cps = next(it)
    st = next(it)
    in_s, in_r, out_s, out_r, h_s, h_r = [next(it) for _ in range(6)]
    hots = (None, a1, a2, a3, a4)

    s = lax.axis_index("space")
    k = lax.axis_index("terms")
    i = term_of(k)

    barrier = pltpu.get_barrier_semaphore()

    def greet(p, _):
        pl.semaphore_signal(
            barrier, inc=1, device_id={"terms": term_of((i + p) % GROUPS)},
            device_id_type=pl.DeviceIdType.MESH,
        )
        return 0

    lax.fori_loop(1, GROUPS, greet, 0)
    for dx, dy in DIRS:
        if dx == 0:
            continue
        there = (s + dx >= 0) & (s + dx < ns) & (i + dy >= 0) & (i + dy < GROUPS)

        @pl.when(there)
        def _():
            pl.semaphore_signal(
                barrier, inc=1,
                device_id={"space": s + dx, "terms": term_of(i + dy)},
                device_id_type=pl.DeviceIdType.MESH,
            )

    for c, (j0, n, ry, rd) in enumerate(CHUNKS):
        def pack(t, _, c=c, j0=j0, n=n, ry=ry):
            j, cx = t // 6, t % 6
            for q in range(4):
                v = fin[pl.ds(pl.multiple_of((j0 * 6 + t) * 32 + 8 * q, 8), 8), :]
                sb[c][pl.ds(8 * q * ry + cx * n + j, 8, stride=ry), :] = v
            return 0

        lax.fori_loop(0, n * 6, pack, 0)

    sides = jnp.where((s > 0) & (s < ns - 1), 2, 1) if ns > 1 else 0
    rows_of = jnp.where((i > 0) & (i < GROUPS - 1), 3, 2)
    pl.semaphore_wait(barrier, GROUPS - 1 + sides * rows_of)

    def transpose_copy(c, p, src, dst, s_sem, r_sem, rd, inward):
        i2 = (i + p) % GROUPS
        k2 = term_of(i2)
        a = i2 if inward else k2
        b = k if inward else i
        return pltpu.make_async_remote_copy(
            src_ref=src.at[pl.ds(pl.multiple_of(a * rd, 8), rd), :],
            dst_ref=dst.at[pl.ds(pl.multiple_of(b * rd, 8), rd), :],
            send_sem=s_sem.at[c, p],
            recv_sem=r_sem.at[c, p],
            device_id={"terms": k2},
            device_id_type=pl.DeviceIdType.MESH,
        )

    def arrival(c, p, src, dst, s_sem, r_sem, rd, inward):
        i2 = (i - p + GROUPS) % GROUPS
        k2 = term_of(i2)
        b = k2 if inward else i2
        return pltpu.make_async_remote_copy(
            src_ref=src.at[pl.ds(0, rd), :],
            dst_ref=dst.at[pl.ds(pl.multiple_of(b * rd, 8), rd), :],
            send_sem=s_sem.at[c, p],
            recv_sem=r_sem.at[c, p],
            device_id={"terms": k2},
            device_id_type=pl.DeviceIdType.MESH,
        )

    def send_all(c, src, dst, s_sem, r_sem, rd, inward):
        def one(p, _):
            transpose_copy(c, p, src, dst, s_sem, r_sem, rd, inward).start()
            return 0

        lax.fori_loop(1, GROUPS, one, 0)
        a = i if inward else k
        b = k if inward else i
        dst[pl.ds(pl.multiple_of(b * rd, 8), rd), :] = src[pl.ds(pl.multiple_of(a * rd, 8), rd), :]

    def wait_all(c, src, dst, s_sem, r_sem, rd, inward):
        def one(p, _):
            arrival(c, p, src, dst, s_sem, r_sem, rd, inward).wait_recv()
            return 0

        lax.fori_loop(1, GROUPS, one, 0)

    def sent_all(c, src, dst, s_sem, r_sem, rd, inward):
        def one(p, _):
            transpose_copy(c, p, src, dst, s_sem, r_sem, rd, inward).wait_send()
            return 0

        lax.fori_loop(1, GROUPS, one, 0)

    for c in range(3):
        send_all(c, sb[c], rb[c], in_s, in_r, CHUNKS[c][3], True)

    inv = [1.0 / jnp.full((8, 128), sten[13, a, a], jnp.float32) for a in range(3)]

    def table(o, _):
        for a in range(3):
            for b in range(3):
                v = jnp.full((8, 128), sten[o, a, b], jnp.float32)
                ct[1, o * 9 + a * 3 + b] = v
                ct[0, o * 9 + a * 3 + b] = -(v * inv[a]) * inv[b]
        return 0

    lax.fori_loop(0, 27, table, 0)
    for a in range(3):
        ct[0, 13 * 9 + a * 4] = inv[a]
    cps[...] = jnp.zeros_like(cps)
    cps[0:TERMS, :] = cp[...]
    for d in range(DIMS):
        for x in range(2):
            for y in range(2):
                ff[d, x, y] = jnp.broadcast_to(fl[d, x, pl.ds(2 * i + y, 1), :], (8, 128))
    for lv in range(5):
        st[lv] = jnp.full((128, 128), -1, jnp.int32)
        for j in range(CAP[lv]):
            for g in range(GROUPS):
                st[lv, j * GROUPS + g : j * GROUPS + g + 1, :] = jnp.full(
                    (1, 128), slots[g * SLOT_DEV + BASE[lv] + j], jnp.int32
                )

    def zero_outside(buf, o):
        n = 2 * o + 2
        rows = buf.shape[3]

        def clear(x0, x1, y0, y1):
            def one(c, _):
                for x in range(x0, x1):
                    for y in range(y0, y1):
                        buf[c, x, y] = jnp.zeros((rows, 128), jnp.float32)
                return 0

            lax.fori_loop(0, 3, one, 0)

        pl.when(s == 0)(lambda: clear(0, o, 0, n))
        pl.when(s == ns - 1)(lambda: clear(o + 2, n, 0, n))
        pl.when(i == 0)(lambda: clear(0, n, 0, o))
        pl.when(i == GROUPS - 1)(lambda: clear(0, n, o + 2, n))

    for lv in range(5):
        zero_outside(load_buf[lv], 2 if WIDE[lv] else 1)
        if lv < 4 and not WIDE[lv]:
            zero_outside(sett_buf[lv], 1)
        if T8[lv] < T16[lv]:
            pad = jnp.zeros((T16[lv] - T8[lv], 128), jnp.float32)
            for c in range(3):
                for x in range(2):
                    for y in range(2):
                        sett_buf[lv][c, 1 + x, 1 + y, T8[lv] :, :] = pad
                        if lv < 4:
                            img_buf[lv][2 * c + x, y, T8[lv] :, :] = pad

    lane = lax.broadcasted_iota(jnp.int32, (8, 128), 1)

    def stencil(src, bx, by, row, which):
        acc = [[[None] * 3 for _ in range(4)] for _ in range(3)]
        for dx in range(3):
            for dy in range(3):
                for b in range(3):
                    coef = [
                        [ct[which, (dx * 9 + dy * 3 + dz) * 9 + a * 3 + b] for dz in range(3)]
                        for a in range(3)
                    ]
                    for p in range(4):
                        v = src[b, bx + p // 2 + dx, by + p % 2 + dy, pl.ds(row, 8), :]
                        for a in range(3):
                            for dz in range(3):
                                t = coef[a][dz] * v
                                old = acc[a][p][dz]
                                acc[a][p][dz] = t if old is None else old + t
        res = []
        for a in range(3):
            line = []
            for p in range(4):
                low, mid, high = acc[a][p]
                low = jnp.where(lane > 0, pltpu.roll(low, 1, 1), 0.0)
                high = jnp.where(lane < 127, pltpu.roll(high, 127, 1), 0.0)
                line.append(mid + low + high)
            res.append(line)
        return res

    def halo_copy(e, n, buf, o, wide):
        dx, dy = DIRS[n]
        w = 2 if wide else 1
        rng = {1: (o + 2 - w, o - w, w), -1: (o, o + 2, w), 0: (o, o, 2)}
        sx, tx, wx = rng[dx]
        sy, ty, wy = rng[dy]
        return pltpu.make_async_remote_copy(
            src_ref=buf.at[:, sx : sx + wx, sy : sy + wy],
            dst_ref=buf.at[:, tx : tx + wx, ty : ty + wy],
            send_sem=h_s.at[e, n],
            recv_sem=h_r.at[e, n],
            device_id={"space": s + dx, "terms": term_of(i + dy)},
            device_id_type=pl.DeviceIdType.MESH,
        )

    def inside(dx, dy):
        return (s + dx >= 0) & (s + dx < ns) & (i + dy >= 0) & (i + dy < GROUPS)

    def halo_start(e, buf, o, wide):
        for n, (dx, dy) in enumerate(DIRS):
            pl.when(inside(dx, dy))(lambda n=n: halo_copy(e, n, buf, o, wide).start())

    def halo_wait(e, buf, o, wide):
        for n, (dx, dy) in enumerate(DIRS):
            pl.when(inside(-dx, -dy))(lambda n=n: halo_copy(e, n, buf, o, wide).wait_recv())

    def halo_sent(e, buf, o, wide):
        for n, (dx, dy) in enumerate(DIRS):
            pl.when(inside(dx, dy))(lambda n=n: halo_copy(e, n, buf, o, wide).wait_send())

    exchanges = []

    def exchange(buf, o, wide):
        e = len(exchanges)
        exchanges.append((e, buf, o, wide))
        halo_start(e, buf, o, wide)
        halo_wait(e, buf, o, wide)

    for lv in range(5):
        c, j0 = CHUNK_OF[lv]
        _, n, ry, rd = CHUNKS[c]
        t8, t16 = T8[lv], T16[lv]
        o = 2 if WIDE[lv] else 1
        if lv == 0 or c != CHUNK_OF[lv - 1][0]:
            wait_all(c, sb[c], rb[c], in_s, in_r, rd, True)
        terms_row = lax.broadcasted_iota(jnp.int32, (128, 128), 1) + START[lv]
        hot = (st[lv] == terms_row).astype(jnp.float32)
        to_slot = hot[0 : 16 * CAP[lv], 0:t16].astype(jnp.bfloat16)
        to_term = jnp.transpose(hot)[0:t16, 0 : 16 * CAP[lv]].astype(jnp.bfloat16)
        if lv > 0:
            weight = [
                jnp.broadcast_to(cps[START[lv] : START[lv] + t16, d : d + 1], (t16, 128))
                for d in range(DIMS)
            ]

        def load_of(cx, _):
            cc, x = cx // 2, cx % 2
            given = []
            for y in range(2):
                pieces = [
                    rb[c][pl.ds(8 * h * rd + y * ry + cx * n + j0 + j, 8, stride=rd), :]
                    for j in range(CAP[lv])
                    for h in range(2)
                ]
                given.append(jnp.concatenate(pieces, axis=0))
            value = dot3(to_term, jnp.concatenate(given, axis=1))
            if lv > 0:
                below = jnp.concatenate([img_buf[lv - 1][cx, 0], img_buf[lv - 1][cx, 1]], axis=1)
                picked = dot(hots[lv][...], jnp.concatenate(parts3(below), axis=0))
            for y in range(2):
                part = value[0:t8, 128 * y : 128 * y + 128]
                if lv > 0:
                    for d in range(DIMS):
                        field = ff[d, x, y, 0:1, :]
                        term = picked[d * t16 : d * t16 + t8, 128 * y : 128 * y + 128]
                        part = part - (weight[d][0:t8] * field) * term
                load_buf[lv][cc, o + x, o + y] = part
            return 0

        lax.fori_loop(0, 6, load_of, 0)
        exchange(load_buf[lv], o, WIDE[lv])

        if WIDE[lv]:
            def settle(t, _):
                r, q = t // 4, t % 4
                qx, qy = q // 2, q % 2
                row = pl.multiple_of(r * 8, 8)
                res = stencil(load_buf[lv], 2 * qx, 2 * qy, row, 0)
                mx = [
                    jnp.where((qx == 0) & (s == 0), 0.0, 1.0),
                    jnp.where((qx == 1) & (s == ns - 1), 0.0, 1.0),
                ]
                my = [
                    jnp.where((qy == 0) & (i == 0), 0.0, 1.0),
                    jnp.where((qy == 1) & (i == GROUPS - 1), 0.0, 1.0),
                ]
                for a in range(3):
                    for p in range(4):
                        keep = mx[p // 2] * my[p % 2]
                        sett_buf[lv][a, 2 * qx + p // 2, 2 * qy + p % 2, pl.ds(row, 8), :] = (
                            res[a][p] * keep
                        )
                return 0

            lax.fori_loop(0, t8 // 8 * 4, settle, 0)
        else:
            def settle(t, _):
                row = pl.multiple_of(t * 8, 8)
                res = stencil(load_buf[lv], 0, 0, row, 0)
                for a in range(3):
                    for p in range(4):
                        sett_buf[lv][a, 1 + p // 2, 1 + p % 2, pl.ds(row, 8), :] = res[a][p]
                return 0

            lax.fori_loop(0, t8 // 8, settle, 0)
            if lv < 4:
                exchange(sett_buf[lv], 1, False)

        if lv < 4:
            def image(t, _):
                row = pl.multiple_of(t * 8, 8)
                res = stencil(sett_buf[lv], 0, 0, row, 1)
                for a in range(3):
                    for p in range(4):
                        img_buf[lv][2 * a + p // 2, p % 2, pl.ds(row, 8), :] = res[a][p]
                return 0

            lax.fori_loop(0, t8 // 8, image, 0)

        def deliver(cx, _):
            cc, x = cx // 2, cx % 2
            both = jnp.concatenate(
                [sett_buf[lv][cc, 1 + x, 1], sett_buf[lv][cc, 1 + x, 2]], axis=1
            )
            rows = dot3(to_slot, both)
            for y in range(2):
                for j in range(CAP[lv]):
                    for h in range(2):
                        q = j * 16 + h * 8
                        ob[c][pl.ds(8 * h * rd + y * ry + cx * n + j0 + j, 8, stride=rd), :] = (
                            rows[q : q + 8, 128 * y : 128 * y + 128]
                        )
            return 0

        lax.fori_loop(0, 6, deliver, 0)
        if lv == 4 or CHUNK_OF[lv + 1][0] != c:
            send_all(c, ob[c], qb[c], out_s, out_r, rd, False)

    for c, (j0, n, ry, rd) in enumerate(CHUNKS):
        wait_all(c, ob[c], qb[c], out_s, out_r, rd, False)

        def unpack(t, _, c=c, j0=j0, n=n, ry=ry):
            j, cx = t // 6, t % 6
            for q in range(4):
                v = qb[c][pl.ds(8 * q * ry + cx * n + j, 8, stride=ry), :]
                out[pl.ds(pl.multiple_of((j0 * 6 + t) * 32 + 8 * q, 8), 8), :] = v
            return 0

        lax.fori_loop(0, n * 6, unpack, 0)

    for c in range(3):
        sent_all(c, sb[c], rb[c], in_s, in_r, CHUNKS[c][3], True)
        sent_all(c, ob[c], qb[c], out_s, out_r, CHUNKS[c][3], False)
    for args in exchanges:
        halo_sent(*args)


def on_device(ns, forcing, stencil, fields, coupling, slot_term):
    rows = forcing.shape[0] * 6 * 32
    vm = pl.BlockSpec(memory_space=pltpu.VMEM)
    sm = pl.BlockSpec(memory_space=pltpu.SMEM)
    f32 = jnp.float32
    message = lambda: [pltpu.VMEM((GROUPS * c[3], 128), f32) for c in CHUNKS]
    scratch = message() + message() + message() + message()
    for lv in range(5):
        side = 6 if WIDE[lv] else 4
        scratch.append(pltpu.VMEM((3, side, side, T8[lv], 128), f32))
    for lv in range(5):
        scratch.append(pltpu.VMEM((3, 4, 4, T16[lv], 128), f32))
    for lv in range(4):
        scratch.append(pltpu.VMEM((6, 2, T16[lv], 128), f32))
    scratch += [
        pltpu.VMEM((2, 243, 8, 128), f32),
        pltpu.VMEM((DIMS, 2, 2, 8, 128), f32),
        pltpu.VMEM((144, DIMS), f32),
        pltpu.VMEM((5, 128, 128), jnp.int32),
    ]
    dma = pltpu.SemaphoreType.DMA
    n_exchange = sum(1 if w else 2 for w in WIDE[:4]) + 1
    scratch += [dma((3, GROUPS)) for _ in range(4)] + [dma((n_exchange, 8)) for _ in range(2)]
    hots = [jnp.asarray(parent_hot(lv), jnp.bfloat16) for lv in range(1, 5)]
    out = pl.pallas_call(
        functools.partial(kernel, ns),
        out_shape=jax.ShapeDtypeStruct((rows, 128), f32),
        in_specs=[vm, vm, vm, vm, vm, vm, vm, sm, sm],
        out_specs=vm,
        scratch_shapes=scratch,
        compiler_params=pltpu.CompilerParams(
            collective_id=0, has_side_effects=True, vmem_limit_bytes=56 << 20
        ),
    )(forcing.reshape(rows, 128), fields, coupling, *hots, slot_term, stencil)
    return out.reshape(forcing.shape)


def solution(mesh):
    return jax.shard_map(
        functools.partial(on_device, mesh.shape["space"]),
        mesh=mesh,
        in_specs=(
            P("terms", None, "space", None, None),
            P(),
            P(None, "space", None, None),
            P(),
            P(),
        ),
        out_specs=P("terms", None, "space", None, None),
        check_vma=False,
    )
```

```python
import functools

import jax
import jax.numpy as jnp
import numpy as np
from jax import lax
from jax.experimental import pallas as pl
from jax.experimental.pallas import tpu as pltpu
from jax.sharding import PartitionSpec as P

DIMS = 5
TERMS = 126
GROUPS = 16
SLOT_DEV = 11
COUNT = (1, 5, 15, 35, 70)
START = (0, 1, 6, 21, 56)
CAP = (1, 1, 1, 3, 5)
BASE = (0, 1, 2, 3, 6)
T8 = (8, 8, 16, 40, 72)
STEP = (2, 6, 16, 12, 14)
CHUNKS = ((0, 1), (1, 2), (3, 3), (6, 5))
CHUNK_OF = ((0, 0), (1, 0), (1, 1), (2, 0), (3, 0))
DIRS = tuple((dx, dz) for dx in (-1, 0, 1) for dz in (-1, 0, 1) if (dx, dz) != (0, 0))
MESH = pl.DeviceIdType.MESH


def compositions(total, pieces_left):
    if pieces_left == 1:
        return [[total]]
    result = []
    for leading in range(total, -1, -1):
        for remainder in compositions(total - leading, pieces_left - 1):
            result.append([leading] + remainder)
    return result


def parent_table():
    table = np.full((TERMS, DIMS), -1, np.int32)
    for level in range(1, 5):
        below = {tuple(v): n for n, v in enumerate(compositions(level - 1, DIMS))}
        for n, v in enumerate(compositions(level, DIMS)):
            for d in range(DIMS):
                if v[d] > 0:
                    w = list(v)
                    w[d] -= 1
                    table[START[level] + n, d] = below[tuple(w)]
    return table.reshape(-1)


def dot(a, b):
    return jnp.dot(a, b, preferred_element_type=jnp.float32)


def term_of(i):
    q, r = i // 4, i % 4
    return q * 4 + r + (q % 2) * (3 - 2 * r)


def kernel(ns, fin, fl, cp, ptab, slots, sten, out, *scr):
    it = iter(scr)
    sb = [next(it) for _ in CHUNKS]
    rb = [next(it) for _ in CHUNKS]
    ob = [next(it) for _ in CHUNKS]
    qb = [next(it) for _ in CHUNKS]
    load_buf = [next(it) for _ in range(5)]
    sett_buf = [next(it) for _ in range(4)]
    own_buf = [next(it) for _ in range(5)]
    img_buf = [next(it) for _ in range(4)]
    faces = [next(it) for _ in range(9)]
    rims = [next(it) for _ in range(9)]
    wh, wl, xs, ff, ft, posv, pos, pos_sem = [next(it) for _ in range(8)]
    in_s, in_r, out_s, out_r, h_s, h_r = [next(it) for _ in range(6)]

    s = lax.axis_index("space")
    k = lax.axis_index("terms")
    i = term_of(k)

    barrier = pltpu.get_barrier_semaphore()

    def greet(p, _):
        pl.semaphore_signal(
            barrier, inc=1, device_id={"terms": term_of((i + p) % GROUPS)}, device_id_type=MESH
        )
        return 0

    lax.fori_loop(1, GROUPS, greet, 0)

    def inside(dx, dz):
        return (s + dx >= 0) & (s + dx < ns) & (i + dz >= 0) & (i + dz < GROUPS)

    for dx, dz in DIRS:
        if dx == 0:
            continue

        @pl.when(inside(dx, dz))
        def _():
            pl.semaphore_signal(
                barrier, inc=1,
                device_id={"space": s + dx, "terms": term_of(i + dz)},
                device_id_type=MESH,
            )

    def pack(c):
        j0, n = CHUNKS[c]

        def one(m, _):
            j, x = j0 + m // 2, m % 2
            rows = [
                fin[pl.ds(pl.multiple_of((j * 6 + a * 2 + x) * 32, 32), 32), :] for a in range(3)
            ]
            turned = jnp.transpose(jnp.concatenate(rows + [jnp.zeros((32, 128), jnp.float32)], axis=0))
            sb[c][:, m] = turned.reshape(GROUPS, 8, 128)
            return 0

        lax.fori_loop(0, 2 * n, one, 0)

    def wait_barrier():
        sides = jnp.where((s > 0) & (s < ns - 1), 2, 1) if ns > 1 else 0
        rows_of = jnp.where((i > 0) & (i < GROUPS - 1), 3, 2)
        pl.semaphore_wait(barrier, GROUPS - 1 + sides * rows_of)

    def leaving(c, p, src, dst, s_sem, r_sem, inward):
        i2 = (i + p) % GROUPS
        k2 = term_of(i2)
        return pltpu.make_async_remote_copy(
            src_ref=src.at[i2 if inward else k2],
            dst_ref=dst.at[k if inward else i],
            send_sem=s_sem.at[c, p],
            recv_sem=r_sem.at[c, p],
            device_id={"terms": k2},
            device_id_type=MESH,
        )

    def arriving(c, p, src, dst, s_sem, r_sem, inward):
        i2 = (i - p + GROUPS) % GROUPS
        k2 = term_of(i2)
        return pltpu.make_async_remote_copy(
            src_ref=src.at[0],
            dst_ref=dst.at[k2 if inward else i2],
            send_sem=s_sem.at[c, p],
            recv_sem=r_sem.at[c, p],
            device_id={"terms": k2},
            device_id_type=MESH,
        )

    def over_peers(fn):
        def one(p, _):
            fn(p)
            return 0

        lax.fori_loop(1, GROUPS, one, 0)

    def send_in(c):
        over_peers(lambda p: leaving(c, p, sb[c], rb[c], in_s, in_r, True).start())
        rb[c][k] = sb[c][i]

    def wait_in(c):
        over_peers(lambda p: arriving(c, p, sb[c], rb[c], in_s, in_r, True).wait_recv())

    def send_out(c):
        over_peers(lambda p: leaving(c, p, ob[c], qb[c], out_s, out_r, False).start())
        qb[c][i] = ob[c][k]

    def wait_out(c):
        over_peers(lambda p: arriving(c, p, ob[c], qb[c], out_s, out_r, False).wait_recv())

    pack(0)
    wait_barrier()
    send_in(0)
    pack(1)
    send_in(1)

    lane8 = lax.broadcasted_iota(jnp.int32, (8, 128), 1)

    def locate(g, acc):
        for j in range(SLOT_DEV):
            acc = jnp.where(lane8 == slots[g * SLOT_DEV + j], g * 16 + j, acc)
        return acc

    posv[...] = lax.fori_loop(0, GROUPS, locate, jnp.zeros((8, 128), jnp.int32))
    to_smem = pltpu.make_async_copy(posv, pos, pos_sem)
    to_smem.start()

    for dz in range(3):
        for which in range(2):
            for w in (wh, wl):
                w[which, (dz * 4 + 3) * 128 : (dz * 4 + 4) * 128, 0:128] = jnp.zeros(
                    (128, 128), jnp.bfloat16
                )
                w[which, dz * 512 : dz * 512 + 128, 128:256] = jnp.zeros((128, 128), jnp.bfloat16)
    lane1 = lax.broadcasted_iota(jnp.int32, (1, 128), 1)
    group = lane1 // 32

    def by_group(v0, v1, v2):
        return jnp.where(
            group == 0, v0, jnp.where(group == 1, v1, jnp.where(group == 2, v2, 0.0))
        ).astype(jnp.float32)

    def splat(v):
        return jnp.full((1, 128), v, jnp.float32)

    inv = [1.0 / splat(sten[a, a, 13]) for a in range(3)]
    inv_lane = by_group(*inv)
    apart = lax.broadcasted_iota(jnp.int32, (32, 128), 0) - lax.broadcasted_iota(
        jnp.int32, (32, 128), 1
    ) % 32

    def table(m, _):
        dx, dz = m // 3, m % 3
        for b in range(4):
            block = [jnp.zeros((32, 128), jnp.float32)] * 2
            if b < 3:
                for dy in range(3):
                    o = dx * 9 + dy * 3 + dz
                    plain = by_group(*[splat(sten[a, b, o]) for a in range(3)])
                    smooth = -(plain * inv_lane) * inv[b]
                    if dy == 1:
                        centre = (group == b) & ((dx == 1) & (dz == 1))
                        smooth = jnp.where(centre, inv_lane, smooth)
                    for which, line in enumerate((smooth, plain)):
                        block[which] = jnp.where(apart == dy - 1, line, block[which])
            for which in range(2):
                hi = block[which].astype(jnp.bfloat16)
                lo = (block[which] - hi.astype(jnp.float32)).astype(jnp.bfloat16)
                for px in range(2):
                    row = pl.multiple_of((dz * 4 + dx + px) * 128 + b * 32, 32)
                    wh[which, pl.ds(row, 32), px * 128 : px * 128 + 128] = hi
                    wl[which, pl.ds(row, 32), px * 128 : px * 128 + 128] = lo
        return 0

    lax.fori_loop(0, 9, table, 0)

    def field(m, _):
        rows = fl[m // 2, m % 2]
        ft[...] = jnp.transpose(jnp.concatenate([rows] * 4, axis=0))
        ff[m] = ft[pl.ds(pl.multiple_of(8 * i, 8), 8), :]
        return 0

    lax.fori_loop(0, 2 * DIMS, field, 0)

    def zero_outside(buf, rim, count):
        def layer(x):
            def one(t, _):
                buf[x, t] = jnp.zeros((24, 128), jnp.float32)
                return 0

            lax.fori_loop(0, count, one, 0)
            for side in range(2):
                rim[side, x] = jnp.zeros(rim.shape[2:], jnp.float32)

        pl.when(s == 0)(lambda: layer(0))
        pl.when(s == ns - 1)(lambda: layer(3))

        def edge(side):
            rim[side] = jnp.zeros(rim.shape[1:], jnp.float32)

        pl.when(i == 0)(lambda: edge(0))
        pl.when(i == GROUPS - 1)(lambda: edge(1))

    for lv in range(5):
        zero_outside(load_buf[lv], rims[2 * lv], COUNT[lv])
        if lv < 4:
            zero_outside(sett_buf[lv], rims[2 * lv + 1], COUNT[lv])

    pack(2)
    pack(3)
    to_smem.wait()

    def halo_copy(e, n, buf, count):
        dx, dz = DIRS[n]
        sx, tx = {1: (2, 0), -1: (1, 3), 0: (0, 0)}[dx]
        if dz == 0:
            src, dst = buf.at[sx, 0:count, 8:16, :], buf.at[tx, 0:count, 8:16, :]
        else:
            side = 1 if dz > 0 else 0
            if dx == 0:
                src, dst = faces[e].at[side], rims[e].at[1 - side, 1:3]
            else:
                src, dst = faces[e].at[side, sx - 1], rims[e].at[1 - side, tx]
        return pltpu.make_async_remote_copy(
            src_ref=src,
            dst_ref=dst,
            send_sem=h_s.at[e, n],
            recv_sem=h_r.at[e, n],
            device_id={"space": s + dx, "terms": term_of(i + dz)},
            device_id_type=MESH,
        )

    def by_five(count, fn):
        w = min(count, 5)

        def some(u, _):
            for v in range(w):
                fn(u * w + v)
            return 0

        lax.fori_loop(0, count // w, some, 0)

    exchanges = []

    def start_exchange(e, buf, count):
        exchanges.append((e, buf, count))
        for n, (dx, dz) in enumerate(DIRS):
            pl.when(inside(dx, dz))(lambda n=n: halo_copy(e, n, buf, count).start())

    def end_exchange(e, buf, count):
        for n, (dx, dz) in enumerate(DIRS):
            pl.when(inside(-dx, -dz))(lambda n=n: halo_copy(e, n, buf, count).wait_recv())

        def spread(t):
            for x in range(4):
                buf[x, t, 7:8, :] = rims[e][0, x, pl.ds(t, 1), :]
                buf[x, t, 16:17, :] = rims[e][1, x, pl.ds(t, 1), :]

        by_five(count, spread)

    def apply(lv, src, which, store):
        step = STEP[lv]
        rows = step * 8

        def chunk(ci, _):
            def pair(u, _):
                t = ci * step + 2 * u
                for dz in range(3):
                    for x in range(4):
                        v = jnp.concatenate(
                            [src[x, t, 7 + dz : 15 + dz, :], src[x, t + 1, 7 + dz : 15 + dz, :]], axis=0
                        )
                        hi = v.astype(jnp.bfloat16)
                        lo = (v - hi.astype(jnp.float32)).astype(jnp.bfloat16)
                        col = (dz * 4 + x) * 128
                        xs[pl.ds(pl.multiple_of(u * 16, 16), 16), col : col + 128] = hi
                        xs[pl.ds(pl.multiple_of(rows + u * 16, 16), 16), col : col + 128] = lo
                return 0

            lax.fori_loop(0, step // 2, pair, 0)
            both = dot(xs[0 : 2 * rows, :], wh[which])
            res = both[0:rows] + both[rows:] + dot(xs[0:rows, :], wl[which])
            for px in range(2):
                store(px, ci * step, res[:, px * 128 : px * 128 + 128].reshape(step, 8, 128))
            return 0

        lax.fori_loop(0, -(-COUNT[lv] // step), chunk, 0)

    e = 0
    for lv in range(5):
        c, j0 = CHUNK_OF[lv]
        step = STEP[lv]
        if lv == 0 or c != CHUNK_OF[lv - 1][0]:
            wait_in(c)
        if lv == 0:
            send_in(2)

        def load_of(t):
            q = pos[0, START[lv] + t]
            g = q // 16
            j = j0 + jnp.clip(q % 16 - BASE[lv], 0, CAP[lv] - 1)
            parts = [rb[c][g, 2 * j + x] for x in range(2)]
            if lv > 0:
                for d in range(DIMS):
                    par = ptab[(START[lv] + t) * DIMS + d]
                    weight = jnp.where(par >= 0, cp[d, START[lv] + t], 0.0)
                    at = jnp.maximum(par, 0)
                    for x in range(2):
                        parts[x] = parts[x] - (weight * ff[2 * d + x]) * img_buf[lv - 1][x, at]
            for x in range(2):
                load_buf[lv][1 + x, t, 8:16, :] = parts[x]
                faces[2 * lv][0, x, pl.ds(t, 1), :] = parts[x][0:1]
                faces[2 * lv][1, x, pl.ds(t, 1), :] = parts[x][7:8]

        by_five(COUNT[lv], load_of)
        start_exchange(2 * lv, load_buf[lv], COUNT[lv])
        end_exchange(2 * lv, load_buf[lv], COUNT[lv])
        if lv == 1:
            send_in(3)

        def settle(px, t0, v):
            own_buf[lv][px, pl.ds(t0, step)] = v
            if lv < 4:
                sett_buf[lv][1 + px, pl.ds(t0, step), 8:16, :] = v

        apply(lv, load_buf[lv], 0, settle)

        if lv < 4:
            def face(t):
                for x in range(2):
                    faces[2 * lv + 1][0, x, pl.ds(t, 1), :] = sett_buf[lv][1 + x, t, 8:9, :]
                    faces[2 * lv + 1][1, x, pl.ds(t, 1), :] = sett_buf[lv][1 + x, t, 15:16, :]

            by_five(COUNT[lv], face)
            start_exchange(2 * lv + 1, sett_buf[lv], COUNT[lv])

        def deliver(g, _):
            for j in range(CAP[lv]):
                q = slots[g * SLOT_DEV + BASE[lv] + j]
                t = jnp.clip(q - START[lv], 0, COUNT[lv] - 1)
                for x in range(2):
                    v = own_buf[lv][x, t]
                    ob[c][g, 2 * (j0 + j) + x] = jnp.where(q >= 0, v, 0.0)
            return 0

        lax.fori_loop(0, GROUPS, deliver, 0)

        if lv < 4:
            end_exchange(2 * lv + 1, sett_buf[lv], COUNT[lv])

            def image(px, t0, v):
                img_buf[lv][px, pl.ds(t0, step)] = v

            apply(lv, sett_buf[lv], 1, image)
        if lv == 4 or CHUNK_OF[lv + 1][0] != c:
            send_out(c)

    for c, (j0, n) in enumerate(CHUNKS):
        wait_out(c)

        def unpack(m, _, c=c, j0=j0):
            j, x = j0 + m // 2, m % 2
            turned = jnp.transpose(qb[c][:, m].reshape(128, 128))
            for a in range(3):
                row = pl.multiple_of((j * 6 + a * 2 + x) * 32, 32)
                out[pl.ds(row, 32), :] = turned[32 * a : 32 * a + 32]
            return 0

        lax.fori_loop(0, 2 * n, unpack, 0)

    for c in range(len(CHUNKS)):
        over_peers(lambda p: leaving(c, p, sb[c], rb[c], in_s, in_r, True).wait_send())
        over_peers(lambda p: leaving(c, p, ob[c], qb[c], out_s, out_r, False).wait_send())
    for e, buf, count in exchanges:
        for n, (dx, dz) in enumerate(DIRS):
            pl.when(inside(dx, dz))(lambda n=n: halo_copy(e, n, buf, count).wait_send())


def on_device(ns, forcing, stencil, fields, coupling, slot_term):
    rows = forcing.shape[0] * 6 * 32
    vm = pl.BlockSpec(memory_space=pltpu.VMEM)
    sm = pl.BlockSpec(memory_space=pltpu.SMEM)
    f32, bf16 = jnp.float32, jnp.bfloat16
    dma = pltpu.SemaphoreType.DMA
    scratch = [pltpu.VMEM((GROUPS, 2 * n, 8, 128), f32) for _ in range(4) for _, n in CHUNKS]
    scratch += [pltpu.VMEM((4, T8[lv], 24, 128), f32) for lv in (0, 1, 2, 3, 4, 0, 1, 2, 3)]
    scratch += [pltpu.VMEM((2, T8[lv], 8, 128), f32) for lv in range(5)]
    scratch += [pltpu.VMEM((2, T8[lv], 8, 128), f32) for lv in range(4)]
    scratch += [pltpu.VMEM((2, 2, T8[e // 2], 128), f32) for e in range(9)]
    scratch += [pltpu.VMEM((2, 4, T8[e // 2], 128), f32) for e in range(9)]
    scratch += [
        pltpu.VMEM((2, 12 * 128, 256), bf16),
        pltpu.VMEM((2, 12 * 128, 256), bf16),
        pltpu.VMEM((2 * 8 * max(STEP), 12 * 128), bf16),
        pltpu.VMEM((2 * DIMS, 8, 128), f32),
        pltpu.VMEM((128, 128), f32),
        pltpu.VMEM((8, 128), jnp.int32),
        pltpu.SMEM((8, 128), jnp.int32),
        dma(()),
    ]
    scratch += [dma((len(CHUNKS), GROUPS)) for _ in range(4)] + [dma((9, 8)) for _ in range(2)]
    out = pl.pallas_call(
        functools.partial(kernel, ns),
        out_shape=jax.ShapeDtypeStruct((rows, 128), f32),
        in_specs=[vm, vm, sm, sm, sm, sm],
        out_specs=vm,
        scratch_shapes=scratch,
        compiler_params=pltpu.CompilerParams(
            collective_id=0, has_side_effects=True, vmem_limit_bytes=56 << 20
        ),
    )(forcing.reshape(rows, 128), fields, coupling.T, jnp.asarray(parent_table()), slot_term, stencil.transpose(1, 2, 0))
    return out.reshape(forcing.shape)


def solution(mesh):
    return jax.shard_map(
        functools.partial(on_device, mesh.shape["space"]),
        mesh=mesh,
        in_specs=(
            P("terms", None, "space", None, None),
            P(),
            P(None, "space", None, None),
            P(),
            P(),
        ),
        out_specs=P("terms", None, "space", None, None),
        check_vma=False,
    )
```

```python
import functools

import jax
import jax.numpy as jnp
import numpy as np
from jax import lax
from jax.experimental import pallas as pl
from jax.experimental.pallas import tpu as pltpu
from jax.sharding import PartitionSpec as P

DIMS = 5
TERMS = 126
GROUPS = 16
SLOT_DEV = 11
COUNT = (1, 5, 15, 35, 70)
START = (0, 1, 6, 21, 56)
CAP = (1, 1, 1, 3, 5)
BASE = (0, 1, 2, 3, 6)
T8 = (8, 8, 16, 40, 72)
STEP = (2, 6, 16, 36, 36)
WIDE = (True, True, True, False, False)
CHUNKS = ((0, 1), (1, 2), (3, 3), (6, 5))
CHUNK_OF = ((0, 0), (1, 0), (1, 1), (2, 0), (3, 0))
DIRS = tuple((dx, dz) for dx in (-1, 0, 1) for dz in (-1, 0, 1) if (dx, dz) != (0, 0))
MESH = pl.DeviceIdType.MESH


def compositions(total, pieces_left):
    if pieces_left == 1:
        return [[total]]
    result = []
    for leading in range(total, -1, -1):
        for remainder in compositions(total - leading, pieces_left - 1):
            result.append([leading] + remainder)
    return result


def parent_table():
    table = np.full((TERMS, DIMS), -1, np.int32)
    for level in range(1, 5):
        below = {tuple(v): n for n, v in enumerate(compositions(level - 1, DIMS))}
        for n, v in enumerate(compositions(level, DIMS)):
            for d in range(DIMS):
                if v[d] > 0:
                    w = list(v)
                    w[d] -= 1
                    table[START[level] + n, d] = below[tuple(w)]
    return table.reshape(-1)


def dot(a, b):
    return jnp.dot(a, b, preferred_element_type=jnp.float32)


def term_of(i):
    q, r = i // 4, i % 4
    return q * 4 + r + (q % 2) * (3 - 2 * r)


def kernel(ns, fin, fl, cp, ptab, slots, sten, out, *scr):
    it = iter(scr)
    sb = [next(it) for _ in CHUNKS]
    rb = [next(it) for _ in CHUNKS]
    ob = [next(it) for _ in CHUNKS]
    qb = [next(it) for _ in CHUNKS]
    load_buf = [next(it) for _ in range(5)]
    sett_buf = [next(it) for _ in range(4)]
    own_buf = [next(it) for _ in range(5)]
    img_buf = [next(it) for _ in range(4)]
    faces = [next(it) for _ in range(9)]
    rims = [next(it) for _ in range(9)]
    wh, wl, xs, ff, ft, posv, pos, pos_sem = [next(it) for _ in range(8)]
    in_s, in_r, out_s, out_r, h_s, h_r = [next(it) for _ in range(6)]

    s = lax.axis_index("space")
    k = lax.axis_index("terms")
    i = term_of(k)

    barrier = pltpu.get_barrier_semaphore()

    def greet(p, _):
        pl.semaphore_signal(
            barrier, inc=1, device_id={"terms": term_of((i + p) % GROUPS)}, device_id_type=MESH
        )
        return 0

    lax.fori_loop(1, GROUPS, greet, 0)

    def inside(dx, dz):
        return (s + dx >= 0) & (s + dx < ns) & (i + dz >= 0) & (i + dz < GROUPS)

    for dx, dz in DIRS:
        if dx == 0:
            continue

        @pl.when(inside(dx, dz))
        def _():
            pl.semaphore_signal(
                barrier, inc=1,
                device_id={"space": s + dx, "terms": term_of(i + dz)},
                device_id_type=MESH,
            )

    def pack(c):
        j0, n = CHUNKS[c]

        def one(m, _):
            j, x = j0 + m // 2, m % 2
            rows = [
                fin[pl.ds(pl.multiple_of((j * 6 + a * 2 + x) * 32, 32), 32), :] for a in range(3)
            ]
            turned = jnp.transpose(jnp.concatenate(rows + [jnp.zeros((32, 128), jnp.float32)], axis=0))
            sb[c][:, m] = turned.reshape(GROUPS, 8, 128)
            return 0

        lax.fori_loop(0, 2 * n, one, 0)

    def wait_barrier():
        sides = jnp.where((s > 0) & (s < ns - 1), 2, 1) if ns > 1 else 0
        rows_of = jnp.where((i > 0) & (i < GROUPS - 1), 3, 2)
        pl.semaphore_wait(barrier, GROUPS - 1 + sides * rows_of)

    def leaving(c, p, src, dst, s_sem, r_sem, inward):
        i2 = (i + p) % GROUPS
        k2 = term_of(i2)
        return pltpu.make_async_remote_copy(
            src_ref=src.at[i2 if inward else k2],
            dst_ref=dst.at[k if inward else i],
            send_sem=s_sem.at[c, p],
            recv_sem=r_sem.at[c, p],
            device_id={"terms": k2},
            device_id_type=MESH,
        )

    def arriving(c, p, src, dst, s_sem, r_sem, inward):
        i2 = (i - p + GROUPS) % GROUPS
        k2 = term_of(i2)
        return pltpu.make_async_remote_copy(
            src_ref=src.at[0],
            dst_ref=dst.at[k2 if inward else i2],
            send_sem=s_sem.at[c, p],
            recv_sem=r_sem.at[c, p],
            device_id={"terms": k2},
            device_id_type=MESH,
        )

    def over_peers(fn):
        def one(p, _):
            fn(p)
            return 0

        lax.fori_loop(1, GROUPS, one, 0)

    def send_in(c):
        over_peers(lambda p: leaving(c, p, sb[c], rb[c], in_s, in_r, True).start())
        rb[c][k] = sb[c][i]

    def wait_in(c):
        over_peers(lambda p: arriving(c, p, sb[c], rb[c], in_s, in_r, True).wait_recv())

    def send_out(c):
        over_peers(lambda p: leaving(c, p, ob[c], qb[c], out_s, out_r, False).start())
        qb[c][i] = ob[c][k]

    def wait_out(c):
        over_peers(lambda p: arriving(c, p, ob[c], qb[c], out_s, out_r, False).wait_recv())

    pack(0)
    wait_barrier()
    send_in(0)
    pack(1)
    send_in(1)

    lane8 = lax.broadcasted_iota(jnp.int32, (8, 128), 1)

    def locate(g, acc):
        for j in range(SLOT_DEV):
            acc = jnp.where(lane8 == slots[g * SLOT_DEV + j], g * 16 + j, acc)
        return acc

    posv[...] = lax.fori_loop(0, GROUPS, locate, jnp.zeros((8, 128), jnp.int32))
    to_smem = pltpu.make_async_copy(posv, pos, pos_sem)
    to_smem.start()

    for dz in range(3):
        for which in range(2):
            for w in (wh, wl):
                w[which, (dz * 4 + 3) * 128 : (dz * 4 + 4) * 128, 0:128] = jnp.zeros(
                    (128, 128), jnp.bfloat16
                )
                w[which, dz * 512 : dz * 512 + 128, 128:256] = jnp.zeros((128, 128), jnp.bfloat16)
    lane1 = lax.broadcasted_iota(jnp.int32, (1, 128), 1)
    group = lane1 // 32

    def by_group(v0, v1, v2):
        return jnp.where(
            group == 0, v0, jnp.where(group == 1, v1, jnp.where(group == 2, v2, 0.0))
        ).astype(jnp.float32)

    def splat(v):
        return jnp.full((1, 128), v, jnp.float32)

    inv = [1.0 / splat(sten[a, a, 13]) for a in range(3)]
    inv_lane = by_group(*inv)
    apart = lax.broadcasted_iota(jnp.int32, (32, 128), 0) - lax.broadcasted_iota(
        jnp.int32, (32, 128), 1
    ) % 32

    def table(m, _):
        dx, dz = m // 3, m % 3
        for b in range(4):
            block = [jnp.zeros((32, 128), jnp.float32)] * 2
            if b < 3:
                for dy in range(3):
                    o = dx * 9 + dy * 3 + dz
                    plain = by_group(*[splat(sten[a, b, o]) for a in range(3)])
                    smooth = -(plain * inv_lane) * inv[b]
                    if dy == 1:
                        centre = (group == b) & ((dx == 1) & (dz == 1))
                        smooth = jnp.where(centre, inv_lane, smooth)
                    for which, line in enumerate((smooth, plain)):
                        block[which] = jnp.where(apart == dy - 1, line, block[which])
            for which in range(2):
                hi = block[which].astype(jnp.bfloat16)
                lo = (block[which] - hi.astype(jnp.float32)).astype(jnp.bfloat16)
                for px in range(2):
                    row = pl.multiple_of((dz * 4 + dx + px) * 128 + b * 32, 32)
                    wh[which, pl.ds(row, 32), px * 128 : px * 128 + 128] = hi
                    wl[which, pl.ds(row, 32), px * 128 : px * 128 + 128] = lo
        return 0

    lax.fori_loop(0, 9, table, 0)

    def field(m, _):
        rows = fl[m // 2, m % 2]
        ft[...] = jnp.transpose(jnp.concatenate([rows] * 4, axis=0))
        ff[m] = ft[pl.ds(pl.multiple_of(8 * i, 8), 8), :]
        return 0

    lax.fori_loop(0, 2 * DIMS, field, 0)

    def zero_outside(buf, rim, count, wide):
        def layer(x):
            def one(t, _):
                buf[x, t] = jnp.zeros((24, 128), jnp.float32)
                return 0

            lax.fori_loop(0, count, one, 0)
            for side in range(2):
                if wide:
                    for row in range(3):
                        rim[side, row, x] = jnp.zeros(rim.shape[3:], jnp.float32)
                else:
                    rim[side, x] = jnp.zeros(rim.shape[2:], jnp.float32)

        def edge(side):
            if wide:
                for row in (side, side + 1):
                    rim[side, row] = jnp.zeros(rim.shape[2:], jnp.float32)
            else:
                rim[side] = jnp.zeros(rim.shape[1:], jnp.float32)

        for x in (0, 1) if wide else (0,):
            pl.when(s == 0)(lambda x=x: layer(x))
        for x in (4, 5) if wide else (3,):
            pl.when(s == ns - 1)(lambda x=x: layer(x))
        pl.when(i == 0)(lambda: edge(0))
        pl.when(i == GROUPS - 1)(lambda: edge(1))

    for lv in range(5):
        zero_outside(load_buf[lv], rims[2 * lv], COUNT[lv], WIDE[lv])
        if lv < 4 and not WIDE[lv]:
            zero_outside(sett_buf[lv], rims[2 * lv + 1], COUNT[lv], False)

    pack(2)
    pack(3)
    to_smem.wait()

    def halo_copy(e, n, buf, count):
        dx, dz = DIRS[n]
        sx, tx = {1: (2, 0), -1: (1, 3), 0: (0, 0)}[dx]
        if buf.shape[0] == 6:
            tx = {1: 0, -1: 4, 0: 2}[dx]
            if dz == 0:
                src, dst = buf.at[2:4, 0:count, 8:16, :], buf.at[tx : tx + 2, 0:count, 8:16, :]
            else:
                side = 1 if dz > 0 else 0
                src = faces[e].at[side]
                dst = rims[e].at[1 - side, 1 - side : 3 - side, tx : tx + 2]
        elif dz == 0:
            src, dst = buf.at[sx, 0:count, 8:16, :], buf.at[tx, 0:count, 8:16, :]
        else:
            side = 1 if dz > 0 else 0
            if dx == 0:
                src, dst = faces[e].at[side], rims[e].at[1 - side, 1:3]
            else:
                src, dst = faces[e].at[side, sx - 1], rims[e].at[1 - side, tx]
        return pltpu.make_async_remote_copy(
            src_ref=src,
            dst_ref=dst,
            send_sem=h_s.at[e, n],
            recv_sem=h_r.at[e, n],
            device_id={"space": s + dx, "terms": term_of(i + dz)},
            device_id_type=MESH,
        )

    def by_five(count, fn):
        w = min(count, 5)

        def some(u, _):
            for v in range(w):
                fn(u * w + v)
            return 0

        lax.fori_loop(0, count // w, some, 0)

    exchanges = []

    def start_exchange(e, buf, count):
        exchanges.append((e, buf, count))
        for n, (dx, dz) in enumerate(DIRS):
            pl.when(inside(dx, dz))(lambda n=n: halo_copy(e, n, buf, count).start())

    def end_exchange(e, buf, count):
        for n, (dx, dz) in enumerate(DIRS):
            pl.when(inside(-dx, -dz))(lambda n=n: halo_copy(e, n, buf, count).wait_recv())

        spread_rim(e, buf, count)

    def spread_rim(e, buf, count):
        def spread(t):
            for x in range(4):
                buf[x, t, 7:8, :] = rims[e][0, x, pl.ds(t, 1), :]
                buf[x, t, 16:17, :] = rims[e][1, x, pl.ds(t, 1), :]

        def spread_wide(t):
            for x in range(6):
                buf[x, t, 7:8, :] = rims[e][0, 1, x, pl.ds(t, 1), :]
                buf[x, t, 16:17, :] = rims[e][1, 1, x, pl.ds(t, 1), :]
                rims[e][0, 2, x, pl.ds(t, 1), :] = buf[x, t, 8:9, :]
                rims[e][1, 0, x, pl.ds(t, 1), :] = buf[x, t, 15:16, :]

        by_five(count, spread_wide if buf.shape[0] == 6 else spread)

    def halves(v):
        hi = v.astype(jnp.bfloat16)
        return hi, (v - hi.astype(jnp.float32)).astype(jnp.bfloat16)

    def product(rows, which):
        both = dot(xs[0 : 2 * rows, :], wh[which])
        return both[0:rows] + both[rows:] + dot(xs[0:rows, :], wl[which])

    def settle_wide(lv):
        src, rim, step, t8 = load_buf[lv], rims[2 * lv], STEP[lv], T8[lv]
        base = 16 * step
        rows = base + 4 * t8

        def put(row, col, v):
            hi, lo = halves(v)
            xs[pl.ds(pl.multiple_of(row, 16), v.shape[0]), col : col + 128] = hi
            xs[pl.ds(pl.multiple_of(rows + row, 16), v.shape[0]), col : col + 128] = lo

        def pair(u, _):
            for dz in range(3):
                for w in range(4):
                    for b in range(2):
                        v = [src[2 * b + w, 2 * u + h, 7 + dz : 15 + dz, :] for h in range(2)]
                        put(b * 8 * step + u * 16, (dz * 4 + w) * 128, jnp.concatenate(v, axis=0))
            return 0

        lax.fori_loop(0, step // 2, pair, 0)
        for side in range(2):
            for dz in range(3):
                for w in range(4):
                    v = [rim[side, dz, 2 * b + w] for b in range(2)]
                    put(base + side * 2 * t8, (dz * 4 + w) * 128, jnp.concatenate(v, axis=0))
        res = product(rows, 0)
        one, zero = jnp.float32(1.0), jnp.float32(0.0)
        in_x = [jnp.where(s > 0, one, zero), one, one, jnp.where(s < ns - 1, one, zero)]
        in_z = [jnp.where(i > 0, one, zero), jnp.where(i < GROUPS - 1, one, zero)]
        for x in range(4):
            b, lanes = x // 2, slice(128 * (x % 2), 128 * (x % 2) + 128)
            v = res[b * 8 * step : (b + 1) * 8 * step, lanes].reshape(step, 8, 128)
            if x in (1, 2):
                own_buf[lv][x - 1, 0:step] = v
            else:
                v = v * in_x[x]
            sett_buf[lv][x, 0:step, 8:16, :] = v
            for side in range(2):
                row = base + side * 2 * t8 + b * t8
                rims[2 * lv + 1][side, x] = res[row : row + t8, lanes] * (in_x[x] * in_z[side])

    def apply(lv, src, which, store):
        step = STEP[lv]
        rows = step * 8

        def chunk(ci, _):
            def pair(u, _):
                t = ci * step + 2 * u
                for dz in range(3):
                    for x in range(4):
                        v = jnp.concatenate(
                            [src[x, t, 7 + dz : 15 + dz, :], src[x, t + 1, 7 + dz : 15 + dz, :]], axis=0
                        )
                        hi, lo = halves(v)
                        col = (dz * 4 + x) * 128
                        xs[pl.ds(pl.multiple_of(u * 16, 16), 16), col : col + 128] = hi
                        xs[pl.ds(pl.multiple_of(rows + u * 16, 16), 16), col : col + 128] = lo
                return 0

            lax.fori_loop(0, step // 2, pair, 0)
            res = product(rows, which)
            for px in range(2):
                store(px, ci * step, res[:, px * 128 : px * 128 + 128].reshape(step, 8, 128))
            return 0

        lax.fori_loop(0, -(-COUNT[lv] // step), chunk, 0)

    pending = []
    for lv in range(5):
        c, j0 = CHUNK_OF[lv]
        step = STEP[lv]
        if lv == 0 or c != CHUNK_OF[lv - 1][0]:
            wait_in(c)
        if lv == 0:
            send_in(2)

        def load_of(t):
            q = pos[0, START[lv] + t]
            g = q // 16
            j = j0 + jnp.clip(q % 16 - BASE[lv], 0, CAP[lv] - 1)
            parts = [rb[c][g, 2 * j + x] for x in range(2)]
            if lv > 0:
                for d in range(DIMS):
                    par = ptab[(START[lv] + t) * DIMS + d]
                    weight = jnp.where(par >= 0, cp[d, START[lv] + t], 0.0)
                    at = jnp.maximum(par, 0)
                    for x in range(2):
                        parts[x] = parts[x] - (weight * ff[2 * d + x]) * img_buf[lv - 1][x, at]
            for x in range(2):
                load_buf[lv][(2 if WIDE[lv] else 1) + x, t, 8:16, :] = parts[x]
                if WIDE[lv]:
                    for row in range(2):
                        faces[2 * lv][0, row, x, pl.ds(t, 1), :] = parts[x][row : row + 1]
                        faces[2 * lv][1, row, x, pl.ds(t, 1), :] = parts[x][6 + row : 7 + row]
                else:
                    faces[2 * lv][0, x, pl.ds(t, 1), :] = parts[x][0:1]
                    faces[2 * lv][1, x, pl.ds(t, 1), :] = parts[x][7:8]

        by_five(COUNT[lv], load_of)
        start_exchange(2 * lv, load_buf[lv], COUNT[lv])
        if pending:
            pending.pop()()
        end_exchange(2 * lv, load_buf[lv], COUNT[lv])
        if lv == 1:
            send_in(3)

        def settle(px, t0, v):
            own_buf[lv][px, pl.ds(t0, step)] = v
            if lv < 4:
                sett_buf[lv][1 + px, pl.ds(t0, step), 8:16, :] = v

        if WIDE[lv]:
            settle_wide(lv)
            spread_rim(2 * lv + 1, sett_buf[lv], COUNT[lv])
        else:
            apply(lv, load_buf[lv], 0, settle)

        if lv < 4 and not WIDE[lv]:
            def face(t):
                for x in range(2):
                    faces[2 * lv + 1][0, x, pl.ds(t, 1), :] = sett_buf[lv][1 + x, t, 8:9, :]
                    faces[2 * lv + 1][1, x, pl.ds(t, 1), :] = sett_buf[lv][1 + x, t, 15:16, :]

            by_five(COUNT[lv], face)
            start_exchange(2 * lv + 1, sett_buf[lv], COUNT[lv])

        def deliver(g, _, lv=lv, c=c, j0=j0):
            for j in range(CAP[lv]):
                q = slots[g * SLOT_DEV + BASE[lv] + j]
                t = jnp.clip(q - START[lv], 0, COUNT[lv] - 1)
                for x in range(2):
                    v = own_buf[lv][x, t]
                    ob[c][g, 2 * (j0 + j) + x] = jnp.where(q >= 0, v, 0.0)
            return 0

        if not WIDE[lv]:
            lax.fori_loop(0, GROUPS, deliver, 0)

        if lv < 4:
            if not WIDE[lv]:
                end_exchange(2 * lv + 1, sett_buf[lv], COUNT[lv])

            def image(px, t0, v):
                img_buf[lv][px, pl.ds(t0, step)] = v

            apply(lv, sett_buf[lv], 1, image)

        def finish(lv=lv, c=c, deliver=deliver):
            if WIDE[lv]:
                lax.fori_loop(0, GROUPS, deliver, 0)
            if lv == 4 or CHUNK_OF[lv + 1][0] != c:
                send_out(c)

        if WIDE[lv]:
            pending.append(finish)
        else:
            finish()

    for c, (j0, n) in enumerate(CHUNKS):
        wait_out(c)

        def unpack(m, _, c=c, j0=j0):
            j, x = j0 + m // 2, m % 2
            turned = jnp.transpose(qb[c][:, m].reshape(128, 128))
            for a in range(3):
                row = pl.multiple_of((j * 6 + a * 2 + x) * 32, 32)
                out[pl.ds(row, 32), :] = turned[32 * a : 32 * a + 32]
            return 0

        lax.fori_loop(0, 2 * n, unpack, 0)

    for c in range(len(CHUNKS)):
        over_peers(lambda p: leaving(c, p, sb[c], rb[c], in_s, in_r, True).wait_send())
        over_peers(lambda p: leaving(c, p, ob[c], qb[c], out_s, out_r, False).wait_send())
    for e, buf, count in exchanges:
        for n, (dx, dz) in enumerate(DIRS):
            pl.when(inside(dx, dz))(lambda n=n: halo_copy(e, n, buf, count).wait_send())


def on_device(ns, forcing, stencil, fields, coupling, slot_term):
    rows = forcing.shape[0] * 6 * 32
    vm = pl.BlockSpec(memory_space=pltpu.VMEM)
    sm = pl.BlockSpec(memory_space=pltpu.SMEM)
    f32, bf16 = jnp.float32, jnp.bfloat16
    dma = pltpu.SemaphoreType.DMA
    scratch = [pltpu.VMEM((GROUPS, 2 * n, 8, 128), f32) for _ in range(4) for _, n in CHUNKS]
    scratch += [pltpu.VMEM((6 if WIDE[lv] else 4, T8[lv], 24, 128), f32) for lv in range(5)]
    scratch += [pltpu.VMEM((4, T8[lv], 24, 128), f32) for lv in range(4)]
    scratch += [pltpu.VMEM((2, T8[lv], 8, 128), f32) for lv in range(5)]
    scratch += [pltpu.VMEM((2, T8[lv], 8, 128), f32) for lv in range(4)]
    wide = [WIDE[e // 2] and e % 2 == 0 for e in range(9)]
    scratch += [pltpu.VMEM((2,) + (2,) * w + (2, T8[e // 2], 128), f32) for e, w in enumerate(wide)]
    scratch += [
        pltpu.VMEM((2, 3, 6, T8[e // 2], 128) if w else (2, 4, T8[e // 2], 128), f32)
        for e, w in enumerate(wide)
    ]
    scratch += [
        pltpu.VMEM((2, 12 * 128, 256), bf16),
        pltpu.VMEM((2, 12 * 128, 256), bf16),
        pltpu.VMEM((640, 12 * 128), bf16),
        pltpu.VMEM((2 * DIMS, 8, 128), f32),
        pltpu.VMEM((128, 128), f32),
        pltpu.VMEM((8, 128), jnp.int32),
        pltpu.SMEM((8, 128), jnp.int32),
        dma(()),
    ]
    scratch += [dma((len(CHUNKS), GROUPS)) for _ in range(4)] + [dma((9, 8)) for _ in range(2)]
    out = pl.pallas_call(
        functools.partial(kernel, ns),
        out_shape=jax.ShapeDtypeStruct((rows, 128), f32),
        in_specs=[vm, vm, sm, sm, sm, sm],
        out_specs=vm,
        scratch_shapes=scratch,
        compiler_params=pltpu.CompilerParams(
            collective_id=0, has_side_effects=True, vmem_limit_bytes=56 << 20
        ),
    )(forcing.reshape(rows, 128), fields, coupling.T, jnp.asarray(parent_table()), slot_term, stencil.transpose(1, 2, 0))
    return out.reshape(forcing.shape)


def solution(mesh):
    return jax.shard_map(
        functools.partial(on_device, mesh.shape["space"]),
        mesh=mesh,
        in_specs=(
            P("terms", None, "space", None, None),
            P(),
            P(None, "space", None, None),
            P(),
            P(),
        ),
        out_specs=P("terms", None, "space", None, None),
        check_vma=False,
    )
```

```python
import functools

import jax
import jax.numpy as jnp
import numpy as np
from jax import lax
from jax.experimental import pallas as pl
from jax.experimental.pallas import tpu as pltpu
from jax.sharding import PartitionSpec as P

DIMS = 5
TERMS = 126
GROUPS = 16
SLOT_DEV = 11
COUNT = (1, 5, 15, 35, 70)
START = (0, 1, 6, 21, 56)
CAP = (1, 1, 1, 3, 5)
BASE = (0, 1, 2, 3, 6)
T8 = (8, 8, 16, 40, 72)
STEP = (2, 6, 16, 0, 0)
PARTS = (((0, 1, 8),), ((0, 5, 8),), ((0, 15, 16),), ((0, 16, 16), (16, 19, 24)), ((0, 32, 32), (32, 38, 40)))
WIDE = (True, True, True, False, False)
CHUNKS = ((0, 1), (1, 2), (3, 3), (6, 5))
OUTS = ((0, 1, (0, 1)), (1, 2, (0, 1)), (3, 3, (0, 1)), (6, 5, (0,)), (6, 5, (1,)))
CHUNK_OF = ((0, 0), (1, 0), (1, 1), (2, 0), (3, 0))
DIRS = tuple((dx, dz) for dx in (-1, 0, 1) for dz in (-1, 0, 1) if (dx, dz) != (0, 0))
MESH = pl.DeviceIdType.MESH


def compositions(total, pieces_left):
    if pieces_left == 1:
        return [[total]]
    result = []
    for leading in range(total, -1, -1):
        for remainder in compositions(total - leading, pieces_left - 1):
            result.append([leading] + remainder)
    return result


def parent_table():
    table = np.full((TERMS, DIMS), -1, np.int32)
    for level in range(1, 5):
        below = {tuple(v): n for n, v in enumerate(compositions(level - 1, DIMS))}
        for n, v in enumerate(compositions(level, DIMS)):
            for d in range(DIMS):
                if v[d] > 0:
                    w = list(v)
                    w[d] -= 1
                    table[START[level] + n, d] = below[tuple(w)]
    return table.reshape(-1)


def dot(a, b):
    return jnp.dot(a, b, preferred_element_type=jnp.float32)


def term_of(i):
    q, r = i // 4, i % 4
    return q * 4 + r + (q % 2) * (3 - 2 * r)


def kernel(ns, fin, fl, cp, ptab, slots, sten, out, *scr):
    it = iter(scr)
    sb = [next(it) for _ in CHUNKS]
    rb = [next(it) for _ in CHUNKS]
    ob = [next(it) for _ in OUTS]
    qb = [next(it) for _ in OUTS]
    load_buf = [next(it) for _ in range(5)]
    sett_buf = [next(it) for _ in range(4)]
    own_buf = [next(it) for _ in range(5)]
    img_buf = [next(it) for _ in range(4)]
    faces = [next(it) for _ in range(9)]
    rims = [next(it) for _ in range(9)]
    wh, wl, wc, xs, ff, ft, posv, pos, pos_sem = [next(it) for _ in range(9)]
    in_s, in_r, out_s, out_r, h_s, h_r = [next(it) for _ in range(6)]

    s = lax.axis_index("space")
    k = lax.axis_index("terms")
    i = term_of(k)

    barrier = pltpu.get_barrier_semaphore()

    def greet(p, _):
        pl.semaphore_signal(
            barrier, inc=1, device_id={"terms": term_of((i + p) % GROUPS)}, device_id_type=MESH
        )
        return 0

    lax.fori_loop(1, GROUPS, greet, 0)

    def inside(dx, dz):
        return (s + dx >= 0) & (s + dx < ns) & (i + dz >= 0) & (i + dz < GROUPS)

    for dx, dz in DIRS:
        if dx == 0:
            continue

        @pl.when(inside(dx, dz))
        def _():
            pl.semaphore_signal(
                barrier, inc=1,
                device_id={"space": s + dx, "terms": term_of(i + dz)},
                device_id_type=MESH,
            )

    def pack(c):
        j0, n = CHUNKS[c]

        def one(m, _):
            j, x = j0 + m // 2, m % 2
            rows = [
                fin[pl.ds(pl.multiple_of((j * 6 + a * 2 + x) * 32, 32), 32), :] for a in range(3)
            ]
            turned = jnp.transpose(jnp.concatenate(rows + [jnp.zeros((32, 128), jnp.float32)], axis=0))
            sb[c][:, m] = turned.reshape(GROUPS, 8, 128)
            return 0

        lax.fori_loop(0, 2 * n, one, 0)

    def wait_barrier():
        sides = jnp.where((s > 0) & (s < ns - 1), 2, 1) if ns > 1 else 0
        rows_of = jnp.where((i > 0) & (i < GROUPS - 1), 3, 2)
        pl.semaphore_wait(barrier, GROUPS - 1 + sides * rows_of)

    def leaving(c, p, src, dst, s_sem, r_sem, inward):
        i2 = (i + p) % GROUPS
        k2 = term_of(i2)
        return pltpu.make_async_remote_copy(
            src_ref=src.at[i2 if inward else k2],
            dst_ref=dst.at[k if inward else i],
            send_sem=s_sem.at[c, p],
            recv_sem=r_sem.at[c, p],
            device_id={"terms": k2},
            device_id_type=MESH,
        )

    def arriving(c, p, src, dst, s_sem, r_sem, inward):
        i2 = (i - p + GROUPS) % GROUPS
        k2 = term_of(i2)
        return pltpu.make_async_remote_copy(
            src_ref=src.at[0],
            dst_ref=dst.at[k2 if inward else i2],
            send_sem=s_sem.at[c, p],
            recv_sem=r_sem.at[c, p],
            device_id={"terms": k2},
            device_id_type=MESH,
        )

    def over_peers(fn):
        def one(p, _):
            fn(p)
            return 0

        lax.fori_loop(1, GROUPS, one, 0)

    def send_in(c):
        over_peers(lambda p: leaving(c, p, sb[c], rb[c], in_s, in_r, True).start())
        rb[c][k] = sb[c][i]

    def wait_in(c):
        over_peers(lambda p: arriving(c, p, sb[c], rb[c], in_s, in_r, True).wait_recv())

    def send_out(c):
        over_peers(lambda p: leaving(c, p, ob[c], qb[c], out_s, out_r, False).start())
        qb[c][i] = ob[c][k]

    def wait_out(c):
        over_peers(lambda p: arriving(c, p, ob[c], qb[c], out_s, out_r, False).wait_recv())

    pack(0)
    wait_barrier()
    send_in(0)
    pack(1)
    send_in(1)

    lane8 = lax.broadcasted_iota(jnp.int32, (8, 128), 1)

    def locate(g, acc):
        for j in range(SLOT_DEV):
            acc = jnp.where(lane8 == slots[g * SLOT_DEV + j], g * 16 + j, acc)
        return acc

    posv[...] = lax.fori_loop(0, GROUPS, locate, jnp.zeros((8, 128), jnp.int32))
    to_smem = pltpu.make_async_copy(posv, pos, pos_sem)
    to_smem.start()

    for which in range(2):
        for w in (wh, wl):
            w[which, 9 * 128 :, 0:128] = jnp.zeros((384, 128), jnp.bfloat16)
            w[which, 0 : 3 * 128, 128:256] = jnp.zeros((384, 128), jnp.bfloat16)
    lane1 = lax.broadcasted_iota(jnp.int32, (1, 128), 1)
    group = lane1 // 32

    def by_group(v0, v1, v2):
        return jnp.where(
            group == 0, v0, jnp.where(group == 1, v1, jnp.where(group == 2, v2, 0.0))
        ).astype(jnp.float32)

    def splat(v):
        return jnp.full((1, 128), v, jnp.float32)

    inv = [1.0 / splat(sten[a, a, 13]) for a in range(3)]
    inv_lane = by_group(*inv)
    apart = lax.broadcasted_iota(jnp.int32, (32, 128), 0) - lax.broadcasted_iota(
        jnp.int32, (32, 128), 1
    ) % 32

    def table(m, _):
        dx, dz = m // 3, m % 3
        for b in range(4):
            block = [jnp.zeros((32, 128), jnp.float32)] * 2
            if b < 3:
                for dy in range(3):
                    o = dx * 9 + dy * 3 + dz
                    plain = by_group(*[splat(sten[a, b, o]) for a in range(3)])
                    smooth = -(plain * inv_lane) * inv[b]
                    if dy == 1:
                        centre = (group == b) & ((dx == 1) & (dz == 1))
                        smooth = jnp.where(centre, inv_lane, smooth)
                    for which, line in enumerate((smooth, plain)):
                        block[which] = jnp.where(apart == dy - 1, line, block[which])
            for which in range(2):
                hi = block[which].astype(jnp.bfloat16)
                lo = (block[which] - hi.astype(jnp.float32)).astype(jnp.bfloat16)
                if which == 0:
                    row = pl.multiple_of((dx * 3 + dz) * 128 + b * 32, 32)
                    wc[pl.ds(row, 32), 0:128] = hi
                    wc[pl.ds(row, 32), 128:256] = lo
                for px in range(2):
                    row = pl.multiple_of(((dx + px) * 3 + dz) * 128 + b * 32, 32)
                    wh[which, pl.ds(row, 32), px * 128 : px * 128 + 128] = hi
                    wl[which, pl.ds(row, 32), px * 128 : px * 128 + 128] = lo
        return 0

    lax.fori_loop(0, 9, table, 0)

    def field(m, _):
        rows = fl[m // 2, m % 2]
        ft[...] = jnp.transpose(jnp.concatenate([rows] * 4, axis=0))
        ff[m] = ft[pl.ds(pl.multiple_of(8 * i, 8), 8), :]
        return 0

    lax.fori_loop(0, 2 * DIMS, field, 0)

    def zero_outside(buf, rim, count, wide):
        def layer(x):
            def one(t, _):
                buf[x, t] = jnp.zeros((24, 128), jnp.float32)
                return 0

            lax.fori_loop(0, count, one, 0)
            for side in range(2):
                if wide:
                    for row in range(3):
                        rim[side, row, x] = jnp.zeros(rim.shape[3:], jnp.float32)
                else:
                    rim[side, x] = jnp.zeros(rim.shape[2:], jnp.float32)

        def edge(side):
            if wide:
                for row in (side, side + 1):
                    rim[side, row] = jnp.zeros(rim.shape[2:], jnp.float32)
            else:
                rim[side] = jnp.zeros(rim.shape[1:], jnp.float32)

        for x in (0, 1) if wide else (0,):
            pl.when(s == 0)(lambda x=x: layer(x))
        for x in (4, 5) if wide else (3,):
            pl.when(s == ns - 1)(lambda x=x: layer(x))
        pl.when(i == 0)(lambda: edge(0))
        pl.when(i == GROUPS - 1)(lambda: edge(1))

    for lv in range(5):
        zero_outside(load_buf[lv], rims[2 * lv], COUNT[lv], WIDE[lv])
        if lv < 4 and not WIDE[lv]:
            zero_outside(sett_buf[lv], rims[2 * lv + 1], COUNT[lv], False)

    pack(2)
    pack(3)
    to_smem.wait()

    def halo_copy(q, n, e, buf, part):
        t0, count, n8 = part
        dx, dz = DIRS[n]
        sx, tx = {1: (2, 0), -1: (1, 3), 0: (0, 0)}[dx]
        if buf.shape[0] == 6:
            tx = {1: 0, -1: 4, 0: 2}[dx]
            if dz == 0:
                src = buf.at[2:4, t0 : t0 + count, 8:16, :]
                dst = buf.at[tx : tx + 2, t0 : t0 + count, 8:16, :]
            else:
                side = 1 if dz > 0 else 0
                src = faces[e].at[side]
                dst = rims[e].at[1 - side, 1 - side : 3 - side, tx : tx + 2]
        elif dz == 0:
            src = buf.at[sx, t0 : t0 + count, 8:16, :]
            dst = buf.at[tx, t0 : t0 + count, 8:16, :]
        else:
            side = 1 if dz > 0 else 0
            if dx == 0:
                src = faces[e].at[side, :, t0 : t0 + n8]
                dst = rims[e].at[1 - side, 1:3, t0 : t0 + n8]
            else:
                src = faces[e].at[side, sx - 1, t0 : t0 + n8]
                dst = rims[e].at[1 - side, tx, t0 : t0 + n8]
        return pltpu.make_async_remote_copy(
            src_ref=src,
            dst_ref=dst,
            send_sem=h_s.at[q, n],
            recv_sem=h_r.at[q, n],
            device_id={"space": s + dx, "terms": term_of(i + dz)},
            device_id_type=MESH,
        )

    def by_five(part, fn):
        t0, count, _ = part
        w = next(w for w in (5, 4, 1) if count % w == 0) if count != 19 and count != 38 else 19

        def some(u, _):
            for v in range(w):
                fn(t0 + u * w + v)
            return 0

        lax.fori_loop(0, count // w, some, 0)

    exchanges = []

    def start_exchange(e, buf, part):
        args = (len(exchanges), e, buf, part)
        exchanges.append(args)
        for n, (dx, dz) in enumerate(DIRS):
            pl.when(inside(dx, dz))(lambda n=n: halo_copy(args[0], n, *args[1:]).start())
        return args

    def end_exchange(q, e, buf, part):
        for n, (dx, dz) in enumerate(DIRS):
            pl.when(inside(-dx, -dz))(lambda n=n: halo_copy(q, n, e, buf, part).wait_recv())
        spread_rim(e, buf, part)

    def spread_rim(e, buf, part):
        def spread(t):
            for x in range(4):
                buf[x, t, 7:8, :] = rims[e][0, x, pl.ds(t, 1), :]
                buf[x, t, 16:17, :] = rims[e][1, x, pl.ds(t, 1), :]

        def spread_wide(t):
            for x in range(6):
                buf[x, t, 7:8, :] = rims[e][0, 1, x, pl.ds(t, 1), :]
                buf[x, t, 16:17, :] = rims[e][1, 1, x, pl.ds(t, 1), :]
                rims[e][0, 2, x, pl.ds(t, 1), :] = buf[x, t, 8:9, :]
                rims[e][1, 0, x, pl.ds(t, 1), :] = buf[x, t, 15:16, :]

        by_five(part, spread_wide if buf.shape[0] == 6 else spread)

    def halves(v):
        hi = v.astype(jnp.bfloat16)
        return hi, (v - hi.astype(jnp.float32)).astype(jnp.bfloat16)

    def product(rows, which):
        both = dot(xs[0 : 2 * rows, :], wh[which])
        return both[0:rows] + both[rows:] + dot(xs[0:rows, :], wl[which])

    def settle_wide(lv):
        src, rim, step, t8 = load_buf[lv], rims[2 * lv], STEP[lv], T8[lv]
        base = 16 * step
        rows = base + 4 * t8

        def put(row, col, v):
            hi, lo = halves(v)
            xs[pl.ds(pl.multiple_of(row, 16), v.shape[0]), col : col + 128] = hi
            xs[pl.ds(pl.multiple_of(rows + row, 16), v.shape[0]), col : col + 128] = lo

        def pair(u, _):
            for dz in range(3):
                for w in range(4):
                    for b in range(2):
                        v = [src[2 * b + w, 2 * u + h, 7 + dz : 15 + dz, :] for h in range(2)]
                        put(b * 8 * step + u * 16, (w * 3 + dz) * 128, jnp.concatenate(v, axis=0))
            return 0

        lax.fori_loop(0, step // 2, pair, 0)
        for side in range(2):
            for dz in range(3):
                for w in range(4):
                    v = [rim[side, dz, 2 * b + w] for b in range(2)]
                    put(base + side * 2 * t8, (w * 3 + dz) * 128, jnp.concatenate(v, axis=0))
        res = product(rows, 0)
        one, zero = jnp.float32(1.0), jnp.float32(0.0)
        in_x = [jnp.where(s > 0, one, zero), one, one, jnp.where(s < ns - 1, one, zero)]
        in_z = [jnp.where(i > 0, one, zero), jnp.where(i < GROUPS - 1, one, zero)]
        for x in range(4):
            b, lanes = x // 2, slice(128 * (x % 2), 128 * (x % 2) + 128)
            v = res[b * 8 * step : (b + 1) * 8 * step, lanes].reshape(step, 8, 128)
            if x in (1, 2):
                own_buf[lv][x - 1, 0:step] = v
            else:
                v = v * in_x[x]
            sett_buf[lv][x, 0:step, 8:16, :] = v
            for side in range(2):
                row = base + side * 2 * t8 + b * t8
                rims[2 * lv + 1][side, x] = res[row : row + t8, lanes] * (in_x[x] * in_z[side])

    def stage_rows(src, part, lo_at, at=0):
        t0, count, _ = part

        def pair(u, _):
            t = t0 + 2 * u
            for dz in range(3):
                for x in range(4):
                    v = jnp.concatenate(
                        [src[x, t, 7 + dz : 15 + dz, :], src[x, t + 1, 7 + dz : 15 + dz, :]], axis=0
                    )
                    hi, lo = halves(v)
                    col = (x * 3 + dz) * 128
                    xs[pl.ds(pl.multiple_of(at + u * 16, 16), 16), col : col + 128] = hi
                    xs[pl.ds(pl.multiple_of(lo_at + u * 16, 16), 16), col : col + 128] = lo
            return 0

        lax.fori_loop(0, (count + 1) // 2, pair, 0)

    def apply(src, part, which, store):
        step = (part[1] + 1) // 2 * 2
        stage_rows(src, part, 8 * step)
        res = product(8 * step, which)
        for px in range(2):
            store(px, part[0], res[:, px * 128 : px * 128 + 128].reshape(step, 8, 128))

    pending = []
    for lv in range(5):
        c, j0 = CHUNK_OF[lv]
        if lv == 0 or c != CHUNK_OF[lv - 1][0]:
            wait_in(c)
        if lv == 0:
            send_in(2)

        def load_of(t):
            q = pos[0, START[lv] + t]
            g = q // 16
            j = j0 + jnp.clip(q % 16 - BASE[lv], 0, CAP[lv] - 1)
            parts = [rb[c][g, 2 * j + x] for x in range(2)]
            if lv > 0:
                for d in range(DIMS):
                    par = ptab[(START[lv] + t) * DIMS + d]
                    weight = jnp.where(par >= 0, cp[d, START[lv] + t], 0.0)
                    at = jnp.maximum(par, 0)
                    for x in range(2):
                        parts[x] = parts[x] - (weight * ff[2 * d + x]) * img_buf[lv - 1][x, at]
            for x in range(2):
                load_buf[lv][(2 if WIDE[lv] else 1) + x, t, 8:16, :] = parts[x]
                if WIDE[lv]:
                    for row in range(2):
                        faces[2 * lv][0, row, x, pl.ds(t, 1), :] = parts[x][row : row + 1]
                        faces[2 * lv][1, row, x, pl.ds(t, 1), :] = parts[x][6 + row : 7 + row]
                else:
                    faces[2 * lv][0, x, pl.ds(t, 1), :] = parts[x][0:1]
                    faces[2 * lv][1, x, pl.ds(t, 1), :] = parts[x][7:8]

        started = []
        for part in PARTS[lv]:
            by_five(part, load_of)
            started.append(start_exchange(2 * lv, load_buf[lv], part))
        if pending:
            pending.pop()()
        if lv == 1:
            send_in(3)

        def deliver_to(o, j0, layers, lv=lv):
            def deliver(g, _):
                for j in range(CAP[lv]):
                    q = slots[g * SLOT_DEV + BASE[lv] + j]
                    t = jnp.clip(q - START[lv], 0, COUNT[lv] - 1)
                    for n, x in enumerate(layers):
                        v = own_buf[lv][x, t]
                        ob[o][g, len(layers) * (j0 + j) + n] = jnp.where(q >= 0, v, 0.0)
                return 0

            lax.fori_loop(0, GROUPS, deliver, 0)

        def face(t):
            for x in range(2):
                faces[2 * lv + 1][0, x, pl.ds(t, 1), :] = sett_buf[lv][1 + x, t, 8:9, :]
                faces[2 * lv + 1][1, x, pl.ds(t, 1), :] = sett_buf[lv][1 + x, t, 15:16, :]

        def settle(px, t0, v):
            own_buf[lv][px, t0 : t0 + v.shape[0]] = v
            sett_buf[lv][1 + px, t0 : t0 + v.shape[0], 8:16, :] = v

        def image(px, t0, v):
            img_buf[lv][px, t0 : t0 + v.shape[0]] = v

        if WIDE[lv]:
            end_exchange(*started[0])
            settle_wide(lv)
            spread_rim(2 * lv + 1, sett_buf[lv], PARTS[lv][0])
            apply(sett_buf[lv], PARTS[lv][0], 1, image)

            def finish(lv=lv, c=c, j0=j0, deliver_to=deliver_to):
                deliver_to(c, j0, (0, 1))
                if CHUNK_OF[lv + 1][0] != c:
                    send_out(c)

            pending.append(finish)
        elif lv < 4:
            rimmed = []
            for part, args in zip(PARTS[lv], started):
                end_exchange(*args)
                apply(load_buf[lv], part, 0, settle)
                by_five(part, face)
                rimmed.append(start_exchange(2 * lv + 1, sett_buf[lv], part))
            deliver_to(c, j0, (0, 1))
            for part, args in zip(PARTS[lv], rimmed):
                end_exchange(*args)
                apply(sett_buf[lv], part, 1, image)
            send_out(c)
        else:
            lo_at = 8 * COUNT[lv]
            for px in range(2):
                for part, args in zip(PARTS[lv], started):
                    at, n = 8 * part[0], 8 * part[1]
                    if px == 0:
                        end_exchange(*args)
                        stage_rows(load_buf[lv], part, lo_at + at, at)
                    cols = slice(384 * px, 384 * px + 1152)
                    wide = dot(xs[at : at + n, cols], wc[...])
                    res = dot(xs[lo_at + at : lo_at + at + n, cols], wc[:, 0:128])
                    res = res + wide[:, 0:128] + wide[:, 128:256]
                    own_buf[lv][px, part[0] : part[0] + part[1]] = res.reshape(part[1], 8, 128)
                deliver_to(3 + px, 0, (px,))
                send_out(3 + px)

    for c, (j0, n, layers) in enumerate(OUTS):
        wait_out(c)

        def unpack(m, _, c=c, j0=j0, layers=layers):
            j = j0 + m // len(layers)
            x = m % 2 if len(layers) == 2 else layers[0]
            turned = jnp.transpose(qb[c][:, m].reshape(128, 128))
            for a in range(3):
                row = pl.multiple_of((j * 6 + a * 2 + x) * 32, 32)
                out[pl.ds(row, 32), :] = turned[32 * a : 32 * a + 32]
            return 0

        lax.fori_loop(0, len(layers) * n, unpack, 0)

    for c in range(len(CHUNKS)):
        over_peers(lambda p: leaving(c, p, sb[c], rb[c], in_s, in_r, True).wait_send())
    for c in range(len(OUTS)):
        over_peers(lambda p: leaving(c, p, ob[c], qb[c], out_s, out_r, False).wait_send())
    for q, e, buf, part in exchanges:
        for n, (dx, dz) in enumerate(DIRS):
            pl.when(inside(dx, dz))(lambda n=n: halo_copy(q, n, e, buf, part).wait_send())


def on_device(ns, forcing, stencil, fields, coupling, slot_term):
    rows = forcing.shape[0] * 6 * 32
    vm = pl.BlockSpec(memory_space=pltpu.VMEM)
    sm = pl.BlockSpec(memory_space=pltpu.SMEM)
    f32, bf16 = jnp.float32, jnp.bfloat16
    dma = pltpu.SemaphoreType.DMA
    scratch = [pltpu.VMEM((GROUPS, 2 * n, 8, 128), f32) for _ in range(2) for _, n in CHUNKS]
    scratch += [
        pltpu.VMEM((GROUPS, len(x) * n, 8, 128), f32) for _ in range(2) for _, n, x in OUTS
    ]
    scratch += [pltpu.VMEM((6 if WIDE[lv] else 4, T8[lv], 24, 128), f32) for lv in range(5)]
    scratch += [pltpu.VMEM((4, T8[lv], 24, 128), f32) for lv in range(4)]
    scratch += [pltpu.VMEM((2, T8[lv], 8, 128), f32) for lv in range(5)]
    scratch += [pltpu.VMEM((2, T8[lv], 8, 128), f32) for lv in range(4)]
    wide = [WIDE[e // 2] and e % 2 == 0 for e in range(9)]
    scratch += [pltpu.VMEM((2,) + (2,) * w + (2, T8[e // 2], 128), f32) for e, w in enumerate(wide)]
    scratch += [
        pltpu.VMEM((2, 3, 6, T8[e // 2], 128) if w else (2, 4, T8[e // 2], 128), f32)
        for e, w in enumerate(wide)
    ]
    scratch += [
        pltpu.VMEM((2, 12 * 128, 256), bf16),
        pltpu.VMEM((2, 12 * 128, 256), bf16),
        pltpu.VMEM((9 * 128, 256), bf16),
        pltpu.VMEM((16 * COUNT[4], 12 * 128), bf16),
        pltpu.VMEM((2 * DIMS, 8, 128), f32),
        pltpu.VMEM((128, 128), f32),
        pltpu.VMEM((8, 128), jnp.int32),
        pltpu.SMEM((8, 128), jnp.int32),
        dma(()),
    ]
    scratch += [dma((len(CHUNKS), GROUPS)) for _ in range(2)]
    scratch += [dma((len(OUTS), GROUPS)) for _ in range(2)] + [dma((9, 8)) for _ in range(2)]
    out = pl.pallas_call(
        functools.partial(kernel, ns),
        out_shape=jax.ShapeDtypeStruct((rows, 128), f32),
        in_specs=[vm, vm, sm, sm, sm, sm],
        out_specs=vm,
        scratch_shapes=scratch,
        compiler_params=pltpu.CompilerParams(
            collective_id=0, has_side_effects=True, vmem_limit_bytes=32 << 20
        ),
    )(forcing.reshape(rows, 128), fields, coupling.T, jnp.asarray(parent_table()), slot_term, stencil.transpose(1, 2, 0))
    return out.reshape(forcing.shape)


def solution(mesh):
    return jax.shard_map(
        functools.partial(on_device, mesh.shape["space"]),
        mesh=mesh,
        in_specs=(
            P("terms", None, "space", None, None),
            P(),
            P(None, "space", None, None),
            P(),
            P(),
        ),
        out_specs=P("terms", None, "space", None, None),
        check_vma=False,
    )
```

```python
import functools

import jax
import jax.numpy as jnp
import numpy as np
from jax import lax
from jax.experimental import pallas as pl
from jax.experimental.pallas import tpu as pltpu
from jax.sharding import PartitionSpec as P

DIMS = 5
TERMS = 126
GROUPS = 16
SLOT_DEV = 11
COUNT = (1, 5, 15, 35, 70)
START = (0, 1, 6, 21, 56)
CAP = (1, 1, 1, 3, 5)
BASE = (0, 1, 2, 3, 6)
T8 = (8, 8, 16, 40, 72)
STEP = (2, 6, 16, 0, 0)
PARTS = (((0, 1, 8),), ((0, 5, 8),), ((0, 15, 16),), ((0, 16, 16), (16, 19, 24)), ((0, 32, 32), (32, 38, 40)))
WIDE = (True, True, True, False, False)
CHUNKS = ((0, 1), (1, 2), (3, 3), (6, 5))
OUTS = ((0, 1, (0, 1)), (1, 2, (0, 1)), (3, 3, (0, 1)), (6, 5, (0,)), (6, 5, (1,)))
CHUNK_OF = ((0, 0), (1, 0), (1, 1), (2, 0), (3, 0))
DIRS = tuple((dx, dz) for dx in (-1, 0, 1) for dz in (-1, 0, 1) if (dx, dz) != (0, 0))
MESH = pl.DeviceIdType.MESH


def compositions(total, pieces_left):
    if pieces_left == 1:
        return [[total]]
    result = []
    for leading in range(total, -1, -1):
        for remainder in compositions(total - leading, pieces_left - 1):
            result.append([leading] + remainder)
    return result


def parent_table():
    table = np.full((TERMS, DIMS), -1, np.int32)
    for level in range(1, 5):
        below = {tuple(v): n for n, v in enumerate(compositions(level - 1, DIMS))}
        for n, v in enumerate(compositions(level, DIMS)):
            for d in range(DIMS):
                if v[d] > 0:
                    w = list(v)
                    w[d] -= 1
                    table[START[level] + n, d] = below[tuple(w)]
    return table.reshape(-1)


def dot(a, b):
    return jnp.dot(a, b, preferred_element_type=jnp.float32)


def term_of(i):
    q, r = i // 4, i % 4
    return q * 4 + r + (q % 2) * (3 - 2 * r)


def kernel(ns, *refs):
    given, out, it = refs[:6], refs[6], iter(refs[7:])
    fin, fl, cp, ptab, slots, sten, given_sem = [next(it) for _ in range(7)]
    fetch = [
        pltpu.make_async_copy(src, dst, given_sem.at[n])
        for n, (src, dst) in enumerate(zip(given, (fin, fl, cp, ptab, slots, sten)))
    ]
    for copy in fetch:
        copy.start()
    sb = [next(it) for _ in CHUNKS]
    rb = [next(it) for _ in CHUNKS]
    ob = [next(it) for _ in OUTS]
    qb = [next(it) for _ in OUTS]
    load_buf = [next(it) for _ in range(5)]
    sett_buf = [next(it) for _ in range(4)]
    own_buf = [next(it) for _ in range(5)]
    img_buf = [next(it) for _ in range(4)]
    faces = [next(it) for _ in range(9)]
    rims = [next(it) for _ in range(9)]
    wh, wc, xs, low, ff, ft, posv, pos, pos_sem = [next(it) for _ in range(9)]
    in_s, in_r, out_s, out_r, h_s, h_r = [next(it) for _ in range(6)]

    s = lax.axis_index("space")
    k = lax.axis_index("terms")
    i = term_of(k)

    barrier = pltpu.get_barrier_semaphore()

    def greet(p, _):
        pl.semaphore_signal(
            barrier, inc=1, device_id={"terms": term_of((i + p) % GROUPS)}, device_id_type=MESH
        )
        return 0

    lax.fori_loop(1, GROUPS, greet, 0)

    def inside(dx, dz):
        return (s + dx >= 0) & (s + dx < ns) & (i + dz >= 0) & (i + dz < GROUPS)

    for dx, dz in DIRS:
        if dx == 0:
            continue

        @pl.when(inside(dx, dz))
        def _():
            pl.semaphore_signal(
                barrier, inc=1,
                device_id={"space": s + dx, "terms": term_of(i + dz)},
                device_id_type=MESH,
            )

    def pack(c):
        j0, n = CHUNKS[c]

        def one(m, _):
            j, x = j0 + m // 2, m % 2
            rows = [
                fin[pl.ds(pl.multiple_of((j * 6 + a * 2 + x) * 32, 32), 32), :] for a in range(3)
            ]
            turned = jnp.transpose(jnp.concatenate(rows + [jnp.zeros((32, 128), jnp.float32)], axis=0))
            sb[c][:, m] = turned.reshape(GROUPS, 8, 128)
            return 0

        lax.fori_loop(0, 2 * n, one, 0)

    def wait_barrier():
        sides = jnp.where((s > 0) & (s < ns - 1), 2, 1) if ns > 1 else 0
        rows_of = jnp.where((i > 0) & (i < GROUPS - 1), 3, 2)
        pl.semaphore_wait(barrier, GROUPS - 1 + sides * rows_of)

    def leaving(c, p, src, dst, s_sem, r_sem, inward):
        i2 = (i + p) % GROUPS
        k2 = term_of(i2)
        return pltpu.make_async_remote_copy(
            src_ref=src.at[i2 if inward else k2],
            dst_ref=dst.at[k if inward else i],
            send_sem=s_sem.at[c, p],
            recv_sem=r_sem.at[c, p],
            device_id={"terms": k2},
            device_id_type=MESH,
        )

    def arriving(c, p, src, dst, s_sem, r_sem, inward):
        i2 = (i - p + GROUPS) % GROUPS
        k2 = term_of(i2)
        return pltpu.make_async_remote_copy(
            src_ref=src.at[0],
            dst_ref=dst.at[k2 if inward else i2],
            send_sem=s_sem.at[c, p],
            recv_sem=r_sem.at[c, p],
            device_id={"terms": k2},
            device_id_type=MESH,
        )

    def over_peers(fn):
        def one(p, _):
            fn(p)
            return 0

        lax.fori_loop(1, GROUPS, one, 0)

    def send_in(c):
        over_peers(lambda p: leaving(c, p, sb[c], rb[c], in_s, in_r, True).start())
        rb[c][k] = sb[c][i]

    def wait_in(c):
        over_peers(lambda p: arriving(c, p, sb[c], rb[c], in_s, in_r, True).wait_recv())

    def send_out(c):
        over_peers(lambda p: leaving(c, p, ob[c], qb[c], out_s, out_r, False).start())
        qb[c][i] = ob[c][k]

    def wait_out(c):
        over_peers(lambda p: arriving(c, p, ob[c], qb[c], out_s, out_r, False).wait_recv())

    fetch[0].wait()
    pack(0)
    wait_barrier()
    send_in(0)
    pack(1)
    send_in(1)

    for copy in fetch[1:]:
        copy.wait()
    lane8 = lax.broadcasted_iota(jnp.int32, (8, 128), 1)

    def locate(g, acc):
        for j in range(SLOT_DEV):
            acc = jnp.where(lane8 == slots[g * SLOT_DEV + j], g * 16 + j, acc)
        return acc

    posv[...] = lax.fori_loop(0, GROUPS, locate, jnp.zeros((8, 128), jnp.int32))
    to_smem = pltpu.make_async_copy(posv, pos, pos_sem)
    to_smem.start()

    for which in range(2):
        wh[which, 9 * 128 :, 0:128] = jnp.zeros((384, 128), jnp.bfloat16)
        wh[which, 0 : 3 * 128, 128:256] = jnp.zeros((384, 128), jnp.bfloat16)
    lane1 = lax.broadcasted_iota(jnp.int32, (1, 128), 1)
    group = lane1 // 32

    def by_group(v0, v1, v2):
        return jnp.where(
            group == 0, v0, jnp.where(group == 1, v1, jnp.where(group == 2, v2, 0.0))
        ).astype(jnp.float32)

    def splat(v):
        return jnp.full((1, 128), v, jnp.float32)

    inv = [1.0 / splat(sten[a, a, 13]) for a in range(3)]
    inv_lane = by_group(*inv)
    apart = lax.broadcasted_iota(jnp.int32, (32, 128), 0) - lax.broadcasted_iota(
        jnp.int32, (32, 128), 1
    ) % 32

    def table(m, _):
        dx, dz = m // 3, m % 3
        for b in range(4):
            block = [jnp.zeros((32, 128), jnp.float32)] * 2
            if b < 3:
                for dy in range(3):
                    o = dx * 9 + dy * 3 + dz
                    plain = by_group(*[splat(sten[a, b, o]) for a in range(3)])
                    smooth = -(plain * inv_lane) * inv[b]
                    if dy == 1:
                        centre = (group == b) & ((dx == 1) & (dz == 1))
                        smooth = jnp.where(centre, inv_lane, smooth)
                    for which, line in enumerate((smooth, plain)):
                        block[which] = jnp.where(apart == dy - 1, line, block[which])
            for which in range(2):
                hi = block[which].astype(jnp.bfloat16)
                lo = (block[which] - hi.astype(jnp.float32)).astype(jnp.bfloat16)
                row = pl.multiple_of((dx * 3 + dz) * 128 + b * 32, 32)
                wc[which, pl.ds(row, 32), 0:128] = hi
                wc[which, pl.ds(row, 32), 128:256] = lo
                for px in range(2):
                    row = pl.multiple_of(((dx + px) * 3 + dz) * 128 + b * 32, 32)
                    wh[which, pl.ds(row, 32), px * 128 : px * 128 + 128] = hi
        return 0

    lax.fori_loop(0, 9, table, 0)

    def field(m, _):
        rows = fl[m // 2, m % 2]
        ft[...] = jnp.transpose(jnp.concatenate([rows] * 4, axis=0))
        ff[m] = ft[pl.ds(pl.multiple_of(8 * i, 8), 8), :]
        return 0

    lax.fori_loop(0, 2 * DIMS, field, 0)

    def zero_outside(buf, rim, count, wide):
        def layer(x):
            def one(t, _):
                buf[x, t] = jnp.zeros((24, 128), jnp.float32)
                return 0

            lax.fori_loop(0, count, one, 0)
            for side in range(2):
                if wide:
                    for row in range(3):
                        rim[side, row, x] = jnp.zeros(rim.shape[3:], jnp.float32)
                else:
                    rim[side, x] = jnp.zeros(rim.shape[2:], jnp.float32)

        def edge(side):
            if wide:
                for row in (side, side + 1):
                    rim[side, row] = jnp.zeros(rim.shape[2:], jnp.float32)
            else:
                rim[side] = jnp.zeros(rim.shape[1:], jnp.float32)

        for x in (0, 1) if wide else (0,):
            pl.when(s == 0)(lambda x=x: layer(x))
        for x in (4, 5) if wide else (3,):
            pl.when(s == ns - 1)(lambda x=x: layer(x))
        pl.when(i == 0)(lambda: edge(0))
        pl.when(i == GROUPS - 1)(lambda: edge(1))

    for lv in range(5):
        zero_outside(load_buf[lv], rims[2 * lv], COUNT[lv], WIDE[lv])
        if lv < 4 and not WIDE[lv]:
            zero_outside(sett_buf[lv], rims[2 * lv + 1], COUNT[lv], False)

    pack(2)
    pack(3)
    to_smem.wait()

    def halo_copy(q, n, e, buf, part):
        t0, count, n8 = part
        dx, dz = DIRS[n]
        sx, tx = {1: (2, 0), -1: (1, 3), 0: (0, 0)}[dx]
        if buf.shape[0] == 6:
            tx = {1: 0, -1: 4, 0: 2}[dx]
            if dz == 0:
                src = buf.at[2:4, t0 : t0 + count, 8:16, :]
                dst = buf.at[tx : tx + 2, t0 : t0 + count, 8:16, :]
            else:
                side = 1 if dz > 0 else 0
                src = faces[e].at[side]
                dst = rims[e].at[1 - side, 1 - side : 3 - side, tx : tx + 2]
        elif dz == 0:
            src = buf.at[sx, t0 : t0 + count, 8:16, :]
            dst = buf.at[tx, t0 : t0 + count, 8:16, :]
        else:
            side = 1 if dz > 0 else 0
            if dx == 0:
                src = faces[e].at[side, :, t0 : t0 + n8]
                dst = rims[e].at[1 - side, 1:3, t0 : t0 + n8]
            else:
                src = faces[e].at[side, sx - 1, t0 : t0 + n8]
                dst = rims[e].at[1 - side, tx, t0 : t0 + n8]
        return pltpu.make_async_remote_copy(
            src_ref=src,
            dst_ref=dst,
            send_sem=h_s.at[q, n],
            recv_sem=h_r.at[q, n],
            device_id={"space": s + dx, "terms": term_of(i + dz)},
            device_id_type=MESH,
        )

    def by_five(part, fn):
        t0, count, _ = part
        w = next(w for w in (5, 4, 1) if count % w == 0) if count != 19 and count != 38 else 19

        def some(u, _):
            for v in range(w):
                fn(t0 + u * w + v)
            return 0

        lax.fori_loop(0, count // w, some, 0)

    exchanges = []

    def start_exchange(e, buf, part):
        args = (len(exchanges), e, buf, part)
        exchanges.append(args)
        for n, (dx, dz) in enumerate(DIRS):
            pl.when(inside(dx, dz))(lambda n=n: halo_copy(args[0], n, *args[1:]).start())
        return args

    def end_exchange(q, e, buf, part):
        for n, (dx, dz) in enumerate(DIRS):
            pl.when(inside(-dx, -dz))(lambda n=n: halo_copy(q, n, e, buf, part).wait_recv())
        spread_rim(e, buf, part)

    def spread_rim(e, buf, part):
        def spread(t):
            for x in range(4):
                buf[x, t, 7:8, :] = rims[e][0, x, pl.ds(t, 1), :]
                buf[x, t, 16:17, :] = rims[e][1, x, pl.ds(t, 1), :]

        def spread_wide(t):
            for x in range(6):
                buf[x, t, 7:8, :] = rims[e][0, 1, x, pl.ds(t, 1), :]
                buf[x, t, 16:17, :] = rims[e][1, 1, x, pl.ds(t, 1), :]
                rims[e][0, 2, x, pl.ds(t, 1), :] = buf[x, t, 8:9, :]
                rims[e][1, 0, x, pl.ds(t, 1), :] = buf[x, t, 15:16, :]

        by_five(part, spread_wide if buf.shape[0] == 6 else spread)

    def halves(v):
        hi = v.astype(jnp.bfloat16)
        return hi, (v - hi.astype(jnp.float32)).astype(jnp.bfloat16)

    def product(rows, which):
        rest = dot(xs[rows : 2 * rows, :], wh[which])
        return [main(0, rows, px, which) + rest[:, 128 * px : 128 * px + 128] for px in range(2)]

    def main(at, rows, px, which):
        both = dot(xs[at : at + rows, 384 * px : 384 * px + 1152], wc[which])
        return both[:, 0:128] + both[:, 128:256]

    def settle_wide(lv):
        src, rim, step, t8 = load_buf[lv], rims[2 * lv], STEP[lv], T8[lv]
        base = 16 * step
        rows = base + 4 * t8

        def put(row, col, v):
            hi, lo = halves(v)
            xs[pl.ds(pl.multiple_of(row, 16), v.shape[0]), col : col + 128] = hi
            xs[pl.ds(pl.multiple_of(rows + row, 16), v.shape[0]), col : col + 128] = lo

        def pair(u, _):
            for dz in range(3):
                for w in range(4):
                    for b in range(2):
                        v = [src[2 * b + w, 2 * u + h, 7 + dz : 15 + dz, :] for h in range(2)]
                        put(b * 8 * step + u * 16, (w * 3 + dz) * 128, jnp.concatenate(v, axis=0))
            return 0

        lax.fori_loop(0, step // 2, pair, 0)
        for side in range(2):
            for dz in range(3):
                for w in range(4):
                    v = [rim[side, dz, 2 * b + w] for b in range(2)]
                    put(base + side * 2 * t8, (w * 3 + dz) * 128, jnp.concatenate(v, axis=0))
        res = product(rows, 0)
        one, zero = jnp.float32(1.0), jnp.float32(0.0)
        in_x = [jnp.where(s > 0, one, zero), one, one, jnp.where(s < ns - 1, one, zero)]
        in_z = [jnp.where(i > 0, one, zero), jnp.where(i < GROUPS - 1, one, zero)]
        for x in range(4):
            b, mine = x // 2, res[x % 2]
            v = mine[b * 8 * step : (b + 1) * 8 * step].reshape(step, 8, 128)
            if x in (1, 2):
                own_buf[lv][x - 1, 0:step] = v
            else:
                v = v * in_x[x]
            sett_buf[lv][x, 0:step, 8:16, :] = v
            for side in range(2):
                row = base + side * 2 * t8 + b * t8
                rims[2 * lv + 1][side, x] = mine[row : row + t8] * (in_x[x] * in_z[side])

    def stage_rows(src, part, lo_at, at=0):
        t0, count, _ = part

        def pair(u, _):
            t = t0 + 2 * u
            for dz in range(3):
                for x in range(4):
                    v = jnp.concatenate(
                        [src[x, t, 7 + dz : 15 + dz, :], src[x, t + 1, 7 + dz : 15 + dz, :]], axis=0
                    )
                    hi, lo = halves(v)
                    col = (x * 3 + dz) * 128
                    xs[pl.ds(pl.multiple_of(at + u * 16, 16), 16), col : col + 128] = hi
                    xs[pl.ds(pl.multiple_of(lo_at + u * 16, 16), 16), col : col + 128] = lo
            return 0

        lax.fori_loop(0, (count + 1) // 2, pair, 0)

    def apply(src, part, which, store):
        step = (part[1] + 1) // 2 * 2
        stage_rows(src, part, 8 * step)
        res = product(8 * step, which)
        for px in range(2):
            store(px, part[0], res[px].reshape(step, 8, 128))

    pending = []
    for lv in range(5):
        c, j0 = CHUNK_OF[lv]
        if lv == 0 or c != CHUNK_OF[lv - 1][0]:
            wait_in(c)
        if lv == 0:
            send_in(2)

        def load_of(t):
            q = pos[0, START[lv] + t]
            g = q // 16
            j = j0 + jnp.clip(q % 16 - BASE[lv], 0, CAP[lv] - 1)
            parts = [rb[c][g, 2 * j + x] for x in range(2)]
            if lv > 0:
                for d in range(DIMS):
                    par = ptab[(START[lv] + t) * DIMS + d]
                    weight = jnp.where(par >= 0, cp[d, START[lv] + t], 0.0)
                    at = jnp.maximum(par, 0)
                    for x in range(2):
                        parts[x] = parts[x] - (weight * ff[2 * d + x]) * img_buf[lv - 1][x, at]
            for x in range(2):
                load_buf[lv][(2 if WIDE[lv] else 1) + x, t, 8:16, :] = parts[x]
                if WIDE[lv]:
                    for row in range(2):
                        faces[2 * lv][0, row, x, pl.ds(t, 1), :] = parts[x][row : row + 1]
                        faces[2 * lv][1, row, x, pl.ds(t, 1), :] = parts[x][6 + row : 7 + row]
                else:
                    faces[2 * lv][0, x, pl.ds(t, 1), :] = parts[x][0:1]
                    faces[2 * lv][1, x, pl.ds(t, 1), :] = parts[x][7:8]

        started = []
        for part in PARTS[lv]:
            by_five(part, load_of)
            started.append(start_exchange(2 * lv, load_buf[lv], part))
        if pending:
            pending.pop()()
        if lv == 1:
            send_in(3)

        def deliver_to(o, j0, layers, lv=lv):
            def deliver(g, _):
                for j in range(CAP[lv]):
                    q = slots[g * SLOT_DEV + BASE[lv] + j]
                    t = jnp.clip(q - START[lv], 0, COUNT[lv] - 1)
                    for n, x in enumerate(layers):
                        v = own_buf[lv][x, t]
                        ob[o][g, len(layers) * (j0 + j) + n] = jnp.where(q >= 0, v, 0.0)
                return 0

            lax.fori_loop(0, GROUPS, deliver, 0)

        def deliver_packed(o, x, lv=lv):
            def deliver(g, _):
                v = []
                for j in range(CAP[lv]):
                    q = slots[g * SLOT_DEV + BASE[lv] + j]
                    t = jnp.clip(q - START[lv], 0, COUNT[lv] - 1)
                    v.append(jnp.where(q >= 0, own_buf[lv][x, t], 0.0))
                r1, r2, r3 = [pltpu.roll(v[1 + n], 96 - 32 * n, 1) for n in range(3)]
                ob[o][g, 0] = jnp.where(lane8 < 96, v[0], r1)
                ob[o][g, 1] = jnp.where(lane8 < 64, r1, r2)
                ob[o][g, 2] = jnp.where(lane8 < 32, r2, r3)
                ob[o][g, 3] = v[4]
                return 0

            lax.fori_loop(0, GROUPS, deliver, 0)

        def face(t):
            for x in range(2):
                faces[2 * lv + 1][0, x, pl.ds(t, 1), :] = sett_buf[lv][1 + x, t, 8:9, :]
                faces[2 * lv + 1][1, x, pl.ds(t, 1), :] = sett_buf[lv][1 + x, t, 15:16, :]

        def settle(px, t0, v):
            own_buf[lv][px, t0 : t0 + v.shape[0]] = v
            sett_buf[lv][1 + px, t0 : t0 + v.shape[0], 8:16, :] = v

        def image(px, t0, v):
            img_buf[lv][px, t0 : t0 + v.shape[0]] = v

        if WIDE[lv]:
            end_exchange(*started[0])
            settle_wide(lv)
            spread_rim(2 * lv + 1, sett_buf[lv], PARTS[lv][0])
            apply(sett_buf[lv], PARTS[lv][0], 1, image)

            def finish(lv=lv, c=c, j0=j0, deliver_to=deliver_to):
                deliver_to(c, j0, (0, 1))
                if CHUNK_OF[lv + 1][0] != c:
                    send_out(c)

            pending.append(finish)
        elif lv < 4:
            rimmed = []
            for part, args in zip(PARTS[lv], started):
                end_exchange(*args)
                apply(load_buf[lv], part, 0, settle)
                by_five(part, face)
                rimmed.append(start_exchange(2 * lv + 1, sett_buf[lv], part))
            deliver_to(c, j0, (0, 1))
            for part, args in zip(PARTS[lv], rimmed):
                end_exchange(*args)
                apply(sett_buf[lv], part, 1, image)
            send_out(c)
        else:
            lo_at = 8 * COUNT[lv]
            for px in range(2):
                for part, args in zip(PARTS[lv], started):
                    at, n = 8 * part[0], 8 * part[1]
                    if px == 0:
                        end_exchange(*args)
                        stage_rows(load_buf[lv], part, lo_at + at, at)
                        low[at : at + n, :] = dot(xs[lo_at + at : lo_at + at + n, :], wh[0])
                    res = main(at, n, px, 0) + low[at : at + n, 128 * px : 128 * px + 128]
                    own_buf[lv][px, part[0] : part[0] + part[1]] = res.reshape(part[1], 8, 128)
                deliver_packed(3 + px, px)
                send_out(3 + px)

    for c, (j0, n, layers) in enumerate(OUTS):
        wait_out(c)
        if len(layers) == 1:
            for m in range(4):
                turned = jnp.transpose(qb[c][:, m].reshape(128, 128))
                for g in range(4 * m, min(4 * m + 4, 15)):
                    row = ((j0 + g // 3) * 6 + g % 3 * 2 + layers[0]) * 32
                    out[row : row + 32, :] = turned[32 * (g - 4 * m) : 32 * (g - 4 * m) + 32]
            continue

        def unpack(m, _, c=c, j0=j0, layers=layers):
            j, x = j0 + m // 2, m % 2
            turned = jnp.transpose(qb[c][:, m].reshape(128, 128))
            for a in range(3):
                row = pl.multiple_of((j * 6 + a * 2 + x) * 32, 32)
                out[pl.ds(row, 32), :] = turned[32 * a : 32 * a + 32]
            return 0

        lax.fori_loop(0, 2 * n, unpack, 0)

    for c in range(len(CHUNKS)):
        over_peers(lambda p: leaving(c, p, sb[c], rb[c], in_s, in_r, True).wait_send())
    for c in range(len(OUTS)):
        over_peers(lambda p: leaving(c, p, ob[c], qb[c], out_s, out_r, False).wait_send())
    for q, e, buf, part in exchanges:
        for n, (dx, dz) in enumerate(DIRS):
            pl.when(inside(dx, dz))(lambda n=n: halo_copy(q, n, e, buf, part).wait_send())


def on_device(ns, forcing, stencil, fields, coupling, slot_term):
    rows = forcing.shape[0] * 6 * 32
    vm = pl.BlockSpec(memory_space=pltpu.VMEM)
    hbm = pl.BlockSpec(memory_space=pltpu.HBM)
    f32, bf16 = jnp.float32, jnp.bfloat16
    dma = pltpu.SemaphoreType.DMA
    scratch = [
        pltpu.VMEM((rows, 128), f32),
        pltpu.VMEM(fields.shape, f32),
        pltpu.SMEM(coupling.shape[::-1], f32),
        pltpu.SMEM((TERMS * DIMS,), jnp.int32),
        pltpu.SMEM(slot_term.shape, jnp.int32),
        pltpu.SMEM((3, 3, 27), f32),
        dma((6,)),
    ]
    scratch += [pltpu.VMEM((GROUPS, 2 * n, 8, 128), f32) for _ in range(2) for _, n in CHUNKS]
    scratch += [
        pltpu.VMEM((GROUPS, 2 * n if len(x) == 2 else 4, 8, 128), f32) for _ in range(2) for _, n, x in OUTS
    ]
    scratch += [pltpu.VMEM((6 if WIDE[lv] else 4, T8[lv], 24, 128), f32) for lv in range(5)]
    scratch += [pltpu.VMEM((4, T8[lv], 24, 128), f32) for lv in range(4)]
    scratch += [pltpu.VMEM((2, T8[lv], 8, 128), f32) for lv in range(5)]
    scratch += [pltpu.VMEM((2, T8[lv], 8, 128), f32) for lv in range(4)]
    wide = [WIDE[e // 2] and e % 2 == 0 for e in range(9)]
    scratch += [pltpu.VMEM((2,) + (2,) * w + (2, T8[e // 2], 128), f32) for e, w in enumerate(wide)]
    scratch += [
        pltpu.VMEM((2, 3, 6, T8[e // 2], 128) if w else (2, 4, T8[e // 2], 128), f32)
        for e, w in enumerate(wide)
    ]
    scratch += [
        pltpu.VMEM((2, 12 * 128, 256), bf16),
        pltpu.VMEM((2, 9 * 128, 256), bf16),
        pltpu.VMEM((16 * COUNT[4], 12 * 128), bf16),
        pltpu.VMEM((8 * COUNT[4], 256), f32),
        pltpu.VMEM((2 * DIMS, 8, 128), f32),
        pltpu.VMEM((128, 128), f32),
        pltpu.VMEM((8, 128), jnp.int32),
        pltpu.SMEM((8, 128), jnp.int32),
        dma(()),
    ]
    scratch += [dma((len(CHUNKS), GROUPS)) for _ in range(2)]
    scratch += [dma((len(OUTS), GROUPS)) for _ in range(2)] + [dma((9, 8)) for _ in range(2)]
    out = pl.pallas_call(
        functools.partial(kernel, ns),
        out_shape=jax.ShapeDtypeStruct((rows, 128), f32),
        in_specs=[hbm] * 6,
        out_specs=vm,
        scratch_shapes=scratch,
        compiler_params=pltpu.CompilerParams(
            collective_id=0, has_side_effects=True, vmem_limit_bytes=58 << 20
        ),
    )(forcing.reshape(rows, 128), fields, coupling.T, jnp.asarray(parent_table()), slot_term, stencil.transpose(1, 2, 0))
    return out.reshape(forcing.shape)


def solution(mesh):
    return jax.shard_map(
        functools.partial(on_device, mesh.shape["space"]),
        mesh=mesh,
        in_specs=(
            P("terms", None, "space", None, None),
            P(),
            P(None, "space", None, None),
            P(),
            P(),
        ),
        out_specs=P("terms", None, "space", None, None),
        check_vma=False,
    )
```

```python
import functools

import jax
import jax.numpy as jnp
import numpy as np
from jax import lax
from jax.experimental import pallas as pl
from jax.experimental.pallas import tpu as pltpu
from jax.sharding import PartitionSpec as P

DIMS = 5
TERMS = 126
GROUPS = 16
SLOT_DEV = 11
COUNT = (1, 5, 15, 35, 70)
START = (0, 1, 6, 21, 56)
CAP = (1, 1, 1, 3, 5)
BASE = (0, 1, 2, 3, 6)
T8 = (8, 8, 16, 40, 72)
STEP = (2, 6, 16, 0, 0)
PARTS = (((0, 1, 8),), ((0, 5, 8),), ((0, 15, 16),), ((0, 16, 16), (16, 19, 24)), ((0, 32, 32), (32, 38, 40)))
WIDE = (True, True, True, False, False)
CHUNKS = ((0, 1), (1, 2), (3, 3), (6, 5))
OUTS = ((0, 1, (0, 1)), (1, 2, (0, 1)), (3, 3, (0, 1)), (6, 5, (0,)), (6, 5, (1,)))
CHUNK_OF = ((0, 0), (1, 0), (1, 1), (2, 0), (3, 0))
DIRS = ((-1, -1), (-1, 1), (1, -1), (1, 1), (0, -1), (0, 1), (-1, 0), (1, 0))
PIECES = ((0, 0, 2), (1, 0, 4), (2, 0, 6), (3, 0, 4), (3, 4, 7), (3, 7, 10))
MESH = pl.DeviceIdType.MESH


def compositions(total, pieces_left):
    if pieces_left == 1:
        return [[total]]
    result = []
    for leading in range(total, -1, -1):
        for remainder in compositions(total - leading, pieces_left - 1):
            result.append([leading] + remainder)
    return result


def parent_table():
    table = np.full((TERMS, DIMS), -1, np.int32)
    for level in range(1, 5):
        below = {tuple(v): n for n, v in enumerate(compositions(level - 1, DIMS))}
        for n, v in enumerate(compositions(level, DIMS)):
            for d in range(DIMS):
                if v[d] > 0:
                    w = list(v)
                    w[d] -= 1
                    table[START[level] + n, d] = below[tuple(w)]
    return table.reshape(-1)


def dot(a, b):
    return jnp.dot(a, b, preferred_element_type=jnp.float32)


def term_of(i):
    q, r = i // 4, i % 4
    return q * 4 + r + (q % 2) * (3 - 2 * r)


def kernel(ns, *refs):
    given, out, it = refs[:6], refs[6], iter(refs[7:])
    fin, fl, cp, ptab, slots, sten, given_sem = [next(it) for _ in range(7)]
    fetch = [
        pltpu.make_async_copy(src, dst, given_sem.at[n])
        for n, (src, dst) in enumerate(zip(given, (fin, fl, cp, ptab, slots, sten)))
    ]
    for copy in fetch:
        copy.start()
    sb = [next(it) for _ in CHUNKS]
    rb = [next(it) for _ in CHUNKS]
    ob = [next(it) for _ in OUTS]
    qb = [next(it) for _ in OUTS]
    load_buf = [next(it) for _ in range(5)]
    sett_buf = [next(it) for _ in range(4)]
    own_buf = [next(it) for _ in range(5)]
    img_buf = [next(it) for _ in range(4)]
    faces = [next(it) for _ in range(9)]
    rims = [next(it) for _ in range(9)]
    wh, wc, xs, low, ff, ft, posv, pos, pos_sem = [next(it) for _ in range(9)]
    in_s, in_r, out_s, out_r, h_s, h_r = [next(it) for _ in range(6)]

    s = lax.axis_index("space")
    k = lax.axis_index("terms")
    i = term_of(k)

    barrier = pltpu.get_barrier_semaphore()

    def greet(p, _):
        pl.semaphore_signal(
            barrier, inc=1, device_id={"terms": term_of((i + p) % GROUPS)}, device_id_type=MESH
        )
        return 0

    lax.fori_loop(1, GROUPS, greet, 0)

    def inside(dx, dz):
        return (s + dx >= 0) & (s + dx < ns) & (i + dz >= 0) & (i + dz < GROUPS)

    for dx, dz in DIRS:
        if dx == 0:
            continue

        @pl.when(inside(dx, dz))
        def _():
            pl.semaphore_signal(
                barrier, inc=1,
                device_id={"space": s + dx, "terms": term_of(i + dz)},
                device_id_type=MESH,
            )

    def pack(c):
        j0, n = CHUNKS[c]

        def one(m, _):
            j, x = j0 + m // 2, m % 2
            rows = [
                fin[pl.ds(pl.multiple_of((j * 6 + a * 2 + x) * 32, 32), 32), :] for a in range(3)
            ]
            turned = jnp.transpose(jnp.concatenate(rows + [jnp.zeros((32, 128), jnp.float32)], axis=0))
            sb[c][:, m] = turned.reshape(GROUPS, 8, 128)
            return 0

        lax.fori_loop(0, 2 * n, one, 0)

    def wait_barrier():
        sides = jnp.where((s > 0) & (s < ns - 1), 2, 1) if ns > 1 else 0
        rows_of = jnp.where((i > 0) & (i < GROUPS - 1), 3, 2)
        pl.semaphore_wait(barrier, GROUPS - 1 + sides * rows_of)

    def leaving(c, p, src, dst, s_sem, r_sem, inward, tiles):
        i2 = (i + p) % GROUPS
        k2 = term_of(i2)
        return pltpu.make_async_remote_copy(
            src_ref=src.at[i2 if inward else k2, tiles],
            dst_ref=dst.at[k if inward else i, tiles],
            send_sem=s_sem.at[c, p],
            recv_sem=r_sem.at[c, p],
            device_id={"terms": k2},
            device_id_type=MESH,
        )

    def arriving(c, p, src, dst, s_sem, r_sem, inward, tiles):
        i2 = (i - p + GROUPS) % GROUPS
        k2 = term_of(i2)
        return pltpu.make_async_remote_copy(
            src_ref=src.at[0, tiles],
            dst_ref=dst.at[k2 if inward else i2, tiles],
            send_sem=s_sem.at[c, p],
            recv_sem=r_sem.at[c, p],
            device_id={"terms": k2},
            device_id_type=MESH,
        )

    def over_peers(fn):
        def one(p, _):
            fn(p)
            return 0

        lax.fori_loop(1, GROUPS, one, 0)

    def piece_in(n):
        c, lo, hi = PIECES[n]
        return (sb[c], rb[c], in_s, in_r, True, slice(lo, hi))

    def send_in(n):
        c, lo, hi = PIECES[n]
        over_peers(lambda p: leaving(n, p, *piece_in(n)).start())
        rb[c][k, lo:hi] = sb[c][i, lo:hi]

    def wait_in(c):
        for n, piece in enumerate(PIECES):
            if piece[0] == c:
                over_peers(lambda p: arriving(n, p, *piece_in(n)).wait_recv())

    def whole_out(c):
        return (ob[c], qb[c], out_s, out_r, False, slice(0, ob[c].shape[1]))

    def send_out(c):
        over_peers(lambda p: leaving(c, p, *whole_out(c)).start())
        qb[c][i] = ob[c][k]

    def wait_out(c):
        over_peers(lambda p: arriving(c, p, *whole_out(c)).wait_recv())

    fetch[0].wait()
    pack(0)
    wait_barrier()
    send_in(0)
    pack(1)
    send_in(1)

    for copy in fetch[1:]:
        copy.wait()
    lane8 = lax.broadcasted_iota(jnp.int32, (8, 128), 1)

    def locate(g, acc):
        for j in range(SLOT_DEV):
            acc = jnp.where(lane8 == slots[g * SLOT_DEV + j], g * 16 + j, acc)
        return acc

    posv[...] = lax.fori_loop(0, GROUPS, locate, jnp.zeros((8, 128), jnp.int32))
    to_smem = pltpu.make_async_copy(posv, pos, pos_sem)
    to_smem.start()

    for which in range(2):
        wh[which, 9 * 128 :, 0:128] = jnp.zeros((384, 128), jnp.bfloat16)
        wh[which, 0 : 3 * 128, 128:256] = jnp.zeros((384, 128), jnp.bfloat16)
    lane1 = lax.broadcasted_iota(jnp.int32, (1, 128), 1)
    group = lane1 // 32

    def by_group(v0, v1, v2):
        return jnp.where(
            group == 0, v0, jnp.where(group == 1, v1, jnp.where(group == 2, v2, 0.0))
        ).astype(jnp.float32)

    def splat(v):
        return jnp.full((1, 128), v, jnp.float32)

    inv = [1.0 / splat(sten[a, a, 13]) for a in range(3)]
    inv_lane = by_group(*inv)
    apart = lax.broadcasted_iota(jnp.int32, (32, 128), 0) - lax.broadcasted_iota(
        jnp.int32, (32, 128), 1
    ) % 32

    def table(m, _):
        dx, dz = m // 3, m % 3
        for b in range(4):
            block = [jnp.zeros((32, 128), jnp.float32)] * 2
            if b < 3:
                for dy in range(3):
                    o = dx * 9 + dy * 3 + dz
                    plain = by_group(*[splat(sten[a, b, o]) for a in range(3)])
                    smooth = -(plain * inv_lane) * inv[b]
                    if dy == 1:
                        centre = (group == b) & ((dx == 1) & (dz == 1))
                        smooth = jnp.where(centre, inv_lane, smooth)
                    for which, line in enumerate((smooth, plain)):
                        block[which] = jnp.where(apart == dy - 1, line, block[which])
            for which in range(2):
                hi = block[which].astype(jnp.bfloat16)
                lo = (block[which] - hi.astype(jnp.float32)).astype(jnp.bfloat16)
                row = pl.multiple_of((dx * 3 + dz) * 128 + b * 32, 32)
                wc[which, pl.ds(row, 32), 0:128] = hi
                wc[which, pl.ds(row, 32), 128:256] = lo
                for px in range(2):
                    row = pl.multiple_of(((dx + px) * 3 + dz) * 128 + b * 32, 32)
                    wh[which, pl.ds(row, 32), px * 128 : px * 128 + 128] = hi
        return 0

    lax.fori_loop(0, 9, table, 0)

    def field(m, _):
        rows = fl[m // 2, m % 2]
        ft[...] = jnp.transpose(jnp.concatenate([rows] * 4, axis=0))
        ff[m] = ft[pl.ds(pl.multiple_of(8 * i, 8), 8), :]
        return 0

    lax.fori_loop(0, 2 * DIMS, field, 0)

    def zero_outside(buf, rim, count, wide):
        def layer(x):
            def one(t, _):
                buf[x, t] = jnp.zeros((24, 128), jnp.float32)
                return 0

            lax.fori_loop(0, count, one, 0)
            for side in range(2):
                if wide:
                    for row in range(3):
                        rim[side, row, x] = jnp.zeros(rim.shape[3:], jnp.float32)
                else:
                    rim[side, x] = jnp.zeros(rim.shape[2:], jnp.float32)

        def edge(side):
            if wide:
                for row in (side, side + 1):
                    rim[side, row] = jnp.zeros(rim.shape[2:], jnp.float32)
            else:
                rim[side] = jnp.zeros(rim.shape[1:], jnp.float32)

        for x in (0, 1) if wide else (0,):
            pl.when(s == 0)(lambda x=x: layer(x))
        for x in (4, 5) if wide else (3,):
            pl.when(s == ns - 1)(lambda x=x: layer(x))
        pl.when(i == 0)(lambda: edge(0))
        pl.when(i == GROUPS - 1)(lambda: edge(1))

    for lv in range(5):
        zero_outside(load_buf[lv], rims[2 * lv], COUNT[lv], WIDE[lv])
        if lv < 4 and not WIDE[lv]:
            zero_outside(sett_buf[lv], rims[2 * lv + 1], COUNT[lv], False)

    pack(2)
    pack(3)
    to_smem.wait()

    def halo_copy(q, n, e, buf, part):
        t0, count, n8 = part
        dx, dz = DIRS[n]
        sx, tx = {1: (2, 0), -1: (1, 3), 0: (0, 0)}[dx]
        if buf.shape[0] == 6:
            tx = {1: 0, -1: 4, 0: 2}[dx]
            if dz == 0:
                src = buf.at[2:4, t0 : t0 + count, 8:16, :]
                dst = buf.at[tx : tx + 2, t0 : t0 + count, 8:16, :]
            else:
                side = 1 if dz > 0 else 0
                src = faces[e].at[side]
                dst = rims[e].at[1 - side, 1 - side : 3 - side, tx : tx + 2]
        elif dz == 0:
            src = buf.at[sx, t0 : t0 + count, 8:16, :]
            dst = buf.at[tx, t0 : t0 + count, 8:16, :]
        else:
            side = 1 if dz > 0 else 0
            if dx == 0:
                src = faces[e].at[side, :, t0 : t0 + n8]
                dst = rims[e].at[1 - side, 1:3, t0 : t0 + n8]
            else:
                src = faces[e].at[side, sx - 1, t0 : t0 + n8]
                dst = rims[e].at[1 - side, tx, t0 : t0 + n8]
        return pltpu.make_async_remote_copy(
            src_ref=src,
            dst_ref=dst,
            send_sem=h_s.at[q, n],
            recv_sem=h_r.at[q, n],
            device_id={"space": s + dx, "terms": term_of(i + dz)},
            device_id_type=MESH,
        )

    def by_five(part, fn):
        t0, count, _ = part
        w = next(w for w in (5, 4, 1) if count % w == 0) if count != 19 and count != 38 else 19

        def some(u, _):
            for v in range(w):
                fn(t0 + u * w + v)
            return 0

        lax.fori_loop(0, count // w, some, 0)

    exchanges = []

    def start_exchange(e, buf, part):
        args = (len(exchanges), e, buf, part)
        exchanges.append(args)
        for n, (dx, dz) in enumerate(DIRS):
            pl.when(inside(dx, dz))(lambda n=n: halo_copy(args[0], n, *args[1:]).start())
        return args

    def end_exchange(q, e, buf, part):
        for n, (dx, dz) in enumerate(DIRS):
            pl.when(inside(-dx, -dz))(lambda n=n: halo_copy(q, n, e, buf, part).wait_recv())
        spread_rim(e, buf, part)

    def spread_rim(e, buf, part):
        def spread(t):
            for x in range(4):
                buf[x, t, 7:8, :] = rims[e][0, x, pl.ds(t, 1), :]
                buf[x, t, 16:17, :] = rims[e][1, x, pl.ds(t, 1), :]

        def spread_wide(t):
            for x in range(6):
                buf[x, t, 7:8, :] = rims[e][0, 1, x, pl.ds(t, 1), :]
                buf[x, t, 16:17, :] = rims[e][1, 1, x, pl.ds(t, 1), :]
                rims[e][0, 2, x, pl.ds(t, 1), :] = buf[x, t, 8:9, :]
                rims[e][1, 0, x, pl.ds(t, 1), :] = buf[x, t, 15:16, :]

        by_five(part, spread_wide if buf.shape[0] == 6 else spread)

    def halves(v):
        hi = v.astype(jnp.bfloat16)
        return hi, (v - hi.astype(jnp.float32)).astype(jnp.bfloat16)

    def product(rows, which):
        rest = dot(xs[rows : 2 * rows, :], wh[which])
        return [main(0, rows, px, which) + rest[:, 128 * px : 128 * px + 128] for px in range(2)]

    def main(at, rows, px, which):
        both = dot(xs[at : at + rows, 384 * px : 384 * px + 1152], wc[which])
        return both[:, 0:128] + both[:, 128:256]

    def settle_wide(lv):
        src, rim, step, t8 = load_buf[lv], rims[2 * lv], STEP[lv], T8[lv]
        base = 16 * step
        rows = base + 4 * t8

        def put(row, col, v):
            hi, lo = halves(v)
            xs[pl.ds(pl.multiple_of(row, 16), v.shape[0]), col : col + 128] = hi
            xs[pl.ds(pl.multiple_of(rows + row, 16), v.shape[0]), col : col + 128] = lo

        def pair(u, _):
            for dz in range(3):
                for w in range(4):
                    for b in range(2):
                        v = [src[2 * b + w, 2 * u + h, 7 + dz : 15 + dz, :] for h in range(2)]
                        put(b * 8 * step + u * 16, (w * 3 + dz) * 128, jnp.concatenate(v, axis=0))
            return 0

        lax.fori_loop(0, step // 2, pair, 0)
        for side in range(2):
            for dz in range(3):
                for w in range(4):
                    v = [rim[side, dz, 2 * b + w] for b in range(2)]
                    put(base + side * 2 * t8, (w * 3 + dz) * 128, jnp.concatenate(v, axis=0))
        res = product(rows, 0)
        one, zero = jnp.float32(1.0), jnp.float32(0.0)
        in_x = [jnp.where(s > 0, one, zero), one, one, jnp.where(s < ns - 1, one, zero)]
        in_z = [jnp.where(i > 0, one, zero), jnp.where(i < GROUPS - 1, one, zero)]
        for x in range(4):
            b, mine = x // 2, res[x % 2]
            v = mine[b * 8 * step : (b + 1) * 8 * step].reshape(step, 8, 128)
            if x in (1, 2):
                own_buf[lv][x - 1, 0:step] = v
            else:
                v = v * in_x[x]
            sett_buf[lv][x, 0:step, 8:16, :] = v
            for side in range(2):
                row = base + side * 2 * t8 + b * t8
                rims[2 * lv + 1][side, x] = mine[row : row + t8] * (in_x[x] * in_z[side])

    def stage_rows(src, part, lo_at, at=0):
        t0, count, _ = part

        def pair(u, _):
            t = t0 + 2 * u
            for dz in range(3):
                for x in range(4):
                    v = jnp.concatenate(
                        [src[x, t, 7 + dz : 15 + dz, :], src[x, t + 1, 7 + dz : 15 + dz, :]], axis=0
                    )
                    hi, lo = halves(v)
                    col = (x * 3 + dz) * 128
                    xs[pl.ds(pl.multiple_of(at + u * 16, 16), 16), col : col + 128] = hi
                    xs[pl.ds(pl.multiple_of(lo_at + u * 16, 16), 16), col : col + 128] = lo
            return 0

        lax.fori_loop(0, (count + 1) // 2, pair, 0)

    def apply(src, part, which, store):
        step = (part[1] + 1) // 2 * 2
        stage_rows(src, part, 8 * step)
        res = product(8 * step, which)
        for px in range(2):
            store(px, part[0], res[px].reshape(step, 8, 128))

    pending = []
    for lv in range(5):
        c, j0 = CHUNK_OF[lv]
        if lv == 0 or c != CHUNK_OF[lv - 1][0]:
            wait_in(c)

        def load_of(t):
            q = pos[0, START[lv] + t]
            g = q // 16
            j = j0 + jnp.clip(q % 16 - BASE[lv], 0, CAP[lv] - 1)
            parts = [rb[c][g, 2 * j + x] for x in range(2)]
            if lv > 0:
                for d in range(DIMS):
                    par = ptab[(START[lv] + t) * DIMS + d]
                    weight = jnp.where(par >= 0, cp[d, START[lv] + t], 0.0)
                    at = jnp.maximum(par, 0)
                    for x in range(2):
                        parts[x] = parts[x] - (weight * ff[2 * d + x]) * img_buf[lv - 1][x, at]
            for x in range(2):
                load_buf[lv][(2 if WIDE[lv] else 1) + x, t, 8:16, :] = parts[x]
                if WIDE[lv]:
                    for row in range(2):
                        faces[2 * lv][0, row, x, pl.ds(t, 1), :] = parts[x][row : row + 1]
                        faces[2 * lv][1, row, x, pl.ds(t, 1), :] = parts[x][6 + row : 7 + row]
                else:
                    faces[2 * lv][0, x, pl.ds(t, 1), :] = parts[x][0:1]
                    faces[2 * lv][1, x, pl.ds(t, 1), :] = parts[x][7:8]

        started = []
        for part in PARTS[lv]:
            by_five(part, load_of)
            started.append(start_exchange(2 * lv, load_buf[lv], part))
        ready = pending.pop()() if pending else None

        def deliver_to(o, j0, layers, lv=lv):
            def deliver(g, _):
                for j in range(CAP[lv]):
                    q = slots[g * SLOT_DEV + BASE[lv] + j]
                    t = jnp.clip(q - START[lv], 0, COUNT[lv] - 1)
                    for n, x in enumerate(layers):
                        v = own_buf[lv][x, t]
                        ob[o][g, len(layers) * (j0 + j) + n] = jnp.where(q >= 0, v, 0.0)
                return 0

            lax.fori_loop(0, GROUPS, deliver, 0)

        def deliver_packed(o, x, lv=lv):
            def deliver(g, _):
                v = []
                for j in range(CAP[lv]):
                    q = slots[g * SLOT_DEV + BASE[lv] + j]
                    t = jnp.clip(q - START[lv], 0, COUNT[lv] - 1)
                    v.append(jnp.where(q >= 0, own_buf[lv][x, t], 0.0))
                r1, r2, r3 = [pltpu.roll(v[1 + n], 96 - 32 * n, 1) for n in range(3)]
                ob[o][g, 0] = jnp.where(lane8 < 96, v[0], r1)
                ob[o][g, 1] = jnp.where(lane8 < 64, r1, r2)
                ob[o][g, 2] = jnp.where(lane8 < 32, r2, r3)
                ob[o][g, 3] = v[4]
                return 0

            lax.fori_loop(0, GROUPS, deliver, 0)

        def face(t):
            for x in range(2):
                faces[2 * lv + 1][0, x, pl.ds(t, 1), :] = sett_buf[lv][1 + x, t, 8:9, :]
                faces[2 * lv + 1][1, x, pl.ds(t, 1), :] = sett_buf[lv][1 + x, t, 15:16, :]

        def settle(px, t0, v):
            own_buf[lv][px, t0 : t0 + v.shape[0]] = v
            sett_buf[lv][1 + px, t0 : t0 + v.shape[0], 8:16, :] = v

        def image(px, t0, v):
            img_buf[lv][px, t0 : t0 + v.shape[0]] = v

        if WIDE[lv]:
            end_exchange(*started[0])
            send_in(2 + lv)
            if ready is not None:
                send_out(ready)
            settle_wide(lv)
            spread_rim(2 * lv + 1, sett_buf[lv], PARTS[lv][0])
            apply(sett_buf[lv], PARTS[lv][0], 1, image)

            def finish(lv=lv, c=c, j0=j0, deliver_to=deliver_to):
                deliver_to(c, j0, (0, 1))
                return c if CHUNK_OF[lv + 1][0] != c else None

            pending.append(finish)
        elif lv < 4:
            rimmed = []
            for part, args in zip(PARTS[lv], started):
                end_exchange(*args)
                if part is PARTS[lv][-1]:
                    send_in(5)
                    send_out(ready)
                apply(load_buf[lv], part, 0, settle)
                by_five(part, face)
                rimmed.append(start_exchange(2 * lv + 1, sett_buf[lv], part))
            deliver_to(c, j0, (0, 1))
            for part, args in zip(PARTS[lv], rimmed):
                end_exchange(*args)
                if part is PARTS[lv][-1]:
                    send_out(c)
                apply(sett_buf[lv], part, 1, image)
        else:
            lo_at = 8 * COUNT[lv]
            for px in range(2):
                for part, args in zip(PARTS[lv], started):
                    at, n = 8 * part[0], 8 * part[1]
                    if px == 0:
                        end_exchange(*args)
                        stage_rows(load_buf[lv], part, lo_at + at, at)
                        low[at : at + n, :] = dot(xs[lo_at + at : lo_at + at + n, :], wh[0])
                    res = main(at, n, px, 0) + low[at : at + n, 128 * px : 128 * px + 128]
                    own_buf[lv][px, part[0] : part[0] + part[1]] = res.reshape(part[1], 8, 128)
                deliver_packed(3 + px, px)
                send_out(3 + px)

    for c, (j0, n, layers) in enumerate(OUTS):
        wait_out(c)
        if len(layers) == 1:
            for m in range(4):
                turned = jnp.transpose(qb[c][:, m].reshape(128, 128))
                for g in range(4 * m, min(4 * m + 4, 15)):
                    row = ((j0 + g // 3) * 6 + g % 3 * 2 + layers[0]) * 32
                    out[row : row + 32, :] = turned[32 * (g - 4 * m) : 32 * (g - 4 * m) + 32]
            continue

        def unpack(m, _, c=c, j0=j0, layers=layers):
            j, x = j0 + m // 2, m % 2
            turned = jnp.transpose(qb[c][:, m].reshape(128, 128))
            for a in range(3):
                row = pl.multiple_of((j * 6 + a * 2 + x) * 32, 32)
                out[pl.ds(row, 32), :] = turned[32 * a : 32 * a + 32]
            return 0

        lax.fori_loop(0, 2 * n, unpack, 0)

    for n in range(len(PIECES)):
        over_peers(lambda p: leaving(n, p, *piece_in(n)).wait_send())
    for c in range(len(OUTS)):
        over_peers(lambda p: leaving(c, p, *whole_out(c)).wait_send())
    for q, e, buf, part in exchanges:
        for n, (dx, dz) in enumerate(DIRS):
            pl.when(inside(dx, dz))(lambda n=n: halo_copy(q, n, e, buf, part).wait_send())


def on_device(ns, forcing, stencil, fields, coupling, slot_term):
    rows = forcing.shape[0] * 6 * 32
    vm = pl.BlockSpec(memory_space=pltpu.VMEM)
    hbm = pl.BlockSpec(memory_space=pltpu.HBM)
    f32, bf16 = jnp.float32, jnp.bfloat16
    dma = pltpu.SemaphoreType.DMA
    scratch = [
        pltpu.VMEM((rows, 128), f32),
        pltpu.VMEM(fields.shape, f32),
        pltpu.SMEM(coupling.shape[::-1], f32),
        pltpu.SMEM((TERMS * DIMS,), jnp.int32),
        pltpu.SMEM(slot_term.shape, jnp.int32),
        pltpu.SMEM((3, 3, 27), f32),
        dma((6,)),
    ]
    scratch += [pltpu.VMEM((GROUPS, 2 * n, 8, 128), f32) for _ in range(2) for _, n in CHUNKS]
    scratch += [
        pltpu.VMEM((GROUPS, 2 * n if len(x) == 2 else 4, 8, 128), f32) for _ in range(2) for _, n, x in OUTS
    ]
    scratch += [pltpu.VMEM((6 if WIDE[lv] else 4, T8[lv], 24, 128), f32) for lv in range(5)]
    scratch += [pltpu.VMEM((4, T8[lv], 24, 128), f32) for lv in range(4)]
    scratch += [pltpu.VMEM((2, T8[lv], 8, 128), f32) for lv in range(5)]
    scratch += [pltpu.VMEM((2, T8[lv], 8, 128), f32) for lv in range(4)]
    wide = [WIDE[e // 2] and e % 2 == 0 for e in range(9)]
    scratch += [pltpu.VMEM((2,) + (2,) * w + (2, T8[e // 2], 128), f32) for e, w in enumerate(wide)]
    scratch += [
        pltpu.VMEM((2, 3, 6, T8[e // 2], 128) if w else (2, 4, T8[e // 2], 128), f32)
        for e, w in enumerate(wide)
    ]
    scratch += [
        pltpu.VMEM((2, 12 * 128, 256), bf16),
        pltpu.VMEM((2, 9 * 128, 256), bf16),
        pltpu.VMEM((16 * COUNT[4], 12 * 128), bf16),
        pltpu.VMEM((8 * COUNT[4], 256), f32),
        pltpu.VMEM((2 * DIMS, 8, 128), f32),
        pltpu.VMEM((128, 128), f32),
        pltpu.VMEM((8, 128), jnp.int32),
        pltpu.SMEM((8, 128), jnp.int32),
        dma(()),
    ]
    scratch += [dma((len(PIECES), GROUPS)) for _ in range(2)]
    scratch += [dma((len(OUTS), GROUPS)) for _ in range(2)] + [dma((9, 8)) for _ in range(2)]
    out = pl.pallas_call(
        functools.partial(kernel, ns),
        out_shape=pltpu.VMEM((rows, 128), f32),
        in_specs=[hbm] * 6,
        out_specs=vm,
        scratch_shapes=scratch,
        compiler_params=pltpu.CompilerParams(
            collective_id=0, has_side_effects=True, vmem_limit_bytes=58 << 20
        ),
    )(forcing.reshape(rows, 128), fields, coupling.T, jnp.asarray(parent_table()), slot_term, stencil.transpose(1, 2, 0))
    return out.reshape(forcing.shape)


def solution(mesh):
    return jax.shard_map(
        functools.partial(on_device, mesh.shape["space"]),
        mesh=mesh,
        in_specs=(
            P("terms", None, "space", None, None),
            P(),
            P(None, "space", None, None),
            P(),
            P(),
        ),
        out_specs=P("terms", None, "space", None, None),
        check_vma=False,
    )
```

```python
import functools

import jax
import jax.numpy as jnp
import numpy as np
from jax import lax
from jax.experimental import pallas as pl
from jax.experimental.pallas import tpu as pltpu
from jax.sharding import PartitionSpec as P

DIMS = 5
TERMS = 126
GROUPS = 16
SLOT_DEV = 11
COUNT = (1, 5, 15, 35, 70)
START = (0, 1, 6, 21, 56)
CAP = (1, 1, 1, 3, 5)
BASE = (0, 1, 2, 3, 6)
T8 = (8, 8, 16, 40, 72)
PARTS = (((0, 1, 8),), ((0, 5, 8),), ((0, 15, 16),), ((0, 16, 16), (16, 19, 24)), ((0, 32, 32), (32, 38, 40)))
WIDE = (True, True, True, True, False)
CHUNKS = ((0, 1), (1, 2), (3, 3), (6, 5))
OUTS = ((0, 1, (0, 1)), (1, 2, (0, 1)), (3, 3, (0, 1)), (6, 5, (0,)), (6, 5, (1,)))
CHUNK_OF = ((0, 0), (1, 0), (1, 1), (2, 0), (3, 0))
DIRS = ((-1, -1), (-1, 1), (1, -1), (1, 1), (0, -1), (0, 1), (-1, 0), (1, 0))
PIECES = ((0, 0, 2), (1, 0, 4), (2, 0, 6), (3, 0, 4), (3, 4, 7), (3, 7, 10))
MESH = pl.DeviceIdType.MESH


def compositions(total, pieces_left):
    if pieces_left == 1:
        return [[total]]
    result = []
    for leading in range(total, -1, -1):
        for remainder in compositions(total - leading, pieces_left - 1):
            result.append([leading] + remainder)
    return result


def parent_table():
    table = np.full((TERMS, DIMS), -1, np.int32)
    for level in range(1, 5):
        below = {tuple(v): n for n, v in enumerate(compositions(level - 1, DIMS))}
        for n, v in enumerate(compositions(level, DIMS)):
            for d in range(DIMS):
                if v[d] > 0:
                    w = list(v)
                    w[d] -= 1
                    table[START[level] + n, d] = below[tuple(w)]
    return table.reshape(-1)


def dot(a, b):
    return jnp.dot(a, b, preferred_element_type=jnp.float32)


def term_of(i):
    q, r = i // 4, i % 4
    return q * 4 + r + (q % 2) * (3 - 2 * r)


def kernel(ns, *refs):
    given, out, it = refs[:6], refs[6], iter(refs[7:])
    fin, fl, cp, ptab, slots, sten, given_sem = [next(it) for _ in range(7)]
    fetch = [
        pltpu.make_async_copy(src, dst, given_sem.at[n])
        for n, (src, dst) in enumerate(zip(given, (fin, fl, cp, ptab, slots, sten)))
    ]
    for copy in fetch:
        copy.start()
    sb = [next(it) for _ in CHUNKS]
    rb = [next(it) for _ in CHUNKS]
    ob = [next(it) for _ in OUTS]
    qb = [next(it) for _ in OUTS]
    load_buf = [next(it) for _ in range(5)]
    sett_buf = [next(it) for _ in range(4)]
    own_buf = [next(it) for _ in range(5)]
    img_buf = [next(it) for _ in range(4)]
    faces = [next(it) for _ in range(9)]
    rims = [next(it) for _ in range(9)]
    wh, wc, xs, low, ff, ft, posv, pos, pos_sem = [next(it) for _ in range(9)]
    in_s, in_r, out_s, out_r, h_s, h_r = [next(it) for _ in range(6)]

    s = lax.axis_index("space")
    k = lax.axis_index("terms")
    i = term_of(k)

    barrier = pltpu.get_barrier_semaphore()

    def greet(p, _):
        pl.semaphore_signal(
            barrier, inc=1, device_id={"terms": term_of((i + p) % GROUPS)}, device_id_type=MESH
        )
        return 0

    lax.fori_loop(1, GROUPS, greet, 0)

    def inside(dx, dz):
        return (s + dx >= 0) & (s + dx < ns) & (i + dz >= 0) & (i + dz < GROUPS)

    for dx, dz in DIRS:
        if dx == 0:
            continue

        @pl.when(inside(dx, dz))
        def _():
            pl.semaphore_signal(
                barrier, inc=1,
                device_id={"space": s + dx, "terms": term_of(i + dz)},
                device_id_type=MESH,
            )

    def pack(c):
        j0, n = CHUNKS[c]

        def one(m, _):
            j, x = j0 + m // 2, m % 2
            rows = [
                fin[pl.ds(pl.multiple_of((j * 6 + a * 2 + x) * 32, 32), 32), :] for a in range(3)
            ]
            turned = jnp.transpose(jnp.concatenate(rows + [jnp.zeros((32, 128), jnp.float32)], axis=0))
            sb[c][:, m] = turned.reshape(GROUPS, 8, 128)
            return 0

        lax.fori_loop(0, 2 * n, one, 0)

    def wait_barrier():
        sides = jnp.where((s > 0) & (s < ns - 1), 2, 1) if ns > 1 else 0
        rows_of = jnp.where((i > 0) & (i < GROUPS - 1), 3, 2)
        pl.semaphore_wait(barrier, GROUPS - 1 + sides * rows_of)

    def leaving(c, p, src, dst, s_sem, r_sem, inward, tiles):
        i2 = (i + p) % GROUPS
        k2 = term_of(i2)
        return pltpu.make_async_remote_copy(
            src_ref=src.at[i2 if inward else k2, tiles],
            dst_ref=dst.at[k if inward else i, tiles],
            send_sem=s_sem.at[c, p],
            recv_sem=r_sem.at[c, p],
            device_id={"terms": k2},
            device_id_type=MESH,
        )

    def arriving(c, p, src, dst, s_sem, r_sem, inward, tiles):
        i2 = (i - p + GROUPS) % GROUPS
        k2 = term_of(i2)
        return pltpu.make_async_remote_copy(
            src_ref=src.at[0, tiles],
            dst_ref=dst.at[k2 if inward else i2, tiles],
            send_sem=s_sem.at[c, p],
            recv_sem=r_sem.at[c, p],
            device_id={"terms": k2},
            device_id_type=MESH,
        )

    def over_peers(fn):
        def one(p, _):
            fn(p)
            return 0

        lax.fori_loop(1, GROUPS, one, 0)

    def piece_in(n):
        c, lo, hi = PIECES[n]
        return (sb[c], rb[c], in_s, in_r, True, slice(lo, hi))

    def send_in(n):
        c, lo, hi = PIECES[n]
        over_peers(lambda p: leaving(n, p, *piece_in(n)).start())
        rb[c][k, lo:hi] = sb[c][i, lo:hi]

    def wait_in(c):
        for n, piece in enumerate(PIECES):
            if piece[0] == c:
                over_peers(lambda p: arriving(n, p, *piece_in(n)).wait_recv())

    def whole_out(c):
        return (ob[c], qb[c], out_s, out_r, False, slice(0, ob[c].shape[1]))

    def send_out(c):
        over_peers(lambda p: leaving(c, p, *whole_out(c)).start())
        qb[c][i] = ob[c][k]

    def wait_out(c):
        over_peers(lambda p: arriving(c, p, *whole_out(c)).wait_recv())

    fetch[0].wait()
    pack(0)
    wait_barrier()
    send_in(0)
    pack(1)
    send_in(1)

    for copy in fetch[1:]:
        copy.wait()
    lane8 = lax.broadcasted_iota(jnp.int32, (8, 128), 1)

    def locate(g, acc):
        for j in range(SLOT_DEV):
            acc = jnp.where(lane8 == slots[g * SLOT_DEV + j], g * 16 + j, acc)
        return acc

    posv[...] = lax.fori_loop(0, GROUPS, locate, jnp.zeros((8, 128), jnp.int32))
    to_smem = pltpu.make_async_copy(posv, pos, pos_sem)
    to_smem.start()

    for which in range(2):
        wh[which, 9 * 128 :, 0:128] = jnp.zeros((384, 128), jnp.bfloat16)
        wh[which, 0 : 3 * 128, 128:256] = jnp.zeros((384, 128), jnp.bfloat16)
    lane1 = lax.broadcasted_iota(jnp.int32, (1, 128), 1)
    group = lane1 // 32

    def by_group(v0, v1, v2):
        return jnp.where(
            group == 0, v0, jnp.where(group == 1, v1, jnp.where(group == 2, v2, 0.0))
        ).astype(jnp.float32)

    def splat(v):
        return jnp.full((1, 128), v, jnp.float32)

    inv = [1.0 / splat(sten[a, a, 13]) for a in range(3)]
    inv_lane = by_group(*inv)
    apart = lax.broadcasted_iota(jnp.int32, (32, 128), 0) - lax.broadcasted_iota(
        jnp.int32, (32, 128), 1
    ) % 32

    def table(m, _):
        dx, dz = m // 3, m % 3
        for b in range(4):
            block = [jnp.zeros((32, 128), jnp.float32)] * 2
            if b < 3:
                for dy in range(3):
                    o = dx * 9 + dy * 3 + dz
                    plain = by_group(*[splat(sten[a, b, o]) for a in range(3)])
                    smooth = -(plain * inv_lane) * inv[b]
                    if dy == 1:
                        centre = (group == b) & ((dx == 1) & (dz == 1))
                        smooth = jnp.where(centre, inv_lane, smooth)
                    for which, line in enumerate((smooth, plain)):
                        block[which] = jnp.where(apart == dy - 1, line, block[which])
            for which in range(2):
                hi = block[which].astype(jnp.bfloat16)
                lo = (block[which] - hi.astype(jnp.float32)).astype(jnp.bfloat16)
                row = pl.multiple_of((dx * 3 + dz) * 128 + b * 32, 32)
                wc[which, pl.ds(row, 32), 0:128] = hi
                wc[which, pl.ds(row, 32), 128:256] = lo
                for px in range(2):
                    row = pl.multiple_of(((dx + px) * 3 + dz) * 128 + b * 32, 32)
                    wh[which, pl.ds(row, 32), px * 128 : px * 128 + 128] = hi
        return 0

    lax.fori_loop(0, 9, table, 0)

    def field(m, _):
        rows = fl[m // 2, m % 2]
        ft[...] = jnp.transpose(jnp.concatenate([rows] * 4, axis=0))
        ff[m] = ft[pl.ds(pl.multiple_of(8 * i, 8), 8), :]
        return 0

    lax.fori_loop(0, 2 * DIMS, field, 0)

    def zero_outside(buf, rim, count, wide):
        def layer(x):
            def one(t, _):
                buf[x, t] = jnp.zeros((24, 128), jnp.float32)
                return 0

            lax.fori_loop(0, count, one, 0)
            for side in range(2):
                if wide:
                    for row in range(3):
                        rim[side, row, x] = jnp.zeros(rim.shape[3:], jnp.float32)
                else:
                    rim[side, x] = jnp.zeros(rim.shape[2:], jnp.float32)

        def edge(side):
            if wide:
                for row in (side, side + 1):
                    rim[side, row] = jnp.zeros(rim.shape[2:], jnp.float32)
            else:
                rim[side] = jnp.zeros(rim.shape[1:], jnp.float32)

        for x in (0, 1) if wide else (0,):
            pl.when(s == 0)(lambda x=x: layer(x))
        for x in (4, 5) if wide else (3,):
            pl.when(s == ns - 1)(lambda x=x: layer(x))
        pl.when(i == 0)(lambda: edge(0))
        pl.when(i == GROUPS - 1)(lambda: edge(1))

    for lv in range(5):
        zero_outside(load_buf[lv], rims[2 * lv], COUNT[lv], WIDE[lv])
        if lv < 4 and not WIDE[lv]:
            zero_outside(sett_buf[lv], rims[2 * lv + 1], COUNT[lv], False)

    pack(2)
    pack(3)
    to_smem.wait()

    def halo_copy(q, n, e, buf, part):
        t0, count, n8 = part
        dx, dz = DIRS[n]
        sx, tx = {1: (2, 0), -1: (1, 3), 0: (0, 0)}[dx]
        if buf.shape[0] == 6:
            tx = {1: 0, -1: 4, 0: 2}[dx]
            if dz == 0:
                src = buf.at[2:4, t0 : t0 + count, 8:16, :]
                dst = buf.at[tx : tx + 2, t0 : t0 + count, 8:16, :]
            else:
                side = 1 if dz > 0 else 0
                src = faces[e].at[side, :, :, t0 : t0 + n8]
                dst = rims[e].at[1 - side, 1 - side : 3 - side, tx : tx + 2, t0 : t0 + n8]
        elif dz == 0:
            src = buf.at[sx, t0 : t0 + count, 8:16, :]
            dst = buf.at[tx, t0 : t0 + count, 8:16, :]
        else:
            side = 1 if dz > 0 else 0
            if dx == 0:
                src = faces[e].at[side, :, t0 : t0 + n8]
                dst = rims[e].at[1 - side, 1:3, t0 : t0 + n8]
            else:
                src = faces[e].at[side, sx - 1, t0 : t0 + n8]
                dst = rims[e].at[1 - side, tx, t0 : t0 + n8]
        return pltpu.make_async_remote_copy(
            src_ref=src,
            dst_ref=dst,
            send_sem=h_s.at[q, n],
            recv_sem=h_r.at[q, n],
            device_id={"space": s + dx, "terms": term_of(i + dz)},
            device_id_type=MESH,
        )

    def by_five(part, fn):
        t0, count, _ = part
        w = next(w for w in (5, 4, 1) if count % w == 0) if count != 19 and count != 38 else 19

        def some(u, _):
            for v in range(w):
                fn(t0 + u * w + v)
            return 0

        lax.fori_loop(0, count // w, some, 0)

    exchanges = []

    def start_exchange(e, buf, part):
        args = (len(exchanges), e, buf, part)
        exchanges.append(args)
        for n, (dx, dz) in enumerate(DIRS):
            pl.when(inside(dx, dz))(lambda n=n: halo_copy(args[0], n, *args[1:]).start())
        return args

    def end_exchange(q, e, buf, part):
        for n, (dx, dz) in enumerate(DIRS):
            pl.when(inside(-dx, -dz))(lambda n=n: halo_copy(q, n, e, buf, part).wait_recv())
        spread_rim(e, buf, part)

    def spread_rim(e, buf, part):
        def spread(t):
            for x in range(4):
                buf[x, t, 7:8, :] = rims[e][0, x, pl.ds(t, 1), :]
                buf[x, t, 16:17, :] = rims[e][1, x, pl.ds(t, 1), :]

        def spread_wide(t):
            for x in range(6):
                buf[x, t, 7:8, :] = rims[e][0, 1, x, pl.ds(t, 1), :]
                buf[x, t, 16:17, :] = rims[e][1, 1, x, pl.ds(t, 1), :]
                rims[e][0, 2, x, pl.ds(t, 1), :] = buf[x, t, 8:9, :]
                rims[e][1, 0, x, pl.ds(t, 1), :] = buf[x, t, 15:16, :]

        by_five(part, spread_wide if buf.shape[0] == 6 else spread)

    def halves(v):
        hi = v.astype(jnp.bfloat16)
        return hi, (v - hi.astype(jnp.float32)).astype(jnp.bfloat16)

    def product(rows, which):
        rest = dot(xs[rows : 2 * rows, :], wh[which])
        return [main(0, rows, px, which) + rest[:, 128 * px : 128 * px + 128] for px in range(2)]

    def main(at, rows, px, which):
        both = dot(xs[at : at + rows, 384 * px : 384 * px + 1152], wc[which])
        return both[:, 0:128] + both[:, 128:256]

    def settle_wide(lv, part):
        t0, count, t8 = part
        src, rim, step = load_buf[lv], rims[2 * lv], (count + 1) // 2 * 2
        base = 16 * step
        rows = base + 4 * t8

        def put(row, col, v):
            hi, lo = halves(v)
            xs[pl.ds(pl.multiple_of(row, 16), v.shape[0]), col : col + 128] = hi
            xs[pl.ds(pl.multiple_of(rows + row, 16), v.shape[0]), col : col + 128] = lo

        def pair(u, _):
            for dz in range(3):
                for w in range(4):
                    for b in range(2):
                        v = [src[2 * b + w, t0 + 2 * u + h, 7 + dz : 15 + dz, :] for h in range(2)]
                        put(b * 8 * step + u * 16, (w * 3 + dz) * 128, jnp.concatenate(v, axis=0))
            return 0

        lax.fori_loop(0, step // 2, pair, 0)
        for side in range(2):
            for dz in range(3):
                for w in range(4):
                    v = [rim[side, dz, 2 * b + w, t0 : t0 + t8] for b in range(2)]
                    put(base + side * 2 * t8, (w * 3 + dz) * 128, jnp.concatenate(v, axis=0))
        res = product(rows, 0)
        one, zero = jnp.float32(1.0), jnp.float32(0.0)
        in_x = [jnp.where(s > 0, one, zero), one, one, jnp.where(s < ns - 1, one, zero)]
        in_z = [jnp.where(i > 0, one, zero), jnp.where(i < GROUPS - 1, one, zero)]
        for x in range(4):
            b, mine = x // 2, res[x % 2]
            v = mine[b * 8 * step : (b + 1) * 8 * step].reshape(step, 8, 128)
            if x in (1, 2):
                own_buf[lv][x - 1, t0 : t0 + step] = v
            else:
                v = v * in_x[x]
            sett_buf[lv][x, t0 : t0 + step, 8:16, :] = v
            for side in range(2):
                row = base + side * 2 * t8 + b * t8
                rims[2 * lv + 1][side, x, t0 : t0 + t8] = mine[row : row + t8] * (in_x[x] * in_z[side])

    def stage_rows(src, part, lo_at, at=0):
        t0, count, _ = part

        def pair(u, _):
            t = t0 + 2 * u
            for dz in range(3):
                for x in range(4):
                    v = jnp.concatenate(
                        [src[x, t, 7 + dz : 15 + dz, :], src[x, t + 1, 7 + dz : 15 + dz, :]], axis=0
                    )
                    hi, lo = halves(v)
                    col = (x * 3 + dz) * 128
                    xs[pl.ds(pl.multiple_of(at + u * 16, 16), 16), col : col + 128] = hi
                    xs[pl.ds(pl.multiple_of(lo_at + u * 16, 16), 16), col : col + 128] = lo
            return 0

        lax.fori_loop(0, (count + 1) // 2, pair, 0)

    def apply(src, part, which, store):
        step = (part[1] + 1) // 2 * 2
        stage_rows(src, part, 8 * step)
        res = product(8 * step, which)
        for px in range(2):
            store(px, part[0], res[px].reshape(step, 8, 128))

    pending = []
    for lv in range(5):
        c, j0 = CHUNK_OF[lv]
        if lv == 0 or c != CHUNK_OF[lv - 1][0]:
            wait_in(c)

        def load_of(t):
            q = pos[0, START[lv] + t]
            g = q // 16
            j = j0 + jnp.clip(q % 16 - BASE[lv], 0, CAP[lv] - 1)
            parts = [rb[c][g, 2 * j + x] for x in range(2)]
            if lv > 0:
                for d in range(DIMS):
                    par = ptab[(START[lv] + t) * DIMS + d]
                    weight = jnp.where(par >= 0, cp[d, START[lv] + t], 0.0)
                    at = jnp.maximum(par, 0)
                    for x in range(2):
                        parts[x] = parts[x] - (weight * ff[2 * d + x]) * img_buf[lv - 1][x, at]
            for x in range(2):
                load_buf[lv][(2 if WIDE[lv] else 1) + x, t, 8:16, :] = parts[x]
                if WIDE[lv]:
                    for row in range(2):
                        faces[2 * lv][0, row, x, pl.ds(t, 1), :] = parts[x][row : row + 1]
                        faces[2 * lv][1, row, x, pl.ds(t, 1), :] = parts[x][6 + row : 7 + row]
                else:
                    faces[2 * lv][0, x, pl.ds(t, 1), :] = parts[x][0:1]
                    faces[2 * lv][1, x, pl.ds(t, 1), :] = parts[x][7:8]

        started = []
        for part in PARTS[lv]:
            by_five(part, load_of)
            started.append(start_exchange(2 * lv, load_buf[lv], part))
        ready = pending.pop()() if pending else None

        def deliver_to(o, j0, layers, lv=lv):
            def deliver(g, _):
                for j in range(CAP[lv]):
                    q = slots[g * SLOT_DEV + BASE[lv] + j]
                    t = jnp.clip(q - START[lv], 0, COUNT[lv] - 1)
                    for n, x in enumerate(layers):
                        v = own_buf[lv][x, t]
                        ob[o][g, len(layers) * (j0 + j) + n] = jnp.where(q >= 0, v, 0.0)
                return 0

            lax.fori_loop(0, GROUPS, deliver, 0)

        def deliver_packed(o, x, lv=lv):
            def deliver(g, _):
                v = []
                for j in range(CAP[lv]):
                    q = slots[g * SLOT_DEV + BASE[lv] + j]
                    t = jnp.clip(q - START[lv], 0, COUNT[lv] - 1)
                    v.append(jnp.where(q >= 0, own_buf[lv][x, t], 0.0))
                r1, r2, r3 = [pltpu.roll(v[1 + n], 96 - 32 * n, 1) for n in range(3)]
                ob[o][g, 0] = jnp.where(lane8 < 96, v[0], r1)
                ob[o][g, 1] = jnp.where(lane8 < 64, r1, r2)
                ob[o][g, 2] = jnp.where(lane8 < 32, r2, r3)
                ob[o][g, 3] = v[4]
                return 0

            lax.fori_loop(0, GROUPS, deliver, 0)

        def image(px, t0, v):
            img_buf[lv][px, t0 : t0 + v.shape[0]] = v

        if WIDE[lv]:
            for part, args in zip(PARTS[lv], started):
                end_exchange(*args)
                if part is PARTS[lv][-1]:
                    send_in(2 + lv)
                    if ready is not None:
                        send_out(ready)
                settle_wide(lv, part)
                spread_rim(2 * lv + 1, sett_buf[lv], part)
                apply(sett_buf[lv], part, 1, image)

            def finish(lv=lv, c=c, j0=j0, deliver_to=deliver_to):
                deliver_to(c, j0, (0, 1))
                return c if CHUNK_OF[lv + 1][0] != c else None

            pending.append(finish)
        else:
            send_out(ready)
            lo_at = 8 * COUNT[lv]
            for px in range(2):
                for part, args in zip(PARTS[lv], started):
                    at, n = 8 * part[0], 8 * part[1]
                    if px == 0:
                        end_exchange(*args)
                        stage_rows(load_buf[lv], part, lo_at + at, at)
                        low[at : at + n, :] = dot(xs[lo_at + at : lo_at + at + n, :], wh[0])
                    res = main(at, n, px, 0) + low[at : at + n, 128 * px : 128 * px + 128]
                    own_buf[lv][px, part[0] : part[0] + part[1]] = res.reshape(part[1], 8, 128)
                deliver_packed(3 + px, px)
                send_out(3 + px)

    for c, (j0, n, layers) in enumerate(OUTS):
        wait_out(c)
        if len(layers) == 1:
            for m in range(4):
                turned = jnp.transpose(qb[c][:, m].reshape(128, 128))
                for g in range(4 * m, min(4 * m + 4, 15)):
                    row = ((j0 + g // 3) * 6 + g % 3 * 2 + layers[0]) * 32
                    out[row : row + 32, :] = turned[32 * (g - 4 * m) : 32 * (g - 4 * m) + 32]
            continue

        def unpack(m, _, c=c, j0=j0, layers=layers):
            j, x = j0 + m // 2, m % 2
            turned = jnp.transpose(qb[c][:, m].reshape(128, 128))
            for a in range(3):
                row = pl.multiple_of((j * 6 + a * 2 + x) * 32, 32)
                out[pl.ds(row, 32), :] = turned[32 * a : 32 * a + 32]
            return 0

        lax.fori_loop(0, 2 * n, unpack, 0)

    for n in range(len(PIECES)):
        over_peers(lambda p: leaving(n, p, *piece_in(n)).wait_send())
    for c in range(len(OUTS)):
        over_peers(lambda p: leaving(c, p, *whole_out(c)).wait_send())
    for q, e, buf, part in exchanges:
        for n, (dx, dz) in enumerate(DIRS):
            pl.when(inside(dx, dz))(lambda n=n: halo_copy(q, n, e, buf, part).wait_send())


def on_device(ns, forcing, stencil, fields, coupling, slot_term):
    rows = forcing.shape[0] * 6 * 32
    vm = pl.BlockSpec(memory_space=pltpu.VMEM)
    hbm = pl.BlockSpec(memory_space=pltpu.HBM)
    f32, bf16 = jnp.float32, jnp.bfloat16
    dma = pltpu.SemaphoreType.DMA
    scratch = [
        pltpu.VMEM((rows, 128), f32),
        pltpu.VMEM(fields.shape, f32),
        pltpu.SMEM(coupling.shape[::-1], f32),
        pltpu.SMEM((TERMS * DIMS,), jnp.int32),
        pltpu.SMEM(slot_term.shape, jnp.int32),
        pltpu.SMEM((3, 3, 27), f32),
        dma((6,)),
    ]
    scratch += [pltpu.VMEM((GROUPS, 2 * n, 8, 128), f32) for _ in range(2) for _, n in CHUNKS]
    scratch += [
        pltpu.VMEM((GROUPS, 2 * n if len(x) == 2 else 4, 8, 128), f32) for _ in range(2) for _, n, x in OUTS
    ]
    scratch += [pltpu.VMEM((6 if WIDE[lv] else 4, T8[lv], 24, 128), f32) for lv in range(5)]
    scratch += [pltpu.VMEM((4, T8[lv], 24, 128), f32) for lv in range(4)]
    scratch += [pltpu.VMEM((2, T8[lv], 8, 128), f32) for lv in range(5)]
    scratch += [pltpu.VMEM((2, T8[lv], 8, 128), f32) for lv in range(4)]
    wide = [WIDE[e // 2] and e % 2 == 0 for e in range(9)]
    scratch += [pltpu.VMEM((2,) + (2,) * w + (2, T8[e // 2], 128), f32) for e, w in enumerate(wide)]
    scratch += [
        pltpu.VMEM((2, 3, 6, T8[e // 2], 128) if w else (2, 4, T8[e // 2], 128), f32)
        for e, w in enumerate(wide)
    ]
    scratch += [
        pltpu.VMEM((2, 12 * 128, 256), bf16),
        pltpu.VMEM((2, 9 * 128, 256), bf16),
        pltpu.VMEM((16 * COUNT[4], 12 * 128), bf16),
        pltpu.VMEM((8 * COUNT[4], 256), f32),
        pltpu.VMEM((2 * DIMS, 8, 128), f32),
        pltpu.VMEM((128, 128), f32),
        pltpu.VMEM((8, 128), jnp.int32),
        pltpu.SMEM((8, 128), jnp.int32),
        dma(()),
    ]
    scratch += [dma((len(PIECES), GROUPS)) for _ in range(2)]
    scratch += [dma((len(OUTS), GROUPS)) for _ in range(2)] + [dma((sum(map(len, PARTS)), 8)) for _ in range(2)]
    out = pl.pallas_call(
        functools.partial(kernel, ns),
        out_shape=pltpu.VMEM((rows, 128), f32),
        in_specs=[hbm] * 6,
        out_specs=vm,
        scratch_shapes=scratch,
        compiler_params=pltpu.CompilerParams(
            collective_id=0, has_side_effects=True, vmem_limit_bytes=58 << 20
        ),
    )(forcing.reshape(rows, 128), fields, coupling.T, jnp.asarray(parent_table()), slot_term, stencil.transpose(1, 2, 0))
    return out.reshape(forcing.shape)


def solution(mesh):
    return jax.shard_map(
        functools.partial(on_device, mesh.shape["space"]),
        mesh=mesh,
        in_specs=(
            P("terms", None, "space", None, None),
            P(),
            P(None, "space", None, None),
            P(),
            P(),
        ),
        out_specs=P("terms", None, "space", None, None),
        check_vma=False,
    )
```

```python
import functools

import jax
import jax.numpy as jnp
import numpy as np
from jax import lax
from jax.experimental import pallas as pl
from jax.experimental.pallas import tpu as pltpu
from jax.sharding import PartitionSpec as P

DIMS = 5
TERMS = 126
GROUPS = 16
SLOT_DEV = 11
COUNT = (1, 5, 15, 35, 70)
START = (0, 1, 6, 21, 56)
CAP = (1, 1, 1, 3, 5)
BASE = (0, 1, 2, 3, 6)
T8 = (8, 8, 16, 40, 72)
PARTS = (((0, 1, 8),), ((0, 5, 8),), ((0, 15, 16),), ((0, 8, 8), (8, 8, 8), (16, 19, 24)), ((0, 24, 24), (24, 24, 24), (48, 22, 24)))
WIDE = (True, True, True, True, False)
CHUNKS = ((0, 1), (1, 2), (3, 3), (6, 5))
OUTS = ((0, 1, (0, 1)), (1, 2, (0, 1)), (3, 3, (0, 1)), (6, 5, (0,)), (6, 5, (1,)))
CHUNK_OF = ((0, 0), (1, 0), (1, 1), (2, 0), (3, 0))
DIRS = ((-1, -1), (-1, 1), (1, -1), (1, 1), (0, -1), (0, 1), (-1, 0), (1, 0))
PIECES = ((0, 0, 2), (1, 0, 4), (2, 0, 6), (3, 0, 4), (3, 4, 7), (3, 7, 10))
MESH = pl.DeviceIdType.MESH


def compositions(total, pieces_left):
    if pieces_left == 1:
        return [[total]]
    result = []
    for leading in range(total, -1, -1):
        for remainder in compositions(total - leading, pieces_left - 1):
            result.append([leading] + remainder)
    return result


def parent_table():
    table = np.full((TERMS, DIMS), -1, np.int32)
    for level in range(1, 5):
        below = {tuple(v): n for n, v in enumerate(compositions(level - 1, DIMS))}
        for n, v in enumerate(compositions(level, DIMS)):
            for d in range(DIMS):
                if v[d] > 0:
                    w = list(v)
                    w[d] -= 1
                    table[START[level] + n, d] = below[tuple(w)]
    return table.reshape(-1)


def dot(a, b):
    return jnp.dot(a, b, preferred_element_type=jnp.float32)


def term_of(i):
    q, r = i // 4, i % 4
    return q * 4 + r + (q % 2) * (3 - 2 * r)


def kernel(ns, *refs):
    given, out, it = refs[:6], refs[6], iter(refs[7:])
    fin, fl, cp, ptab, slots, sten, given_sem = [next(it) for _ in range(7)]
    fetch = [
        pltpu.make_async_copy(src, dst, given_sem.at[n])
        for n, (src, dst) in enumerate(zip(given, (fin, fl, cp, ptab, slots, sten)))
    ]
    for copy in fetch:
        copy.start()
    sb = [next(it) for _ in CHUNKS]
    rb = [next(it) for _ in CHUNKS]
    ob = [next(it) for _ in OUTS]
    qb = [next(it) for _ in OUTS]
    load_buf = [next(it) for _ in range(5)]
    sett_buf = [next(it) for _ in range(4)]
    own_buf = [next(it) for _ in range(5)]
    img_buf = [next(it) for _ in range(4)]
    faces = [next(it) for _ in range(9)]
    rims = [next(it) for _ in range(9)]
    wh, wc, xs, low, ff, ft, posv, pos, pos_sem = [next(it) for _ in range(9)]
    in_s, in_r, out_s, out_r, h_s, h_r = [next(it) for _ in range(6)]

    s = lax.axis_index("space")
    k = lax.axis_index("terms")
    i = term_of(k)

    barrier = pltpu.get_barrier_semaphore()

    def greet(p, _):
        pl.semaphore_signal(
            barrier, inc=1, device_id={"terms": term_of((i + p) % GROUPS)}, device_id_type=MESH
        )
        return 0

    lax.fori_loop(1, GROUPS, greet, 0)

    def inside(dx, dz):
        return (s + dx >= 0) & (s + dx < ns) & (i + dz >= 0) & (i + dz < GROUPS)

    for dx, dz in DIRS:
        if dx == 0:
            continue

        @pl.when(inside(dx, dz))
        def _():
            pl.semaphore_signal(
                barrier, inc=1,
                device_id={"space": s + dx, "terms": term_of(i + dz)},
                device_id_type=MESH,
            )

    def pack(c):
        j0, n = CHUNKS[c]

        def one(m, _):
            j, x = j0 + m // 2, m % 2
            rows = [
                fin[pl.ds(pl.multiple_of((j * 6 + a * 2 + x) * 32, 32), 32), :] for a in range(3)
            ]
            turned = jnp.transpose(jnp.concatenate(rows + [jnp.zeros((32, 128), jnp.float32)], axis=0))
            sb[c][:, m] = turned.reshape(GROUPS, 8, 128)
            return 0

        lax.fori_loop(0, 2 * n, one, 0)

    def wait_barrier():
        sides = jnp.where((s > 0) & (s < ns - 1), 2, 1) if ns > 1 else 0
        rows_of = jnp.where((i > 0) & (i < GROUPS - 1), 3, 2)
        pl.semaphore_wait(barrier, GROUPS - 1 + sides * rows_of)

    def leaving(c, p, src, dst, s_sem, r_sem, inward, tiles):
        i2 = (i + p) % GROUPS
        k2 = term_of(i2)
        return pltpu.make_async_remote_copy(
            src_ref=src.at[i2 if inward else k2, tiles],
            dst_ref=dst.at[k if inward else i, tiles],
            send_sem=s_sem.at[c, p],
            recv_sem=r_sem.at[c, p],
            device_id={"terms": k2},
            device_id_type=MESH,
        )

    def arriving(c, p, src, dst, s_sem, r_sem, inward, tiles):
        i2 = (i - p + GROUPS) % GROUPS
        k2 = term_of(i2)
        return pltpu.make_async_remote_copy(
            src_ref=src.at[0, tiles],
            dst_ref=dst.at[k2 if inward else i2, tiles],
            send_sem=s_sem.at[c, p],
            recv_sem=r_sem.at[c, p],
            device_id={"terms": k2},
            device_id_type=MESH,
        )

    def over_peers(fn):
        def one(p, _):
            fn(p)
            return 0

        lax.fori_loop(1, GROUPS, one, 0)

    def piece_in(n):
        c, lo, hi = PIECES[n]
        return (sb[c], rb[c], in_s, in_r, True, slice(lo, hi))

    def send_in(n):
        c, lo, hi = PIECES[n]
        over_peers(lambda p: leaving(n, p, *piece_in(n)).start())
        rb[c][k, lo:hi] = sb[c][i, lo:hi]

    def wait_in(c):
        for n, piece in enumerate(PIECES):
            if piece[0] == c:
                over_peers(lambda p: arriving(n, p, *piece_in(n)).wait_recv())

    def whole_out(c):
        return (ob[c], qb[c], out_s, out_r, False, slice(0, ob[c].shape[1]))

    def send_out(c):
        over_peers(lambda p: leaving(c, p, *whole_out(c)).start())
        qb[c][i] = ob[c][k]

    def wait_out(c):
        over_peers(lambda p: arriving(c, p, *whole_out(c)).wait_recv())

    fetch[0].wait()
    pack(0)
    wait_barrier()
    send_in(0)
    pack(1)
    send_in(1)

    for copy in fetch[1:]:
        copy.wait()
    lane8 = lax.broadcasted_iota(jnp.int32, (8, 128), 1)

    def locate(g, acc):
        for j in range(SLOT_DEV):
            acc = jnp.where(lane8 == slots[g * SLOT_DEV + j], g * 16 + j, acc)
        return acc

    posv[...] = lax.fori_loop(0, GROUPS, locate, jnp.zeros((8, 128), jnp.int32))
    to_smem = pltpu.make_async_copy(posv, pos, pos_sem)
    to_smem.start()

    for which in range(2):
        wh[which, 9 * 128 :, 0:128] = jnp.zeros((384, 128), jnp.bfloat16)
        wh[which, 0 : 3 * 128, 128:256] = jnp.zeros((384, 128), jnp.bfloat16)
    lane1 = lax.broadcasted_iota(jnp.int32, (1, 128), 1)
    group = lane1 // 32

    def by_group(v0, v1, v2):
        return jnp.where(
            group == 0, v0, jnp.where(group == 1, v1, jnp.where(group == 2, v2, 0.0))
        ).astype(jnp.float32)

    def splat(v):
        return jnp.full((1, 128), v, jnp.float32)

    inv = [1.0 / splat(sten[a, a, 13]) for a in range(3)]
    inv_lane = by_group(*inv)
    apart = lax.broadcasted_iota(jnp.int32, (32, 128), 0) - lax.broadcasted_iota(
        jnp.int32, (32, 128), 1
    ) % 32

    def table(m, _):
        dx, dz = m // 3, m % 3
        for b in range(4):
            block = [jnp.zeros((32, 128), jnp.float32)] * 2
            if b < 3:
                for dy in range(3):
                    o = dx * 9 + dy * 3 + dz
                    plain = by_group(*[splat(sten[a, b, o]) for a in range(3)])
                    smooth = -(plain * inv_lane) * inv[b]
                    if dy == 1:
                        centre = (group == b) & ((dx == 1) & (dz == 1))
                        smooth = jnp.where(centre, inv_lane, smooth)
                    for which, line in enumerate((smooth, plain)):
                        block[which] = jnp.where(apart == dy - 1, line, block[which])
            for which in range(2):
                hi = block[which].astype(jnp.bfloat16)
                lo = (block[which] - hi.astype(jnp.float32)).astype(jnp.bfloat16)
                row = pl.multiple_of((dx * 3 + dz) * 128 + b * 32, 32)
                wc[which, pl.ds(row, 32), 0:128] = hi
                wc[which, pl.ds(row, 32), 128:256] = lo
                for px in range(2):
                    row = pl.multiple_of(((dx + px) * 3 + dz) * 128 + b * 32, 32)
                    wh[which, pl.ds(row, 32), px * 128 : px * 128 + 128] = hi
        return 0

    lax.fori_loop(0, 9, table, 0)

    def field(m, _):
        rows = fl[m // 2, m % 2]
        ft[...] = jnp.transpose(jnp.concatenate([rows] * 4, axis=0))
        ff[m] = ft[pl.ds(pl.multiple_of(8 * i, 8), 8), :]
        return 0

    lax.fori_loop(0, 2 * DIMS, field, 0)

    def zero_outside(buf, rim, count, wide):
        def layer(x):
            def one(t, _):
                buf[x, t] = jnp.zeros((24, 128), jnp.float32)
                return 0

            lax.fori_loop(0, count, one, 0)
            for side in range(2):
                if wide:
                    for row in range(3):
                        rim[side, row, x] = jnp.zeros(rim.shape[3:], jnp.float32)
                else:
                    rim[side, x] = jnp.zeros(rim.shape[2:], jnp.float32)

        def edge(side):
            if wide:
                for row in (side, side + 1):
                    rim[side, row] = jnp.zeros(rim.shape[2:], jnp.float32)
            else:
                rim[side] = jnp.zeros(rim.shape[1:], jnp.float32)

        for x in (0, 1) if wide else (0,):
            pl.when(s == 0)(lambda x=x: layer(x))
        for x in (4, 5) if wide else (3,):
            pl.when(s == ns - 1)(lambda x=x: layer(x))
        pl.when(i == 0)(lambda: edge(0))
        pl.when(i == GROUPS - 1)(lambda: edge(1))

    for lv in range(5):
        zero_outside(load_buf[lv], rims[2 * lv], COUNT[lv], WIDE[lv])
        if lv < 4 and not WIDE[lv]:
            zero_outside(sett_buf[lv], rims[2 * lv + 1], COUNT[lv], False)

    pack(2)
    pack(3)
    to_smem.wait()

    def halo_copy(q, n, e, buf, part):
        t0, count, n8 = part
        dx, dz = DIRS[n]
        sx, tx = {1: (2, 0), -1: (1, 3), 0: (0, 0)}[dx]
        if buf.shape[0] == 6:
            tx = {1: 0, -1: 4, 0: 2}[dx]
            if dz == 0:
                src = buf.at[2:4, t0 : t0 + count, 8:16, :]
                dst = buf.at[tx : tx + 2, t0 : t0 + count, 8:16, :]
            else:
                side = 1 if dz > 0 else 0
                src = faces[e].at[side, :, :, t0 : t0 + n8]
                dst = rims[e].at[1 - side, 1 - side : 3 - side, tx : tx + 2, t0 : t0 + n8]
        elif dz == 0:
            src = buf.at[sx, t0 : t0 + count, 8:16, :]
            dst = buf.at[tx, t0 : t0 + count, 8:16, :]
        else:
            side = 1 if dz > 0 else 0
            if dx == 0:
                src = faces[e].at[side, :, t0 : t0 + n8]
                dst = rims[e].at[1 - side, 1:3, t0 : t0 + n8]
            else:
                src = faces[e].at[side, sx - 1, t0 : t0 + n8]
                dst = rims[e].at[1 - side, tx, t0 : t0 + n8]
        return pltpu.make_async_remote_copy(
            src_ref=src,
            dst_ref=dst,
            send_sem=h_s.at[q, n],
            recv_sem=h_r.at[q, n],
            device_id={"space": s + dx, "terms": term_of(i + dz)},
            device_id_type=MESH,
        )

    def by_five(part, fn):
        t0, count, _ = part
        w = next(w for w in (19, 12, 11, 8, 5, 1) if count % w == 0)

        def some(u, _):
            for v in range(w):
                fn(t0 + u * w + v)
            return 0

        lax.fori_loop(0, count // w, some, 0)

    exchanges = []

    def start_exchange(e, buf, part):
        args = (len(exchanges), e, buf, part)
        exchanges.append(args)
        for n, (dx, dz) in enumerate(DIRS):
            pl.when(inside(dx, dz))(lambda n=n: halo_copy(args[0], n, *args[1:]).start())
        return args

    def end_exchange(q, e, buf, part):
        for n, (dx, dz) in enumerate(DIRS):
            pl.when(inside(-dx, -dz))(lambda n=n: halo_copy(q, n, e, buf, part).wait_recv())
        spread_rim(e, buf, part)

    def spread_rim(e, buf, part):
        def spread(t):
            for x in range(4):
                buf[x, t, 7:8, :] = rims[e][0, x, pl.ds(t, 1), :]
                buf[x, t, 16:17, :] = rims[e][1, x, pl.ds(t, 1), :]

        def spread_wide(t):
            for x in range(6):
                buf[x, t, 7:8, :] = rims[e][0, 1, x, pl.ds(t, 1), :]
                buf[x, t, 16:17, :] = rims[e][1, 1, x, pl.ds(t, 1), :]
                rims[e][0, 2, x, pl.ds(t, 1), :] = buf[x, t, 8:9, :]
                rims[e][1, 0, x, pl.ds(t, 1), :] = buf[x, t, 15:16, :]

        by_five(part, spread_wide if buf.shape[0] == 6 else spread)

    def halves(v):
        hi = v.astype(jnp.bfloat16)
        return hi, (v - hi.astype(jnp.float32)).astype(jnp.bfloat16)

    def product(rows, which):
        rest = dot(xs[rows : 2 * rows, :], wh[which])
        return [main(0, rows, px, which) + rest[:, 128 * px : 128 * px + 128] for px in range(2)]

    def main(at, rows, px, which):
        both = dot(xs[at : at + rows, 384 * px : 384 * px + 1152], wc[which])
        return both[:, 0:128] + both[:, 128:256]

    def settle_wide(lv, part):
        t0, count, t8 = part
        src, rim, step = load_buf[lv], rims[2 * lv], (count + 1) // 2 * 2
        base = 16 * step
        rows = base + 4 * t8

        def put(row, col, v):
            hi, lo = halves(v)
            xs[pl.ds(pl.multiple_of(row, 16), v.shape[0]), col : col + 128] = hi
            xs[pl.ds(pl.multiple_of(rows + row, 16), v.shape[0]), col : col + 128] = lo

        def pair(u, _):
            for dz in range(3):
                for w in range(4):
                    for b in range(2):
                        v = [src[2 * b + w, t0 + 2 * u + h, 7 + dz : 15 + dz, :] for h in range(2)]
                        put(b * 8 * step + u * 16, (w * 3 + dz) * 128, jnp.concatenate(v, axis=0))
            return 0

        lax.fori_loop(0, step // 2, pair, 0)
        for side in range(2):
            for dz in range(3):
                for w in range(4):
                    v = [rim[side, dz, 2 * b + w, t0 : t0 + t8] for b in range(2)]
                    put(base + side * 2 * t8, (w * 3 + dz) * 128, jnp.concatenate(v, axis=0))
        res = product(rows, 0)
        one, zero = jnp.float32(1.0), jnp.float32(0.0)
        in_x = [jnp.where(s > 0, one, zero), one, one, jnp.where(s < ns - 1, one, zero)]
        in_z = [jnp.where(i > 0, one, zero), jnp.where(i < GROUPS - 1, one, zero)]
        for x in range(4):
            b, mine = x // 2, res[x % 2]
            v = mine[b * 8 * step : (b + 1) * 8 * step].reshape(step, 8, 128)
            if x in (1, 2):
                own_buf[lv][x - 1, t0 : t0 + step] = v
            else:
                v = v * in_x[x]
            sett_buf[lv][x, t0 : t0 + step, 8:16, :] = v
            for side in range(2):
                row = base + side * 2 * t8 + b * t8
                rims[2 * lv + 1][side, x, t0 : t0 + t8] = mine[row : row + t8] * (in_x[x] * in_z[side])

    def stage_rows(src, part, lo_at, at=0):
        t0, count, _ = part

        def pair(u, _):
            t = t0 + 2 * u
            for dz in range(3):
                for x in range(4):
                    v = jnp.concatenate(
                        [src[x, t, 7 + dz : 15 + dz, :], src[x, t + 1, 7 + dz : 15 + dz, :]], axis=0
                    )
                    hi, lo = halves(v)
                    col = (x * 3 + dz) * 128
                    xs[pl.ds(pl.multiple_of(at + u * 16, 16), 16), col : col + 128] = hi
                    xs[pl.ds(pl.multiple_of(lo_at + u * 16, 16), 16), col : col + 128] = lo
            return 0

        lax.fori_loop(0, (count + 1) // 2, pair, 0)

    def apply(src, part, which, store):
        step = (part[1] + 1) // 2 * 2
        stage_rows(src, part, 8 * step)
        res = product(8 * step, which)
        for px in range(2):
            store(px, part[0], res[px].reshape(step, 8, 128))

    pending = []
    for lv in range(5):
        c, j0 = CHUNK_OF[lv]
        if lv == 0 or c != CHUNK_OF[lv - 1][0]:
            wait_in(c)

        def load_of(t):
            q = pos[0, START[lv] + t]
            g = q // 16
            j = j0 + jnp.clip(q % 16 - BASE[lv], 0, CAP[lv] - 1)
            parts = [rb[c][g, 2 * j + x] for x in range(2)]
            if lv > 0:
                for d in range(DIMS):
                    par = ptab[(START[lv] + t) * DIMS + d]
                    weight = jnp.where(par >= 0, cp[d, START[lv] + t], 0.0)
                    at = jnp.maximum(par, 0)
                    for x in range(2):
                        parts[x] = parts[x] - (weight * ff[2 * d + x]) * img_buf[lv - 1][x, at]
            for x in range(2):
                load_buf[lv][(2 if WIDE[lv] else 1) + x, t, 8:16, :] = parts[x]
                if WIDE[lv]:
                    for row in range(2):
                        faces[2 * lv][0, row, x, pl.ds(t, 1), :] = parts[x][row : row + 1]
                        faces[2 * lv][1, row, x, pl.ds(t, 1), :] = parts[x][6 + row : 7 + row]
                else:
                    faces[2 * lv][0, x, pl.ds(t, 1), :] = parts[x][0:1]
                    faces[2 * lv][1, x, pl.ds(t, 1), :] = parts[x][7:8]

        started = []
        for part in PARTS[lv]:
            by_five(part, load_of)
            started.append(start_exchange(2 * lv, load_buf[lv], part))
        ready = pending.pop()() if pending else None

        def deliver_to(o, j0, layers, lv=lv):
            def deliver(g, _):
                for j in range(CAP[lv]):
                    q = slots[g * SLOT_DEV + BASE[lv] + j]
                    t = jnp.clip(q - START[lv], 0, COUNT[lv] - 1)
                    for n, x in enumerate(layers):
                        v = own_buf[lv][x, t]
                        ob[o][g, len(layers) * (j0 + j) + n] = jnp.where(q >= 0, v, 0.0)
                return 0

            lax.fori_loop(0, GROUPS, deliver, 0)

        def deliver_packed(o, x, lv=lv):
            def deliver(g, _):
                v = []
                for j in range(CAP[lv]):
                    q = slots[g * SLOT_DEV + BASE[lv] + j]
                    t = jnp.clip(q - START[lv], 0, COUNT[lv] - 1)
                    v.append(jnp.where(q >= 0, own_buf[lv][x, t], 0.0))
                r1, r2, r3 = [pltpu.roll(v[1 + n], 96 - 32 * n, 1) for n in range(3)]
                ob[o][g, 0] = jnp.where(lane8 < 96, v[0], r1)
                ob[o][g, 1] = jnp.where(lane8 < 64, r1, r2)
                ob[o][g, 2] = jnp.where(lane8 < 32, r2, r3)
                ob[o][g, 3] = v[4]
                return 0

            lax.fori_loop(0, GROUPS, deliver, 0)

        def image(px, t0, v):
            img_buf[lv][px, t0 : t0 + v.shape[0]] = v

        if WIDE[lv]:
            for part, args in zip(PARTS[lv], started):
                end_exchange(*args)
                if part is PARTS[lv][-1]:
                    send_in(2 + lv)
                    if ready is not None:
                        send_out(ready)
                settle_wide(lv, part)
                spread_rim(2 * lv + 1, sett_buf[lv], part)
                apply(sett_buf[lv], part, 1, image)

            def finish(lv=lv, c=c, j0=j0, deliver_to=deliver_to):
                deliver_to(c, j0, (0, 1))
                return c if CHUNK_OF[lv + 1][0] != c else None

            pending.append(finish)
        else:
            send_out(ready)
            lo_at = 8 * COUNT[lv]
            for px in range(2):
                for part, args in zip(PARTS[lv], started):
                    at, n = 8 * part[0], 8 * part[1]
                    if px == 0:
                        end_exchange(*args)
                        stage_rows(load_buf[lv], part, lo_at + at, at)
                        low[at : at + n, :] = dot(xs[lo_at + at : lo_at + at + n, :], wh[0])
                    res = main(at, n, px, 0) + low[at : at + n, 128 * px : 128 * px + 128]
                    own_buf[lv][px, part[0] : part[0] + part[1]] = res.reshape(part[1], 8, 128)
                deliver_packed(3 + px, px)
                send_out(3 + px)

    for c, (j0, n, layers) in enumerate(OUTS):
        wait_out(c)
        if len(layers) == 1:
            for m in range(4):
                turned = jnp.transpose(qb[c][:, m].reshape(128, 128))
                for g in range(4 * m, min(4 * m + 4, 15)):
                    row = ((j0 + g // 3) * 6 + g % 3 * 2 + layers[0]) * 32
                    out[row : row + 32, :] = turned[32 * (g - 4 * m) : 32 * (g - 4 * m) + 32]
            continue

        def unpack(m, _, c=c, j0=j0, layers=layers):
            j, x = j0 + m // 2, m % 2
            turned = jnp.transpose(qb[c][:, m].reshape(128, 128))
            for a in range(3):
                row = pl.multiple_of((j * 6 + a * 2 + x) * 32, 32)
                out[pl.ds(row, 32), :] = turned[32 * a : 32 * a + 32]
            return 0

        lax.fori_loop(0, 2 * n, unpack, 0)

    for n in range(len(PIECES)):
        over_peers(lambda p: leaving(n, p, *piece_in(n)).wait_send())
    for c in range(len(OUTS)):
        over_peers(lambda p: leaving(c, p, *whole_out(c)).wait_send())
    for q, e, buf, part in exchanges:
        for n, (dx, dz) in enumerate(DIRS):
            pl.when(inside(dx, dz))(lambda n=n: halo_copy(q, n, e, buf, part).wait_send())


def on_device(ns, forcing, stencil, fields, coupling, slot_term):
    rows = forcing.shape[0] * 6 * 32
    vm = pl.BlockSpec(memory_space=pltpu.VMEM)
    hbm = pl.BlockSpec(memory_space=pltpu.HBM)
    f32, bf16 = jnp.float32, jnp.bfloat16
    dma = pltpu.SemaphoreType.DMA
    scratch = [
        pltpu.VMEM((rows, 128), f32),
        pltpu.VMEM(fields.shape, f32),
        pltpu.SMEM(coupling.shape[::-1], f32),
        pltpu.SMEM((TERMS * DIMS,), jnp.int32),
        pltpu.SMEM(slot_term.shape, jnp.int32),
        pltpu.SMEM((3, 3, 27), f32),
        dma((6,)),
    ]
    scratch += [pltpu.VMEM((GROUPS, 2 * n, 8, 128), f32) for _ in range(2) for _, n in CHUNKS]
    scratch += [
        pltpu.VMEM((GROUPS, 2 * n if len(x) == 2 else 4, 8, 128), f32) for _ in range(2) for _, n, x in OUTS
    ]
    scratch += [pltpu.VMEM((6 if WIDE[lv] else 4, T8[lv], 24, 128), f32) for lv in range(5)]
    scratch += [pltpu.VMEM((4, T8[lv], 24, 128), f32) for lv in range(4)]
    scratch += [pltpu.VMEM((2, T8[lv], 8, 128), f32) for lv in range(5)]
    scratch += [pltpu.VMEM((2, T8[lv], 8, 128), f32) for lv in range(4)]
    wide = [WIDE[e // 2] and e % 2 == 0 for e in range(9)]
    scratch += [pltpu.VMEM((2,) + (2,) * w + (2, T8[e // 2], 128), f32) for e, w in enumerate(wide)]
    scratch += [
        pltpu.VMEM((2, 3, 6, T8[e // 2], 128) if w else (2, 4, T8[e // 2], 128), f32)
        for e, w in enumerate(wide)
    ]
    scratch += [
        pltpu.VMEM((2, 12 * 128, 256), bf16),
        pltpu.VMEM((2, 9 * 128, 256), bf16),
        pltpu.VMEM((16 * COUNT[4], 12 * 128), bf16),
        pltpu.VMEM((8 * COUNT[4], 256), f32),
        pltpu.VMEM((2 * DIMS, 8, 128), f32),
        pltpu.VMEM((128, 128), f32),
        pltpu.VMEM((8, 128), jnp.int32),
        pltpu.SMEM((8, 128), jnp.int32),
        dma(()),
    ]
    scratch += [dma((len(PIECES), GROUPS)) for _ in range(2)]
    scratch += [dma((len(OUTS), GROUPS)) for _ in range(2)] + [dma((sum(map(len, PARTS)), 8)) for _ in range(2)]
    out = pl.pallas_call(
        functools.partial(kernel, ns),
        out_shape=pltpu.VMEM((rows, 128), f32),
        in_specs=[hbm] * 6,
        out_specs=vm,
        scratch_shapes=scratch,
        compiler_params=pltpu.CompilerParams(
            collective_id=0, has_side_effects=True, vmem_limit_bytes=58 << 20
        ),
    )(forcing.reshape(rows, 128), fields, coupling.T, jnp.asarray(parent_table()), slot_term, stencil.transpose(1, 2, 0))
    return out.reshape(forcing.shape)


def solution(mesh):
    return jax.shard_map(
        functools.partial(on_device, mesh.shape["space"]),
        mesh=mesh,
        in_specs=(
            P("terms", None, "space", None, None),
            P(),
            P(None, "space", None, None),
            P(),
            P(),
        ),
        out_specs=P("terms", None, "space", None, None),
        check_vma=False,
    )
```

```python
import functools

import jax
import jax.numpy as jnp
import numpy as np
from jax import lax
from jax.experimental import pallas as pl
from jax.experimental.pallas import tpu as pltpu
from jax.sharding import PartitionSpec as P

DIMS = 5
TERMS = 126
GROUPS = 16
SLOT_DEV = 11
COUNT = (1, 5, 15, 35, 70)
START = (0, 1, 6, 21, 56)
CAP = (1, 1, 1, 3, 5)
BASE = (0, 1, 2, 3, 6)
T8 = (8, 8, 16, 40, 72)
PARTS = (((0, 1, 8),), ((0, 5, 8),), ((0, 15, 16),), ((0, 8, 8), (8, 8, 8), (16, 19, 24)), ((0, 24, 24), (24, 24, 24), (48, 22, 24)))
WIDE = (True, True, True, True, False)
CHUNKS = ((0, 1), (1, 2), (3, 3), (6, 5))
OUTS = ((0, 1, (0, 1)), (1, 2, (0, 1)), (3, 3, (0, 1)), (6, 5, (0,)), (6, 5, (1,)))
CHUNK_OF = ((0, 0), (1, 0), (1, 1), (2, 0), (3, 0))
DIRS = ((-1, -1), (-1, 1), (1, -1), (1, 1), (0, -1), (0, 1), (-1, 0), (1, 0))
PIECES = ((0, 0, 2), (1, 0, 4), (2, 0, 6), (3, 0, 4), (3, 4, 7), (3, 7, 10))
MESH = pl.DeviceIdType.MESH


def compositions(total, pieces_left):
    if pieces_left == 1:
        return [[total]]
    result = []
    for leading in range(total, -1, -1):
        for remainder in compositions(total - leading, pieces_left - 1):
            result.append([leading] + remainder)
    return result


def parent_table():
    table = np.full((TERMS, DIMS), -1, np.int32)
    for level in range(1, 5):
        below = {tuple(v): n for n, v in enumerate(compositions(level - 1, DIMS))}
        for n, v in enumerate(compositions(level, DIMS)):
            for d in range(DIMS):
                if v[d] > 0:
                    w = list(v)
                    w[d] -= 1
                    table[START[level] + n, d] = below[tuple(w)]
    return table.reshape(-1)


def dot(a, b):
    return jnp.dot(a, b, preferred_element_type=jnp.float32)


def term_of(i):
    q, r = i // 4, i % 4
    return q * 4 + r + (q % 2) * (3 - 2 * r)


def kernel(ns, *refs):
    given, out, it = refs[:6], refs[6], iter(refs[7:])
    fin, fl, cp, ptab, slots, sten, given_sem = [next(it) for _ in range(7)]
    fetch = [
        pltpu.make_async_copy(src, dst, given_sem.at[n])
        for n, (src, dst) in enumerate(zip(given, (fin, fl, cp, ptab, slots, sten)))
    ]
    for copy in fetch:
        copy.start()
    sb = [next(it) for _ in CHUNKS]
    rb = [next(it) for _ in CHUNKS]
    ob = [next(it) for _ in OUTS]
    qb = [next(it) for _ in OUTS]
    load_buf = [next(it) for _ in range(5)]
    sett_buf = [next(it) for _ in range(4)]
    own_buf = [next(it) for _ in range(5)]
    img_buf = [next(it) for _ in range(4)]
    faces = [next(it) for _ in range(9)]
    rims = [next(it) for _ in range(9)]
    wh, wc, xs, low, ff, ft, posv, pos, pos_sem = [next(it) for _ in range(9)]
    in_s, in_r, out_s, out_r, h_s, h_r = [next(it) for _ in range(6)]

    s = lax.axis_index("space")
    k = lax.axis_index("terms")
    i = term_of(k)

    barrier = pltpu.get_barrier_semaphore()

    def greet(p, _):
        pl.semaphore_signal(
            barrier, inc=1, device_id={"terms": term_of((i + p) % GROUPS)}, device_id_type=MESH
        )
        return 0

    lax.fori_loop(1, GROUPS, greet, 0)

    def inside(dx, dz):
        return (s + dx >= 0) & (s + dx < ns) & (i + dz >= 0) & (i + dz < GROUPS)

    for dx, dz in DIRS:
        if dx == 0:
            continue

        @pl.when(inside(dx, dz))
        def _():
            pl.semaphore_signal(
                barrier, inc=1,
                device_id={"space": s + dx, "terms": term_of(i + dz)},
                device_id_type=MESH,
            )

    def pack(c):
        j0, n = CHUNKS[c]

        def one(m, _):
            j, x = j0 + m // 2, m % 2
            rows = [
                fin[pl.ds(pl.multiple_of((j * 6 + a * 2 + x) * 32, 32), 32), :] for a in range(3)
            ]
            turned = jnp.transpose(jnp.concatenate(rows + [jnp.zeros((32, 128), jnp.float32)], axis=0))
            sb[c][:, m] = turned.reshape(GROUPS, 8, 128)
            return 0

        lax.fori_loop(0, 2 * n, one, 0)

    def wait_barrier():
        sides = jnp.where((s > 0) & (s < ns - 1), 2, 1) if ns > 1 else 0
        rows_of = jnp.where((i > 0) & (i < GROUPS - 1), 3, 2)
        pl.semaphore_wait(barrier, GROUPS - 1 + sides * rows_of)

    def leaving(c, p, src, dst, s_sem, r_sem, inward, tiles):
        i2 = (i + p) % GROUPS
        k2 = term_of(i2)
        return pltpu.make_async_remote_copy(
            src_ref=src.at[i2 if inward else k2, tiles],
            dst_ref=dst.at[k if inward else i, tiles],
            send_sem=s_sem.at[c, p],
            recv_sem=r_sem.at[c, p],
            device_id={"terms": k2},
            device_id_type=MESH,
        )

    def arriving(c, p, src, dst, s_sem, r_sem, inward, tiles):
        i2 = (i - p + GROUPS) % GROUPS
        k2 = term_of(i2)
        return pltpu.make_async_remote_copy(
            src_ref=src.at[0, tiles],
            dst_ref=dst.at[k2 if inward else i2, tiles],
            send_sem=s_sem.at[c, p],
            recv_sem=r_sem.at[c, p],
            device_id={"terms": k2},
            device_id_type=MESH,
        )

    def over_peers(fn):
        def one(p, _):
            fn(p)
            return 0

        lax.fori_loop(1, GROUPS, one, 0)

    def piece_in(n):
        c, lo, hi = PIECES[n]
        return (sb[c], rb[c], in_s, in_r, True, slice(lo, hi))

    def send_in(n):
        c, lo, hi = PIECES[n]
        over_peers(lambda p: leaving(n, p, *piece_in(n)).start())
        rb[c][k, lo:hi] = sb[c][i, lo:hi]

    def wait_in(c):
        for n, piece in enumerate(PIECES):
            if piece[0] == c:
                over_peers(lambda p: arriving(n, p, *piece_in(n)).wait_recv())

    def whole_out(c):
        return (ob[c], qb[c], out_s, out_r, False, slice(0, ob[c].shape[1]))

    def send_out(c):
        over_peers(lambda p: leaving(c, p, *whole_out(c)).start())
        qb[c][i] = ob[c][k]

    def wait_out(c):
        over_peers(lambda p: arriving(c, p, *whole_out(c)).wait_recv())

    fetch[0].wait()
    pack(0)
    wait_barrier()
    send_in(0)
    pack(1)
    send_in(1)

    for copy in fetch[1:]:
        copy.wait()
    lane8 = lax.broadcasted_iota(jnp.int32, (8, 128), 1)

    def locate(g, acc):
        for j in range(SLOT_DEV):
            acc = jnp.where(lane8 == slots[g * SLOT_DEV + j], g * 16 + j, acc)
        return acc

    posv[...] = lax.fori_loop(0, GROUPS, locate, jnp.zeros((8, 128), jnp.int32))
    to_smem = pltpu.make_async_copy(posv, pos, pos_sem)
    to_smem.start()

    for which in range(2):
        wh[which, 9 * 128 :, 0:128] = jnp.zeros((384, 128), jnp.bfloat16)
        wh[which, 0 : 3 * 128, 128:256] = jnp.zeros((384, 128), jnp.bfloat16)
    lane1 = lax.broadcasted_iota(jnp.int32, (1, 128), 1)
    group = lane1 // 32

    def by_group(v0, v1, v2):
        return jnp.where(
            group == 0, v0, jnp.where(group == 1, v1, jnp.where(group == 2, v2, 0.0))
        ).astype(jnp.float32)

    def splat(v):
        return jnp.full((1, 128), v, jnp.float32)

    inv = [1.0 / splat(sten[a, a, 13]) for a in range(3)]
    inv_lane = by_group(*inv)
    apart = lax.broadcasted_iota(jnp.int32, (32, 128), 0) - lax.broadcasted_iota(
        jnp.int32, (32, 128), 1
    ) % 32

    def table(m, _):
        dx, dz = m // 3, m % 3
        for b in range(4):
            block = [jnp.zeros((32, 128), jnp.float32)] * 2
            if b < 3:
                for dy in range(3):
                    o = dx * 9 + dy * 3 + dz
                    plain = by_group(*[splat(sten[a, b, o]) for a in range(3)])
                    smooth = -(plain * inv_lane) * inv[b]
                    if dy == 1:
                        centre = (group == b) & ((dx == 1) & (dz == 1))
                        smooth = jnp.where(centre, inv_lane, smooth)
                    for which, line in enumerate((smooth, plain)):
                        block[which] = jnp.where(apart == dy - 1, line, block[which])
            for which in range(2):
                hi = block[which].astype(jnp.bfloat16)
                lo = (block[which] - hi.astype(jnp.float32)).astype(jnp.bfloat16)
                row = pl.multiple_of((dx * 3 + dz) * 128 + b * 32, 32)
                wc[which, pl.ds(row, 32), 0:128] = hi
                wc[which, pl.ds(row, 32), 128:256] = lo
                for px in range(2):
                    row = pl.multiple_of(((dx + px) * 3 + dz) * 128 + b * 32, 32)
                    wh[which, pl.ds(row, 32), px * 128 : px * 128 + 128] = hi
        return 0

    lax.fori_loop(0, 9, table, 0)

    def field(m, _):
        rows = fl[m // 2, m % 2]
        ft[...] = jnp.transpose(jnp.concatenate([rows] * 4, axis=0))
        ff[m] = ft[pl.ds(pl.multiple_of(8 * i, 8), 8), :]
        return 0

    lax.fori_loop(0, 2 * DIMS, field, 0)

    def zero_outside(buf, rim, count, wide):
        def layer(x):
            def one(t, _):
                buf[x, t] = jnp.zeros((24, 128), jnp.float32)
                return 0

            lax.fori_loop(0, count, one, 0)
            for side in range(2):
                if wide:
                    for row in range(3):
                        rim[side, row, x] = jnp.zeros(rim.shape[3:], jnp.float32)
                else:
                    rim[side, x] = jnp.zeros(rim.shape[2:], jnp.float32)

        def edge(side):
            if wide:
                for row in (side, side + 1):
                    rim[side, row] = jnp.zeros(rim.shape[2:], jnp.float32)
            else:
                rim[side] = jnp.zeros(rim.shape[1:], jnp.float32)

        for x in (0, 1) if wide else (0,):
            pl.when(s == 0)(lambda x=x: layer(x))
        for x in (4, 5) if wide else (3,):
            pl.when(s == ns - 1)(lambda x=x: layer(x))
        pl.when(i == 0)(lambda: edge(0))
        pl.when(i == GROUPS - 1)(lambda: edge(1))

    for lv in range(5):
        zero_outside(load_buf[lv], rims[2 * lv], COUNT[lv], WIDE[lv])
        if lv < 4 and not WIDE[lv]:
            zero_outside(sett_buf[lv], rims[2 * lv + 1], COUNT[lv], False)

    pack(2)
    pack(3)
    to_smem.wait()

    def halo_copy(q, n, e, buf, part):
        t0, count, n8 = part
        dx, dz = DIRS[n]
        sx, tx = {1: (2, 0), -1: (1, 3), 0: (0, 0)}[dx]
        if buf.shape[0] == 6:
            tx = {1: 0, -1: 4, 0: 2}[dx]
            if dz == 0:
                src = buf.at[2:4, t0 : t0 + count, 8:16, :]
                dst = buf.at[tx : tx + 2, t0 : t0 + count, 8:16, :]
            else:
                side = 1 if dz > 0 else 0
                src = faces[e].at[side, :, :, t0 : t0 + n8]
                dst = rims[e].at[1 - side, 1 - side : 3 - side, tx : tx + 2, t0 : t0 + n8]
        elif dz == 0:
            src = buf.at[sx, t0 : t0 + count, 8:16, :]
            dst = buf.at[tx, t0 : t0 + count, 8:16, :]
        else:
            side = 1 if dz > 0 else 0
            if dx == 0:
                src = faces[e].at[side, :, t0 : t0 + n8]
                dst = rims[e].at[1 - side, 1:3, t0 : t0 + n8]
            else:
                src = faces[e].at[side, sx - 1, t0 : t0 + n8]
                dst = rims[e].at[1 - side, tx, t0 : t0 + n8]
        return pltpu.make_async_remote_copy(
            src_ref=src,
            dst_ref=dst,
            send_sem=h_s.at[q, n],
            recv_sem=h_r.at[q, n],
            device_id={"space": s + dx, "terms": term_of(i + dz)},
            device_id_type=MESH,
        )

    def by_five(part, fn):
        t0, count, _ = part
        w = next(w for w in (19, 12, 11, 8, 5, 1) if count % w == 0)

        def some(u, _):
            for v in range(w):
                fn(t0 + u * w + v)
            return 0

        lax.fori_loop(0, count // w, some, 0)

    exchanges = []

    def start_exchange(e, buf, part):
        args = (len(exchanges), e, buf, part)
        exchanges.append(args)
        for n, (dx, dz) in enumerate(DIRS):
            pl.when(inside(dx, dz))(lambda n=n: halo_copy(args[0], n, *args[1:]).start())
        return args

    def end_exchange(q, e, buf, part):
        for n, (dx, dz) in enumerate(DIRS):
            pl.when(inside(-dx, -dz))(lambda n=n: halo_copy(q, n, e, buf, part).wait_recv())
        spread_rim(e, buf, part)

    def spread_rim(e, buf, part):
        def spread(t):
            for x in range(4):
                buf[x, t, 7:8, :] = rims[e][0, x, pl.ds(t, 1), :]
                buf[x, t, 16:17, :] = rims[e][1, x, pl.ds(t, 1), :]

        def spread_wide(t):
            for x in range(6):
                buf[x, t, 7:8, :] = rims[e][0, 1, x, pl.ds(t, 1), :]
                buf[x, t, 16:17, :] = rims[e][1, 1, x, pl.ds(t, 1), :]
                rims[e][0, 2, x, pl.ds(t, 1), :] = buf[x, t, 8:9, :]
                rims[e][1, 0, x, pl.ds(t, 1), :] = buf[x, t, 15:16, :]

        by_five(part, spread_wide if buf.shape[0] == 6 else spread)

    def halves(v):
        hi = v.astype(jnp.bfloat16)
        return hi, (v - hi.astype(jnp.float32)).astype(jnp.bfloat16)

    def product(rows, which):
        rest = dot(xs[rows : 2 * rows, :], wh[which])
        return [main(0, rows, px, which) + rest[:, 128 * px : 128 * px + 128] for px in range(2)]

    def main(at, rows, px, which):
        both = dot(xs[at : at + rows, 384 * px : 384 * px + 1152], wc[which])
        return both[:, 0:128] + both[:, 128:256]

    def settle_wide(lv, part):
        t0, count, t8 = part
        src, rim, step = load_buf[lv], rims[2 * lv], (count + 1) // 2 * 2
        base = 16 * step
        rows = base + 4 * t8

        def put(row, col, v):
            hi, lo = halves(v)
            xs[pl.ds(pl.multiple_of(row, 16), v.shape[0]), col : col + 128] = hi
            xs[pl.ds(pl.multiple_of(rows + row, 16), v.shape[0]), col : col + 128] = lo

        def pair(u, _):
            for dz in range(3):
                for w in range(4):
                    for b in range(2):
                        v = [src[2 * b + w, t0 + 2 * u + h, 7 + dz : 15 + dz, :] for h in range(2)]
                        put(b * 8 * step + u * 16, (w * 3 + dz) * 128, jnp.concatenate(v, axis=0))
            return 0

        lax.fori_loop(0, step // 2, pair, 0)
        for side in range(2):
            for dz in range(3):
                for w in range(4):
                    v = [rim[side, dz, 2 * b + w, t0 : t0 + t8] for b in range(2)]
                    put(base + side * 2 * t8, (w * 3 + dz) * 128, jnp.concatenate(v, axis=0))
        res = product(rows, 0)
        one, zero = jnp.float32(1.0), jnp.float32(0.0)
        in_x = [jnp.where(s > 0, one, zero), one, one, jnp.where(s < ns - 1, one, zero)]
        in_z = [jnp.where(i > 0, one, zero), jnp.where(i < GROUPS - 1, one, zero)]
        for x in range(4):
            b, mine = x // 2, res[x % 2]
            v = mine[b * 8 * step : (b + 1) * 8 * step].reshape(step, 8, 128)
            if x in (1, 2):
                own_buf[lv][x - 1, t0 : t0 + step] = v
            else:
                v = v * in_x[x]
            sett_buf[lv][x, t0 : t0 + step, 8:16, :] = v
            for side in range(2):
                row = base + side * 2 * t8 + b * t8
                rims[2 * lv + 1][side, x, t0 : t0 + t8] = mine[row : row + t8] * (in_x[x] * in_z[side])

    def stage_rows(src, part, lo_at, at=0):
        t0, count, _ = part

        def pair(u, _):
            t = t0 + 2 * u
            for dz in range(3):
                for x in range(4):
                    v = jnp.concatenate(
                        [src[x, t, 7 + dz : 15 + dz, :], src[x, t + 1, 7 + dz : 15 + dz, :]], axis=0
                    )
                    hi, lo = halves(v)
                    col = (x * 3 + dz) * 128
                    xs[pl.ds(pl.multiple_of(at + u * 16, 16), 16), col : col + 128] = hi
                    xs[pl.ds(pl.multiple_of(lo_at + u * 16, 16), 16), col : col + 128] = lo
            return 0

        lax.fori_loop(0, (count + 1) // 2, pair, 0)

    def apply(src, part, which, store):
        step = (part[1] + 1) // 2 * 2
        stage_rows(src, part, 8 * step)
        res = product(8 * step, which)
        for px in range(2):
            store(px, part[0], res[px].reshape(step, 8, 128))

    pending = []
    for lv in range(5):
        c, j0 = CHUNK_OF[lv]
        if lv == 0 or c != CHUNK_OF[lv - 1][0]:
            wait_in(c)

        def load_of(t):
            q = pos[0, START[lv] + t]
            g = q // 16
            j = j0 + jnp.clip(q % 16 - BASE[lv], 0, CAP[lv] - 1)
            parts = [rb[c][g, 2 * j + x] for x in range(2)]
            if lv > 0:
                for d in range(DIMS):
                    par = ptab[(START[lv] + t) * DIMS + d]
                    weight = jnp.where(par >= 0, cp[d, START[lv] + t], 0.0)
                    at = jnp.maximum(par, 0)
                    for x in range(2):
                        parts[x] = parts[x] - (weight * ff[2 * d + x]) * img_buf[lv - 1][x, at]
            for x in range(2):
                load_buf[lv][(2 if WIDE[lv] else 1) + x, t, 8:16, :] = parts[x]
                if WIDE[lv]:
                    for row in range(2):
                        faces[2 * lv][0, row, x, pl.ds(t, 1), :] = parts[x][row : row + 1]
                        faces[2 * lv][1, row, x, pl.ds(t, 1), :] = parts[x][6 + row : 7 + row]
                else:
                    faces[2 * lv][0, x, pl.ds(t, 1), :] = parts[x][0:1]
                    faces[2 * lv][1, x, pl.ds(t, 1), :] = parts[x][7:8]

        started = []
        for part in PARTS[lv]:
            by_five(part, load_of)
            started.append(start_exchange(2 * lv, load_buf[lv], part))
        ready = pending.pop()() if pending else None

        def deliver_to(o, j0, layers, lv=lv):
            def deliver(g, _):
                for j in range(CAP[lv]):
                    q = slots[g * SLOT_DEV + BASE[lv] + j]
                    t = jnp.clip(q - START[lv], 0, COUNT[lv] - 1)
                    for n, x in enumerate(layers):
                        v = own_buf[lv][x, t]
                        ob[o][g, len(layers) * (j0 + j) + n] = jnp.where(q >= 0, v, 0.0)
                return 0

            lax.fori_loop(0, GROUPS, deliver, 0)

        def deliver_packed(o, x, lv=lv):
            def deliver(g, _):
                v = []
                for j in range(CAP[lv]):
                    q = slots[g * SLOT_DEV + BASE[lv] + j]
                    t = jnp.clip(q - START[lv], 0, COUNT[lv] - 1)
                    v.append(jnp.where(q >= 0, own_buf[lv][x, t], 0.0))
                r1, r2, r3 = [pltpu.roll(v[1 + n], 96 - 32 * n, 1) for n in range(3)]
                ob[o][g, 0] = jnp.where(lane8 < 96, v[0], r1)
                ob[o][g, 1] = jnp.where(lane8 < 64, r1, r2)
                ob[o][g, 2] = jnp.where(lane8 < 32, r2, r3)
                ob[o][g, 3] = v[4]
                return 0

            lax.fori_loop(0, GROUPS, deliver, 0)

        def image(px, t0, v):
            img_buf[lv][px, t0 : t0 + v.shape[0]] = v

        if WIDE[lv]:
            for part, args in zip(PARTS[lv], started):
                end_exchange(*args)
                if part is PARTS[lv][-1]:
                    send_in(2 + lv)
                    if ready is not None:
                        send_out(ready)
                settle_wide(lv, part)
                spread_rim(2 * lv + 1, sett_buf[lv], part)
                apply(sett_buf[lv], part, 1, image)

            def finish(lv=lv, c=c, j0=j0, deliver_to=deliver_to):
                deliver_to(c, j0, (0, 1))
                return c if CHUNK_OF[lv + 1][0] != c else None

            pending.append(finish)
        else:
            send_out(ready)
            lo_at = 8 * COUNT[lv]
            for px in range(2):
                for part, args in zip(PARTS[lv], started):
                    at, n = 8 * part[0], 8 * part[1]
                    if px == 0:
                        end_exchange(*args)
                        stage_rows(load_buf[lv], part, lo_at + at, at)
                        low[at : at + n, :] = dot(xs[lo_at + at : lo_at + at + n, :], wh[0])
                    res = main(at, n, px, 0) + low[at : at + n, 128 * px : 128 * px + 128]
                    own_buf[lv][px, part[0] : part[0] + part[1]] = res.reshape(part[1], 8, 128)
                deliver_packed(3 + px, px)
                send_out(3 + px)

    def sent_early():
        for n in range(len(PIECES)):
            over_peers(lambda p: leaving(n, p, *piece_in(n)).wait_send())
        for c in range(3):
            over_peers(lambda p: leaving(c, p, *whole_out(c)).wait_send())
        for q, e, buf, part in exchanges:
            for n, (dx, dz) in enumerate(DIRS):
                pl.when(inside(dx, dz))(lambda n=n: halo_copy(q, n, e, buf, part).wait_send())

    for c, (j0, n, layers) in enumerate(OUTS):
        if c == 3:
            sent_early()
        wait_out(c)
        if len(layers) == 1:
            for m in range(4):
                turned = jnp.transpose(qb[c][:, m].reshape(128, 128))
                for g in range(4 * m, min(4 * m + 4, 15)):
                    row = ((j0 + g // 3) * 6 + g % 3 * 2 + layers[0]) * 32
                    out[row : row + 32, :] = turned[32 * (g - 4 * m) : 32 * (g - 4 * m) + 32]
            continue

        def unpack(m, _, c=c, j0=j0, layers=layers):
            j, x = j0 + m // 2, m % 2
            turned = jnp.transpose(qb[c][:, m].reshape(128, 128))
            for a in range(3):
                row = pl.multiple_of((j * 6 + a * 2 + x) * 32, 32)
                out[pl.ds(row, 32), :] = turned[32 * a : 32 * a + 32]
            return 0

        lax.fori_loop(0, 2 * n, unpack, 0)

    for c in range(3, len(OUTS)):
        over_peers(lambda p: leaving(c, p, *whole_out(c)).wait_send())


def on_device(ns, forcing, stencil, fields, coupling, slot_term):
    rows = forcing.shape[0] * 6 * 32
    vm = pl.BlockSpec(memory_space=pltpu.VMEM)
    hbm = pl.BlockSpec(memory_space=pltpu.HBM)
    f32, bf16 = jnp.float32, jnp.bfloat16
    dma = pltpu.SemaphoreType.DMA
    scratch = [
        pltpu.VMEM((rows, 128), f32),
        pltpu.VMEM(fields.shape, f32),
        pltpu.SMEM(coupling.shape[::-1], f32),
        pltpu.SMEM((TERMS * DIMS,), jnp.int32),
        pltpu.SMEM(slot_term.shape, jnp.int32),
        pltpu.SMEM((3, 3, 27), f32),
        dma((6,)),
    ]
    scratch += [pltpu.VMEM((GROUPS, 2 * n, 8, 128), f32) for _ in range(2) for _, n in CHUNKS]
    scratch += [
        pltpu.VMEM((GROUPS, 2 * n if len(x) == 2 else 4, 8, 128), f32) for _ in range(2) for _, n, x in OUTS
    ]
    scratch += [pltpu.VMEM((6 if WIDE[lv] else 4, T8[lv], 24, 128), f32) for lv in range(5)]
    scratch += [pltpu.VMEM((4, T8[lv], 24, 128), f32) for lv in range(4)]
    scratch += [pltpu.VMEM((2, T8[lv], 8, 128), f32) for lv in range(5)]
    scratch += [pltpu.VMEM((2, T8[lv], 8, 128), f32) for lv in range(4)]
    wide = [WIDE[e // 2] and e % 2 == 0 for e in range(9)]
    scratch += [pltpu.VMEM((2,) + (2,) * w + (2, T8[e // 2], 128), f32) for e, w in enumerate(wide)]
    scratch += [
        pltpu.VMEM((2, 3, 6, T8[e // 2], 128) if w else (2, 4, T8[e // 2], 128), f32)
        for e, w in enumerate(wide)
    ]
    scratch += [
        pltpu.VMEM((2, 12 * 128, 256), bf16),
        pltpu.VMEM((2, 9 * 128, 256), bf16),
        pltpu.VMEM((16 * COUNT[4], 12 * 128), bf16),
        pltpu.VMEM((8 * COUNT[4], 256), f32),
        pltpu.VMEM((2 * DIMS, 8, 128), f32),
        pltpu.VMEM((128, 128), f32),
        pltpu.VMEM((8, 128), jnp.int32),
        pltpu.SMEM((8, 128), jnp.int32),
        dma(()),
    ]
    scratch += [dma((len(PIECES), GROUPS)) for _ in range(2)]
    scratch += [dma((len(OUTS), GROUPS)) for _ in range(2)] + [dma((sum(map(len, PARTS)), 8)) for _ in range(2)]
    out = pl.pallas_call(
        functools.partial(kernel, ns),
        out_shape=pltpu.VMEM((rows, 128), f32),
        in_specs=[hbm] * 6,
        out_specs=vm,
        scratch_shapes=scratch,
        compiler_params=pltpu.CompilerParams(
            collective_id=0, has_side_effects=True, vmem_limit_bytes=58 << 20
        ),
    )(forcing.reshape(rows, 128), fields, coupling.T, jnp.asarray(parent_table()), slot_term, stencil.transpose(1, 2, 0))
    return out.reshape(forcing.shape)


def solution(mesh):
    return jax.shard_map(
        functools.partial(on_device, mesh.shape["space"]),
        mesh=mesh,
        in_specs=(
            P("terms", None, "space", None, None),
            P(),
            P(None, "space", None, None),
            P(),
            P(),
        ),
        out_specs=P("terms", None, "space", None, None),
        check_vma=False,
    )
```

```python
import functools

import jax
import jax.numpy as jnp
import numpy as np
from jax import lax
from jax.experimental import pallas as pl
from jax.experimental.pallas import tpu as pltpu
from jax.sharding import PartitionSpec as P

DIMS = 5
TERMS = 126
GROUPS = 16
SLOT_DEV = 11
COUNT = (1, 5, 15, 35, 70)
START = (0, 1, 6, 21, 56)
CAP = (1, 1, 1, 3, 5)
BASE = (0, 1, 2, 3, 6)
T8 = (8, 8, 16, 40, 72)
PARTS = (((0, 1, 8),), ((0, 5, 8),), ((0, 15, 16),), ((0, 8, 8), (8, 8, 8), (16, 19, 24)), ((0, 24, 24), (24, 24, 24), (48, 22, 24)))
WIDE = (True, True, True, True, False)
CHUNKS = ((0, 1), (1, 2), (3, 3), (6, 5))
OUTS = ((0, 1, (0, 1)), (1, 2, (0, 1)), (3, 3, (0, 1)), (6, 5, (0,)), (6, 5, (1,)))
CHUNK_OF = ((0, 0), (1, 0), (1, 1), (2, 0), (3, 0))
DIRS = ((-1, -1), (-1, 1), (1, -1), (1, 1), (0, -1), (0, 1), (-1, 0), (1, 0))
PIECES = ((0, 0, 2), (1, 0, 4), (2, 0, 6), (3, 0, 4), (3, 4, 7), (3, 7, 10))
MESH = pl.DeviceIdType.MESH


def compositions(total, pieces_left):
    if pieces_left == 1:
        return [[total]]
    result = []
    for leading in range(total, -1, -1):
        for remainder in compositions(total - leading, pieces_left - 1):
            result.append([leading] + remainder)
    return result


def parent_table():
    table = np.full((TERMS, DIMS), -1, np.int32)
    for level in range(1, 5):
        below = {tuple(v): n for n, v in enumerate(compositions(level - 1, DIMS))}
        for n, v in enumerate(compositions(level, DIMS)):
            for d in range(DIMS):
                if v[d] > 0:
                    w = list(v)
                    w[d] -= 1
                    table[START[level] + n, d] = below[tuple(w)]
    return table.reshape(-1)


def dot(a, b):
    return jnp.dot(a, b, preferred_element_type=jnp.float32)


def term_of(i):
    q, r = i // 4, i % 4
    return q * 4 + r + (q % 2) * (3 - 2 * r)


def kernel(ns, *refs):
    given, out, it = refs[:6], refs[6], iter(refs[7:])
    fin, fl, cp, ptab, slots, sten, given_sem = [next(it) for _ in range(7)]
    fetch = [
        pltpu.make_async_copy(src, dst, given_sem.at[n])
        for n, (src, dst) in enumerate(zip(given, (fin, fl, cp, ptab, slots, sten)))
    ]
    for copy in fetch:
        copy.start()
    sb = [next(it) for _ in CHUNKS]
    rb = [next(it) for _ in CHUNKS]
    ob = [next(it) for _ in OUTS]
    qb = [next(it) for _ in OUTS]
    load_buf = [next(it) for _ in range(5)]
    sett_buf = [next(it) for _ in range(4)]
    own_buf = [next(it) for _ in range(5)]
    img_buf = [next(it) for _ in range(4)]
    faces = [next(it) for _ in range(9)]
    rims = [next(it) for _ in range(9)]
    wh, wc, xs, low, ff, ft, posv, pos, pos_sem = [next(it) for _ in range(9)]
    in_s, in_r, out_s, out_r, h_s, h_r = [next(it) for _ in range(6)]

    s = lax.axis_index("space")
    k = lax.axis_index("terms")
    i = term_of(k)

    barrier = pltpu.get_barrier_semaphore()

    def greet(p, _):
        pl.semaphore_signal(
            barrier, inc=1, device_id={"terms": term_of((i + p) % GROUPS)}, device_id_type=MESH
        )
        return 0

    lax.fori_loop(1, GROUPS, greet, 0)

    def inside(dx, dz):
        return (s + dx >= 0) & (s + dx < ns) & (i + dz >= 0) & (i + dz < GROUPS)

    for dx, dz in DIRS:
        if dx == 0:
            continue

        @pl.when(inside(dx, dz))
        def _():
            pl.semaphore_signal(
                barrier, inc=1,
                device_id={"space": s + dx, "terms": term_of(i + dz)},
                device_id_type=MESH,
            )

    def pack(c):
        j0, n = CHUNKS[c]

        def one(m, _):
            j, x = j0 + m // 2, m % 2
            rows = [
                fin[pl.ds(pl.multiple_of((j * 6 + a * 2 + x) * 32, 32), 32), :] for a in range(3)
            ]
            turned = jnp.transpose(jnp.concatenate(rows + [jnp.zeros((32, 128), jnp.float32)], axis=0))
            sb[c][:, m] = turned.reshape(GROUPS, 8, 128)
            return 0

        lax.fori_loop(0, 2 * n, one, 0)

    def wait_barrier():
        sides = jnp.where((s > 0) & (s < ns - 1), 2, 1) if ns > 1 else 0
        rows_of = jnp.where((i > 0) & (i < GROUPS - 1), 3, 2)
        pl.semaphore_wait(barrier, GROUPS - 1 + sides * rows_of)

    def leaving(c, p, src, dst, s_sem, r_sem, inward, tiles):
        i2 = (i + p) % GROUPS
        k2 = term_of(i2)
        return pltpu.make_async_remote_copy(
            src_ref=src.at[i2 if inward else k2, tiles],
            dst_ref=dst.at[k if inward else i, tiles],
            send_sem=s_sem.at[c, p],
            recv_sem=r_sem.at[c, p],
            device_id={"terms": k2},
            device_id_type=MESH,
        )

    def arriving(c, p, src, dst, s_sem, r_sem, inward, tiles):
        i2 = (i - p + GROUPS) % GROUPS
        k2 = term_of(i2)
        return pltpu.make_async_remote_copy(
            src_ref=src.at[0, tiles],
            dst_ref=dst.at[k2 if inward else i2, tiles],
            send_sem=s_sem.at[c, p],
            recv_sem=r_sem.at[c, p],
            device_id={"terms": k2},
            device_id_type=MESH,
        )

    def over_peers(fn):
        def one(p, _):
            fn(p)
            return 0

        lax.fori_loop(1, GROUPS, one, 0)

    def piece_in(n):
        c, lo, hi = PIECES[n]
        return (sb[c], rb[c], in_s, in_r, True, slice(lo, hi))

    def send_in(n):
        c, lo, hi = PIECES[n]
        over_peers(lambda p: leaving(n, p, *piece_in(n)).start())
        rb[c][k, lo:hi] = sb[c][i, lo:hi]

    def wait_in(c):
        for n, piece in enumerate(PIECES):
            if piece[0] == c:
                over_peers(lambda p: arriving(n, p, *piece_in(n)).wait_recv())

    def whole_out(c):
        return (ob[c], qb[c], out_s, out_r, False, slice(0, ob[c].shape[1]))

    def send_out(c):
        over_peers(lambda p: leaving(c, p, *whole_out(c)).start())
        qb[c][i] = ob[c][k]

    def wait_out(c):
        over_peers(lambda p: arriving(c, p, *whole_out(c)).wait_recv())

    fetch[0].wait()
    pack(0)
    wait_barrier()
    send_in(0)
    pack(1)
    send_in(1)

    for copy in fetch[1:]:
        copy.wait()
    lane8 = lax.broadcasted_iota(jnp.int32, (8, 128), 1)

    def locate(g, acc):
        for j in range(SLOT_DEV):
            acc = jnp.where(lane8 == slots[g * SLOT_DEV + j], g * 16 + j, acc)
        return acc

    posv[...] = lax.fori_loop(0, GROUPS, locate, jnp.zeros((8, 128), jnp.int32))
    to_smem = pltpu.make_async_copy(posv, pos, pos_sem)
    to_smem.start()

    for which in range(2):
        wh[which, 9 * 128 :, 0:128] = jnp.zeros((384, 128), jnp.bfloat16)
        wh[which, 0 : 3 * 128, 128:256] = jnp.zeros((384, 128), jnp.bfloat16)
    lane1 = lax.broadcasted_iota(jnp.int32, (1, 128), 1)
    group = lane1 // 32

    def by_group(v0, v1, v2):
        return jnp.where(
            group == 0, v0, jnp.where(group == 1, v1, jnp.where(group == 2, v2, 0.0))
        ).astype(jnp.float32)

    def splat(v):
        return jnp.full((1, 128), v, jnp.float32)

    inv = [1.0 / splat(sten[a, a, 13]) for a in range(3)]
    inv_lane = by_group(*inv)
    apart = lax.broadcasted_iota(jnp.int32, (32, 128), 0) - lax.broadcasted_iota(
        jnp.int32, (32, 128), 1
    ) % 32

    def table(m, _):
        dx, dz = m // 3, m % 3
        for b in range(4):
            block = [jnp.zeros((32, 128), jnp.float32)] * 2
            if b < 3:
                for dy in range(3):
                    o = dx * 9 + dy * 3 + dz
                    plain = by_group(*[splat(sten[a, b, o]) for a in range(3)])
                    smooth = -(plain * inv_lane) * inv[b]
                    if dy == 1:
                        centre = (group == b) & ((dx == 1) & (dz == 1))
                        smooth = jnp.where(centre, inv_lane, smooth)
                    for which, line in enumerate((smooth, plain)):
                        block[which] = jnp.where(apart == dy - 1, line, block[which])
            for which in range(2):
                hi = block[which].astype(jnp.bfloat16)
                lo = (block[which] - hi.astype(jnp.float32)).astype(jnp.bfloat16)
                row = pl.multiple_of((dx * 3 + dz) * 128 + b * 32, 32)
                wc[which, pl.ds(row, 32), 0:128] = hi
                wc[which, pl.ds(row, 32), 128:256] = lo
                for px in range(2):
                    row = pl.multiple_of(((dx + px) * 3 + dz) * 128 + b * 32, 32)
                    wh[which, pl.ds(row, 32), px * 128 : px * 128 + 128] = hi
        return 0

    lax.fori_loop(0, 9, table, 0)

    def field(m, _):
        rows = fl[m // 2, m % 2]
        ft[...] = jnp.transpose(jnp.concatenate([rows] * 4, axis=0))
        ff[m] = ft[pl.ds(pl.multiple_of(8 * i, 8), 8), :]
        return 0

    lax.fori_loop(0, 2 * DIMS, field, 0)

    def zero_outside(buf, rim, count, wide):
        def layer(x):
            def one(t, _):
                buf[x, t] = jnp.zeros((24, 128), jnp.float32)
                return 0

            lax.fori_loop(0, count, one, 0)
            for side in range(2):
                if wide:
                    for row in range(3):
                        rim[side, row, x] = jnp.zeros(rim.shape[3:], jnp.float32)
                else:
                    rim[side, x] = jnp.zeros(rim.shape[2:], jnp.float32)

        def edge(side):
            if wide:
                for row in (side, side + 1):
                    rim[side, row] = jnp.zeros(rim.shape[2:], jnp.float32)
            else:
                rim[side] = jnp.zeros(rim.shape[1:], jnp.float32)

        for x in (0, 1) if wide else (0,):
            pl.when(s == 0)(lambda x=x: layer(x))
        for x in (4, 5) if wide else (3,):
            pl.when(s == ns - 1)(lambda x=x: layer(x))
        pl.when(i == 0)(lambda: edge(0))
        pl.when(i == GROUPS - 1)(lambda: edge(1))


    to_smem.wait()

    def halo_copy(q, n, e, buf, part):
        t0, count, n8 = part
        dx, dz = DIRS[n]
        sx, tx = {1: (2, 0), -1: (1, 3), 0: (0, 0)}[dx]
        if buf.shape[0] == 6:
            tx = {1: 0, -1: 4, 0: 2}[dx]
            if dz == 0:
                src = buf.at[2:4, t0 : t0 + count, 8:16, :]
                dst = buf.at[tx : tx + 2, t0 : t0 + count, 8:16, :]
            else:
                side = 1 if dz > 0 else 0
                src = faces[e].at[side, :, :, t0 : t0 + n8]
                dst = rims[e].at[1 - side, 1 - side : 3 - side, tx : tx + 2, t0 : t0 + n8]
        elif dz == 0:
            src = buf.at[sx, t0 : t0 + count, 8:16, :]
            dst = buf.at[tx, t0 : t0 + count, 8:16, :]
        else:
            side = 1 if dz > 0 else 0
            if dx == 0:
                src = faces[e].at[side, :, t0 : t0 + n8]
                dst = rims[e].at[1 - side, 1:3, t0 : t0 + n8]
            else:
                src = faces[e].at[side, sx - 1, t0 : t0 + n8]
                dst = rims[e].at[1 - side, tx, t0 : t0 + n8]
        return pltpu.make_async_remote_copy(
            src_ref=src,
            dst_ref=dst,
            send_sem=h_s.at[q, n],
            recv_sem=h_r.at[q, n],
            device_id={"space": s + dx, "terms": term_of(i + dz)},
            device_id_type=MESH,
        )

    def by_five(part, fn):
        t0, count, _ = part
        w = next(w for w in (19, 12, 11, 8, 5, 1) if count % w == 0)

        def some(u, _):
            for v in range(w):
                fn(t0 + u * w + v)
            return 0

        lax.fori_loop(0, count // w, some, 0)

    exchanges = []

    def start_exchange(e, buf, part):
        args = (len(exchanges), e, buf, part)
        exchanges.append(args)
        for n, (dx, dz) in enumerate(DIRS):
            pl.when(inside(dx, dz))(lambda n=n: halo_copy(args[0], n, *args[1:]).start())
        return args

    def end_exchange(q, e, buf, part):
        for n, (dx, dz) in enumerate(DIRS):
            pl.when(inside(-dx, -dz))(lambda n=n: halo_copy(q, n, e, buf, part).wait_recv())
        spread_rim(e, buf, part)

    def spread_rim(e, buf, part):
        def spread(t):
            for x in range(4):
                buf[x, t, 7:8, :] = rims[e][0, x, pl.ds(t, 1), :]
                buf[x, t, 16:17, :] = rims[e][1, x, pl.ds(t, 1), :]

        def spread_wide(t):
            for x in range(6):
                buf[x, t, 7:8, :] = rims[e][0, 1, x, pl.ds(t, 1), :]
                buf[x, t, 16:17, :] = rims[e][1, 1, x, pl.ds(t, 1), :]
                rims[e][0, 2, x, pl.ds(t, 1), :] = buf[x, t, 8:9, :]
                rims[e][1, 0, x, pl.ds(t, 1), :] = buf[x, t, 15:16, :]

        by_five(part, spread_wide if buf.shape[0] == 6 else spread)

    def halves(v):
        hi = v.astype(jnp.bfloat16)
        return hi, (v - hi.astype(jnp.float32)).astype(jnp.bfloat16)

    def product(rows, which):
        rest = dot(xs[rows : 2 * rows, :], wh[which])
        return [main(0, rows, px, which) + rest[:, 128 * px : 128 * px + 128] for px in range(2)]

    def main(at, rows, px, which):
        both = dot(xs[at : at + rows, 384 * px : 384 * px + 1152], wc[which])
        return both[:, 0:128] + both[:, 128:256]

    def settle_wide(lv, part):
        t0, count, t8 = part
        src, rim, step = load_buf[lv], rims[2 * lv], (count + 1) // 2 * 2
        base = 16 * step
        rows = base + 4 * t8

        def put(row, col, v):
            hi, lo = halves(v)
            xs[pl.ds(pl.multiple_of(row, 16), v.shape[0]), col : col + 128] = hi
            xs[pl.ds(pl.multiple_of(rows + row, 16), v.shape[0]), col : col + 128] = lo

        def pair(u, _):
            for dz in range(3):
                for w in range(4):
                    for b in range(2):
                        v = [src[2 * b + w, t0 + 2 * u + h, 7 + dz : 15 + dz, :] for h in range(2)]
                        put(b * 8 * step + u * 16, (w * 3 + dz) * 128, jnp.concatenate(v, axis=0))
            return 0

        lax.fori_loop(0, step // 2, pair, 0)
        for side in range(2):
            for dz in range(3):
                for w in range(4):
                    v = [rim[side, dz, 2 * b + w, t0 : t0 + t8] for b in range(2)]
                    put(base + side * 2 * t8, (w * 3 + dz) * 128, jnp.concatenate(v, axis=0))
        res = product(rows, 0)
        one, zero = jnp.float32(1.0), jnp.float32(0.0)
        in_x = [jnp.where(s > 0, one, zero), one, one, jnp.where(s < ns - 1, one, zero)]
        in_z = [jnp.where(i > 0, one, zero), jnp.where(i < GROUPS - 1, one, zero)]
        for x in range(4):
            b, mine = x // 2, res[x % 2]
            v = mine[b * 8 * step : (b + 1) * 8 * step].reshape(step, 8, 128)
            if x in (1, 2):
                own_buf[lv][x - 1, t0 : t0 + step] = v
            else:
                v = v * in_x[x]
            sett_buf[lv][x, t0 : t0 + step, 8:16, :] = v
            for side in range(2):
                row = base + side * 2 * t8 + b * t8
                rims[2 * lv + 1][side, x, t0 : t0 + t8] = mine[row : row + t8] * (in_x[x] * in_z[side])

    def stage_rows(src, part, lo_at, at=0):
        t0, count, _ = part

        def pair(u, _):
            t = t0 + 2 * u
            for dz in range(3):
                for x in range(4):
                    v = jnp.concatenate(
                        [src[x, t, 7 + dz : 15 + dz, :], src[x, t + 1, 7 + dz : 15 + dz, :]], axis=0
                    )
                    hi, lo = halves(v)
                    col = (x * 3 + dz) * 128
                    xs[pl.ds(pl.multiple_of(at + u * 16, 16), 16), col : col + 128] = hi
                    xs[pl.ds(pl.multiple_of(lo_at + u * 16, 16), 16), col : col + 128] = lo
            return 0

        lax.fori_loop(0, (count + 1) // 2, pair, 0)

    def apply(src, part, which, store):
        step = (part[1] + 1) // 2 * 2
        stage_rows(src, part, 8 * step)
        res = product(8 * step, which)
        for px in range(2):
            store(px, part[0], res[px].reshape(step, 8, 128))

    pending = []
    for lv in range(5):
        c, j0 = CHUNK_OF[lv]
        if lv == 0 or c != CHUNK_OF[lv - 1][0]:
            wait_in(c)

        def load_of(t):
            q = pos[0, START[lv] + t]
            g = q // 16
            j = j0 + jnp.clip(q % 16 - BASE[lv], 0, CAP[lv] - 1)
            parts = [rb[c][g, 2 * j + x] for x in range(2)]
            if lv > 0:
                for d in range(DIMS):
                    par = ptab[(START[lv] + t) * DIMS + d]
                    weight = jnp.where(par >= 0, cp[d, START[lv] + t], 0.0)
                    at = jnp.maximum(par, 0)
                    for x in range(2):
                        parts[x] = parts[x] - (weight * ff[2 * d + x]) * img_buf[lv - 1][x, at]
            for x in range(2):
                load_buf[lv][(2 if WIDE[lv] else 1) + x, t, 8:16, :] = parts[x]
                if WIDE[lv]:
                    for row in range(2):
                        faces[2 * lv][0, row, x, pl.ds(t, 1), :] = parts[x][row : row + 1]
                        faces[2 * lv][1, row, x, pl.ds(t, 1), :] = parts[x][6 + row : 7 + row]
                else:
                    faces[2 * lv][0, x, pl.ds(t, 1), :] = parts[x][0:1]
                    faces[2 * lv][1, x, pl.ds(t, 1), :] = parts[x][7:8]

        started = []
        for part in PARTS[lv]:
            by_five(part, load_of)
            started.append(start_exchange(2 * lv, load_buf[lv], part))
        zero_outside(load_buf[lv], rims[2 * lv], COUNT[lv], WIDE[lv])
        if lv < 2:
            pack(2 + lv)
        ready = pending.pop()() if pending else None

        def deliver_to(o, j0, layers, lv=lv):
            def deliver(g, _):
                for j in range(CAP[lv]):
                    q = slots[g * SLOT_DEV + BASE[lv] + j]
                    t = jnp.clip(q - START[lv], 0, COUNT[lv] - 1)
                    for n, x in enumerate(layers):
                        v = own_buf[lv][x, t]
                        ob[o][g, len(layers) * (j0 + j) + n] = jnp.where(q >= 0, v, 0.0)
                return 0

            lax.fori_loop(0, GROUPS, deliver, 0)

        def deliver_packed(o, x, lv=lv):
            def deliver(g, _):
                v = []
                for j in range(CAP[lv]):
                    q = slots[g * SLOT_DEV + BASE[lv] + j]
                    t = jnp.clip(q - START[lv], 0, COUNT[lv] - 1)
                    v.append(jnp.where(q >= 0, own_buf[lv][x, t], 0.0))
                r1, r2, r3 = [pltpu.roll(v[1 + n], 96 - 32 * n, 1) for n in range(3)]
                ob[o][g, 0] = jnp.where(lane8 < 96, v[0], r1)
                ob[o][g, 1] = jnp.where(lane8 < 64, r1, r2)
                ob[o][g, 2] = jnp.where(lane8 < 32, r2, r3)
                ob[o][g, 3] = v[4]
                return 0

            lax.fori_loop(0, GROUPS, deliver, 0)

        def image(px, t0, v):
            img_buf[lv][px, t0 : t0 + v.shape[0]] = v

        if WIDE[lv]:
            for part, args in zip(PARTS[lv], started):
                end_exchange(*args)
                if part is PARTS[lv][-1]:
                    send_in(2 + lv)
                    if ready is not None:
                        send_out(ready)
                settle_wide(lv, part)
                spread_rim(2 * lv + 1, sett_buf[lv], part)
                apply(sett_buf[lv], part, 1, image)

            def finish(lv=lv, c=c, j0=j0, deliver_to=deliver_to):
                deliver_to(c, j0, (0, 1))
                return c if CHUNK_OF[lv + 1][0] != c else None

            pending.append(finish)
        else:
            send_out(ready)
            lo_at = 8 * COUNT[lv]
            for px in range(2):
                for part, args in zip(PARTS[lv], started):
                    at, n = 8 * part[0], 8 * part[1]
                    if px == 0:
                        end_exchange(*args)
                        stage_rows(load_buf[lv], part, lo_at + at, at)
                        low[at : at + n, :] = dot(xs[lo_at + at : lo_at + at + n, :], wh[0])
                    res = main(at, n, px, 0) + low[at : at + n, 128 * px : 128 * px + 128]
                    own_buf[lv][px, part[0] : part[0] + part[1]] = res.reshape(part[1], 8, 128)
                deliver_packed(3 + px, px)
                send_out(3 + px)

    def sent_early():
        for n in range(len(PIECES)):
            over_peers(lambda p: leaving(n, p, *piece_in(n)).wait_send())
        for c in range(3):
            over_peers(lambda p: leaving(c, p, *whole_out(c)).wait_send())
        for q, e, buf, part in exchanges:
            for n, (dx, dz) in enumerate(DIRS):
                pl.when(inside(dx, dz))(lambda n=n: halo_copy(q, n, e, buf, part).wait_send())

    for c, (j0, n, layers) in enumerate(OUTS):
        if c == 3:
            sent_early()
        wait_out(c)
        if len(layers) == 1:
            for m in range(4):
                turned = jnp.transpose(qb[c][:, m].reshape(128, 128))
                for g in range(4 * m, min(4 * m + 4, 15)):
                    row = ((j0 + g // 3) * 6 + g % 3 * 2 + layers[0]) * 32
                    out[row : row + 32, :] = turned[32 * (g - 4 * m) : 32 * (g - 4 * m) + 32]
            continue

        def unpack(m, _, c=c, j0=j0, layers=layers):
            j, x = j0 + m // 2, m % 2
            turned = jnp.transpose(qb[c][:, m].reshape(128, 128))
            for a in range(3):
                row = pl.multiple_of((j * 6 + a * 2 + x) * 32, 32)
                out[pl.ds(row, 32), :] = turned[32 * a : 32 * a + 32]
            return 0

        lax.fori_loop(0, 2 * n, unpack, 0)

    for c in range(3, len(OUTS)):
        over_peers(lambda p: leaving(c, p, *whole_out(c)).wait_send())


def on_device(ns, forcing, stencil, fields, coupling, slot_term):
    rows = forcing.shape[0] * 6 * 32
    vm = pl.BlockSpec(memory_space=pltpu.VMEM)
    hbm = pl.BlockSpec(memory_space=pltpu.HBM)
    f32, bf16 = jnp.float32, jnp.bfloat16
    dma = pltpu.SemaphoreType.DMA
    scratch = [
        pltpu.VMEM((rows, 128), f32),
        pltpu.VMEM(fields.shape, f32),
        pltpu.SMEM(coupling.shape[::-1], f32),
        pltpu.SMEM((TERMS * DIMS,), jnp.int32),
        pltpu.SMEM(slot_term.shape, jnp.int32),
        pltpu.SMEM((3, 3, 27), f32),
        dma((6,)),
    ]
    scratch += [pltpu.VMEM((GROUPS, 2 * n, 8, 128), f32) for _ in range(2) for _, n in CHUNKS]
    scratch += [
        pltpu.VMEM((GROUPS, 2 * n if len(x) == 2 else 4, 8, 128), f32) for _ in range(2) for _, n, x in OUTS
    ]
    scratch += [pltpu.VMEM((6 if WIDE[lv] else 4, T8[lv], 24, 128), f32) for lv in range(5)]
    scratch += [pltpu.VMEM((4, T8[lv], 24, 128), f32) for lv in range(4)]
    scratch += [pltpu.VMEM((2, T8[lv], 8, 128), f32) for lv in range(5)]
    scratch += [pltpu.VMEM((2, T8[lv], 8, 128), f32) for lv in range(4)]
    wide = [WIDE[e // 2] and e % 2 == 0 for e in range(9)]
    scratch += [pltpu.VMEM((2,) + (2,) * w + (2, T8[e // 2], 128), f32) for e, w in enumerate(wide)]
    scratch += [
        pltpu.VMEM((2, 3, 6, T8[e // 2], 128) if w else (2, 4, T8[e // 2], 128), f32)
        for e, w in enumerate(wide)
    ]
    scratch += [
        pltpu.VMEM((2, 12 * 128, 256), bf16),
        pltpu.VMEM((2, 9 * 128, 256), bf16),
        pltpu.VMEM((16 * COUNT[4], 12 * 128), bf16),
        pltpu.VMEM((8 * COUNT[4], 256), f32),
        pltpu.VMEM((2 * DIMS, 8, 128), f32),
        pltpu.VMEM((128, 128), f32),
        pltpu.VMEM((8, 128), jnp.int32),
        pltpu.SMEM((8, 128), jnp.int32),
        dma(()),
    ]
    scratch += [dma((len(PIECES), GROUPS)) for _ in range(2)]
    scratch += [dma((len(OUTS), GROUPS)) for _ in range(2)] + [dma((sum(map(len, PARTS)), 8)) for _ in range(2)]
    out = pl.pallas_call(
        functools.partial(kernel, ns),
        out_shape=pltpu.VMEM((rows, 128), f32),
        in_specs=[hbm] * 6,
        out_specs=vm,
        scratch_shapes=scratch,
        compiler_params=pltpu.CompilerParams(
            collective_id=0, has_side_effects=True, vmem_limit_bytes=58 << 20
        ),
    )(forcing.reshape(rows, 128), fields, coupling.T, jnp.asarray(parent_table()), slot_term, stencil.transpose(1, 2, 0))
    return out.reshape(forcing.shape)


def solution(mesh):
    return jax.shard_map(
        functools.partial(on_device, mesh.shape["space"]),
        mesh=mesh,
        in_specs=(
            P("terms", None, "space", None, None),
            P(),
            P(None, "space", None, None),
            P(),
            P(),
        ),
        out_specs=P("terms", None, "space", None, None),
        check_vma=False,
    )
```
